32 devices in a mesh: fsdp: 16 (over z, x, core), tp: 2 (over y).
Axes of the slice: x: 2, y: 2, z: 4, core: 2. Of those that a mesh axis runs over, the one named last changes fastest.
Arguments:
- layer_in: bfloat16 [32768, 1536], P(('fsdp', 'tp')), may hold values from -6 to 6
- seg_ids: int32 [32768], P('fsdp'), may hold values from 0 to 127, as said below
- gain_one: float32 [1536], replicated, may hold values from 0.5 to 1.5
- x_weight: bfloat16 [1536, 3072], P('fsdp', 'tp'), may hold values from -0.15625 to 0.15625
- z_weight: bfloat16 [1536, 3072], P('fsdp', 'tp'), may hold values from -0.15625 to 0.15625
- dt_weight: bfloat16 [1536, 48], P('fsdp', 'tp'), may hold values from -0.15625 to 0.15625
- bc_weight: bfloat16 [1536, 32], P('fsdp'), may hold values from -0.078125 to 0.078125
- conv_weight: float32 [4, 3072], P(None, 'tp'), may hold values from -3 to 3
- conv_bias: float32 [3072], P('tp'), may hold values from -0.5 to 0.5
- dt_bias: float32 [48], P('tp'), may hold values from -4 to -1
- a_log: float32 [48], P('tp'), may hold values from -4.5 to 0.5
- d_skip: float32 [48], P('tp'), may hold values from 0.5 to 1.5
- out_weight: bfloat16 [1536, 3072], P('fsdp', 'tp'), may hold values from -0.109375 to 0.109375
- gain_two: float32 [1536], replicated, may hold values from 0.5 to 1.5
- gate_weight: bfloat16 [1536, 4096], P('fsdp', 'tp'), may hold values from -0.15625 to 0.15625
- up_weight: bfloat16 [1536, 4096], P('fsdp', 'tp'), may hold values from -0.15625 to 0.15625
- down_weight: bfloat16 [1536, 4096], P('fsdp', 'tp'), may hold values from -0.09375 to 0.09375
- cotangent: bfloat16 [32768, 1536], P(('fsdp', 'tp')), may hold values from -6 to 6
Outputs:
- layer_out: bfloat16 [32768, 1536], P(('fsdp', 'tp'))
- input_grad: float32 [32768, 1536], P(('fsdp', 'tp'))
- gain_one_grad: float32 [1536], replicated
- x_weight_grad: float32 [1536, 3072], P('fsdp', 'tp')
- z_weight_grad: float32 [1536, 3072], P('fsdp', 'tp')
- dt_weight_grad: float32 [1536, 48], P('fsdp', 'tp')
- bc_weight_grad: float32 [1536, 32], P('fsdp')
- conv_weight_grad: float32 [4, 3072], P(None, 'tp')
- conv_bias_grad: float32 [3072], P('tp')
- dt_bias_grad: float32 [48], P('tp')
- a_log_grad: float32 [48], P('tp')
- d_skip_grad: float32 [48], P('tp')
- out_weight_grad: float32 [1536, 3072], P('fsdp', 'tp')
- gain_two_grad: float32 [1536], replicated
- gate_weight_grad: float32 [1536, 4096], P('fsdp', 'tp')
- up_weight_grad: float32 [1536, 4096], P('fsdp', 'tp')
- down_weight_grad: float32 [1536, 4096], P('fsdp', 'tp')
The draws below stay inside these ranges and needn't reach their ends.
Inputs may be any that keep to these rules, and one draw needn't show every extreme that they name: `seg_ids`: within each sequence of 2048 tokens the ids never fall; every document has between 409 and 1365 tokens unless a sequence's end cuts it; ids of different sequences differ.
All inputs are finite; a program needn't handle non-finite values.
Results may differ from the reference program's by a relative error of at most 0.0099.
Values may be sent and summed in bfloat16 or wider, within the bound.
A program may use at most 384 MiB of HBM per device.

```python
import math
import jax
import jax.numpy as jnp
from jax import lax

D = 1536
INNER = 3072
NSTATE = 16
KCONV = 4
HEADDIM = 64
HEADS = 48
FF = 4096
BLOCK_LEN = 256
SEQ_LEN = 2048
TOKENS = 32768


def draw_seg_ids(key, part):
    sequences = TOKENS // SEQ_LEN
    most_docs = 8
    doc_lengths = jax.random.randint(key, (sequences, most_docs), max(SEQ_LEN // 5, 1), SEQ_LEN * 2 // 3 + 1)
    doc_ends = jnp.cumsum(doc_lengths, axis=1)
    places = jnp.arange(SEQ_LEN)
    doc_index = jnp.sum((places[None, :, None] >= doc_ends[:, None, :]).astype(jnp.int32), axis=2)
    last_index = doc_index[:, SEQ_LEN - 1]
    seq_index = jnp.arange(sequences)
    lift = jnp.where(seq_index == sequences - 1, most_docs - 1 - last_index, 0)
    segment_ids = doc_index + most_docs * seq_index[:, None] + lift[:, None]
    return segment_ids.reshape(-1).astype(jnp.int32)


def block_scale(rng, dims, shards, low, top_value):
    def one(dim, parts):
        draws = jax.random.uniform(jax.random.fold_in(jax.random.fold_in(rng, 6), dim), (parts,), jnp.float32, low / len(shards), top_value / len(shards))
        return jnp.repeat(jnp.exp(draws), dims[dim] // parts).reshape((-1,) + (1,) * (len(dims) - dim - 1))

    loudness = one(*shards[0])
    for cut in shards[1:]:
        loudness = loudness * one(*cut)
    return loudness


def scatter_about(stream_key, extent, deviation, bound, shards=(), held_as=jnp.bfloat16):
    values = deviation * jax.random.normal(stream_key, extent, jnp.float32)
    if shards:
        values = values * block_scale(stream_key, extent, shards, -0.22, 0.18)
    return jnp.clip(values, -bound, bound).astype(held_as)


def setup_inputs(seed: int = 0) -> dict:
    key_list = jax.random.split(jax.random.key(seed), 19)
    return {
        "layer_in": scatter_about(key_list[0], (TOKENS, D), 1.0, 6.0, ((0, 32),)),
        "seg_ids": draw_seg_ids(jax.random.fold_in(key_list[18], 71), 0),
        "gain_one": jnp.clip(1.0 + 0.1 * jax.random.normal(key_list[2], (D,), jnp.float32), 0.5, 1.5),
        "x_weight": scatter_about(key_list[3], (D, INNER), D ** -0.5, 0.15625, ((0, 16), (1, 2))),
        "z_weight": scatter_about(key_list[4], (D, INNER), D ** -0.5, 0.15625, ((0, 16), (1, 2))),
        "dt_weight": scatter_about(key_list[5], (D, HEADS), D ** -0.5, 0.15625, ((0, 16), (1, 2))),
        "bc_weight": scatter_about(key_list[6], (D, 2 * NSTATE), (4 * D) ** -0.5, 0.078125, ((0, 16),)),
        "conv_weight": scatter_about(key_list[7], (KCONV, INNER), KCONV ** -0.5, 3.0, ((1, 2),), jnp.float32),
        "conv_bias": jnp.clip(jax.random.uniform(key_list[8], (INNER,), jnp.float32, -0.5, 0.5) * block_scale(key_list[8], (INNER,), ((0, 2),), -0.4, 0.0), -0.5, 0.5),
        "dt_bias": jnp.clip(-4.0 + 3.0 * jax.random.uniform(key_list[9], (HEADS,), jnp.float32) ** block_scale(key_list[9], (HEADS,), ((0, 2),), -0.2, 0.2), -4.0, -1.0),
        "a_log": jnp.clip(-4.5 + 5.0 * jax.random.uniform(key_list[10], (HEADS,), jnp.float32) ** block_scale(key_list[10], (HEADS,), ((0, 2),), -0.2, 0.2), -4.5, 0.5),
        "d_skip": jnp.clip(0.5 + 1.0 * jax.random.uniform(key_list[11], (HEADS,), jnp.float32) ** block_scale(key_list[11], (HEADS,), ((0, 2),), -0.2, 0.2), 0.5, 1.5),
        "out_weight": scatter_about(key_list[12], (D, INNER), INNER ** -0.5, 0.109375, ((0, 16), (1, 2))),
        "gain_two": jnp.clip(1.0 + 0.1 * jax.random.normal(key_list[13], (D,), jnp.float32), 0.5, 1.5),
        "gate_weight": scatter_about(key_list[14], (D, FF), D ** -0.5, 0.15625, ((0, 16), (1, 2))),
        "up_weight": scatter_about(key_list[15], (D, FF), D ** -0.5, 0.15625, ((0, 16), (1, 2))),
        "down_weight": scatter_about(key_list[16], (D, FF), FF ** -0.5, 0.09375, ((0, 16), (1, 2))),
        "cotangent": scatter_about(key_list[17], (TOKENS, D), 1.0, 6.0, ((0, 32),)),
    }


@jax.custom_vjp
def low(v):
    return lax.optimization_barrier(v.astype(jnp.bfloat16)).astype(jnp.float32)

@jax.custom_vjp
def low_back(v):
    return v

def low_keep(v):
    return (low(v), None)

def low_pass(kept, grad):
    return (grad,)

def back_keep(v):
    return (v, None)

def back_low(kept, grad):
    return (low(grad),)
low.defvjp(low_keep, low_pass)
low_back.defvjp(back_keep, back_low)
highest = lax.Precision.HIGHEST
epsilon = 1e-05

def high_dot(left_arg, right_arg):
    return jnp.dot(left_arg, right_arg, precision=highest, preferred_element_type=jnp.float32)

def rms_norm(values, gain_row):
    return values * lax.rsqrt(lax.optimization_barrier(jnp.mean(values * values, axis=-1, keepdims=True)) + epsilon) * gain_row

def conv_restart(x_in, seg_rows, conv_weight, conv_bias):
    summed = conv_bias[None, :] + conv_weight[0][None, :] * x_in
    for offset in range(1, conv_weight.shape[0]):
        shifted = jnp.pad(x_in, ((offset, 0), (0, 0)))[:-offset]
        earlier = jnp.pad(seg_rows, (offset, 0), constant_values=-1)[:-offset]
        same_seg = (earlier == seg_rows).astype(x_in.dtype)
        summed = summed + conv_weight[offset][None, :] * shifted * same_seg[:, None]
    return summed

def block_step(carry_in, pieces, a_rate):
    carried, prev_seg = carry_in
    values, steps_dt, b_rows, c_rows, seg_block = pieces
    length = seg_block.shape[0]
    running = jnp.cumsum(steps_dt * a_rate[None, :], axis=0)
    places = jnp.arange(length)
    same_doc = (seg_block[:, None] == seg_block[None, :]) & (places[:, None] >= places[None, :])
    log_gaps = running.T[:, :, None] - running.T[:, None, :]
    decays = jnp.where(same_doc[None], jnp.exp(jnp.where(same_doc[None], log_gaps, 0.0)), 0.0)
    scores = jnp.dot(c_rows, b_rows.T, precision=highest)
    scaled = steps_dt[:, :, None] * values
    within = jnp.einsum('hts,shp->thp', decays * scores[None], scaled, precision=highest)
    carry_on = (seg_block == prev_seg).astype(values.dtype)
    from_state = jnp.einsum('tn,hpn->thp', c_rows, carried, precision=highest)
    within = within + from_state * (jnp.exp(running) * carry_on[:, None])[:, :, None]
    last_seg = seg_block[length - 1]
    tail_weight = (seg_block == last_seg).astype(values.dtype)[:, None] * jnp.exp(running[length - 1][None, :] - running)
    fresh = jnp.einsum('sh,shp,sn->hpn', tail_weight, scaled, b_rows, precision=highest)
    keep_state = jnp.where(last_seg == prev_seg, 1.0, 0.0) * jnp.exp(running[length - 1])
    return ((keep_state[:, None, None] * carried + fresh, last_seg), within)

def mixer(x_in, z_in, bc_rows, dt_raw, conv_weight, conv_bias, dt_bias, a_log, d_skip, seg_rows):
    values = jax.nn.silu(conv_restart(x_in, seg_rows, conv_weight, conv_bias))
    steps_dt = jax.nn.softplus(dt_raw + dt_bias[None, :])
    a_rate = -jnp.exp(a_log)
    tokens, channels = values.shape
    heads = channels // HEADDIM
    state_n = bc_rows.shape[1] // 2
    blocks = tokens // BLOCK_LEN
    per_block = (values.reshape(blocks, BLOCK_LEN, heads, HEADDIM), steps_dt.reshape(blocks, BLOCK_LEN, heads), bc_rows[:, :state_n].reshape(blocks, BLOCK_LEN, state_n), bc_rows[:, state_n:].reshape(blocks, BLOCK_LEN, state_n), seg_rows.reshape(blocks, BLOCK_LEN))

    def advance(carry_in, pieces):
        return block_step(carry_in, pieces, a_rate)
    start = (jnp.zeros((heads, HEADDIM, state_n), values.dtype), jnp.array(-1, jnp.int32))
    final_state, scanned = lax.scan(jax.checkpoint(advance), start, per_block)
    scanned = scanned.reshape(tokens, channels)
    skipped = jnp.repeat(d_skip, HEADDIM)[None, :] * values
    return (scanned + skipped) * jax.nn.silu(z_in)

def layer(weights_all, rows, seg_rows):
    gain_one, x_weight, z_weight, dt_weight, bc_weight, conv_weight, conv_bias, dt_bias, a_log, d_skip, out_weight, gain_two, gate_weight, up_weight, down_weight = weights_all
    normed = low(rms_norm(rows, gain_one))
    x_in = low_back(high_dot(normed, x_weight))
    z_in = low_back(high_dot(normed, z_weight))
    dt_raw = low_back(high_dot(normed, dt_weight))
    bc_rows = low_back(high_dot(normed, bc_weight))
    gated = low(mixer(x_in, z_in, bc_rows, dt_raw, conv_weight, conv_bias, dt_bias, a_log, d_skip, seg_rows))
    mixed = low_back(high_dot(gated, out_weight.T))
    hidden = rows + mixed
    normed_two = low(rms_norm(hidden, gain_two))
    gate = low_back(high_dot(normed_two, gate_weight))
    up_rows = low_back(high_dot(normed_two, up_weight))
    act = low(jax.nn.silu(gate) * up_rows)
    fed = low_back(high_dot(act, down_weight.T))
    return hidden + fed

def reference(layer_in, seg_ids, gain_one, x_weight, z_weight, dt_weight, bc_weight, conv_weight, conv_bias, dt_bias, a_log, d_skip, out_weight, gain_two, gate_weight, up_weight, down_weight, cotangent):
    weights_all = tuple((item.astype(jnp.float32) for item in (gain_one, x_weight, z_weight, dt_weight, bc_weight, conv_weight, conv_bias, dt_bias, a_log, d_skip, out_weight, gain_two, gate_weight, up_weight, down_weight)))
    sequences = TOKENS // SEQ_LEN
    per_step = math.gcd(sequences, max(1, 4096 // SEQ_LEN))
    step_tokens = per_step * SEQ_LEN
    steps_count = sequences // per_step
    rows_in = layer_in.astype(jnp.float32).reshape(steps_count, step_tokens, D)
    rows_seg = seg_ids.reshape(steps_count, step_tokens)
    rows_cot = cotangent.astype(jnp.float32).reshape(steps_count, step_tokens, D)

    def one_step(totals, pieces):
        block_in, block_seg, block_cot = pieces

        def forward_block(weights_now, rows_now):
            return layer(weights_now, rows_now, block_seg)
        block_out, pullback = jax.vjp(forward_block, weights_all, block_in)
        weight_grads, rows_grad = pullback(block_cot)
        return (jax.tree.map(jnp.add, totals, weight_grads), (block_out, rows_grad))
    zeros_all = jax.tree.map(jnp.zeros_like, weights_all)
    totals, (outs_all, grads_all) = lax.scan(one_step, zeros_all, (rows_in, rows_seg, rows_cot))
    layer_out = outs_all.reshape(TOKENS, D).astype(jnp.bfloat16)
    input_grad = grads_all.reshape(TOKENS, D)
    return (layer_out, input_grad, totals[0], totals[1], totals[2], totals[3], totals[4], totals[5], totals[6], totals[7], totals[8], totals[9], totals[10], totals[11], totals[12], totals[13], totals[14])
```

```python
import jax
import jax.numpy as jnp
from jax import lax
from jax.experimental import pallas as pl
from jax.experimental.pallas import tpu as pltpu
from jax.sharding import PartitionSpec as P

HEADDIM = 64
HEADS = 24
STATES = 16
Q = 128
HALO = 16
EXTRA = 128
RUN, DT, DEC, TAIL, SEG, CONT, LAST, LOGDT = 0, 24, 48, 72, 96, 100, 101, 104
COLB, COLC = HEADS, HEADS + STATES

f32 = jnp.float32
bf16 = jnp.bfloat16
highest = lax.Precision.HIGHEST
epsilon = 1e-05
NEG = -1e30


def dot(a, b, precision=None):
    return jnp.dot(a, b, preferred_element_type=f32, precision=precision)


def dot_t(a, b):
    return lax.dot_general(a, b, (((1,), (1,)), ((), ())), preferred_element_type=f32)


def split(v):
    high = v.astype(bf16)
    return high, (v - high.astype(f32)).astype(bf16)


def wide_left(v):
    high, low = split(v)
    return jnp.concatenate([high, low, high], axis=1)


def stack_right(v):
    high, low = split(v)
    return jnp.concatenate([high, high, low], axis=0)


def sigmoid(v):
    return 0.5 * jnp.tanh(0.5 * v) + 0.5


def lanes_of(rows=Q):
    return lax.broadcasted_iota(jnp.int32, (rows, 128), 1)


def pair_cols(col, first, j, left):
    a = col[:, first + 2 * j : first + 2 * j + 1]
    b = col[:, first + 2 * j + 1 : first + 2 * j + 2]
    return jnp.where(left, a, b)


def triangle(strict=False, transposed=False):
    i = lax.broadcasted_iota(jnp.int32, (Q, Q), 1 if transposed else 0)
    k = lax.broadcasted_iota(jnp.int32, (Q, Q), 0 if transposed else 1)
    return (i > k) if strict else (i >= k)


def conv_rows(x_ref, xp_ref, halo_ref, cw_ref, col, q, lanes):
    x = x_ref[:, lanes]
    prev = jnp.where(q == 0, halo_ref[:, lanes], xp_ref[:, lanes])
    cat = jnp.concatenate([prev, x], axis=0)
    acc = cw_ref[4:5, lanes] + cw_ref[0:1, lanes] * x
    shifted = []
    for k in (1, 2, 3):
        back = pltpu.roll(cat, k, 0)[HALO:, :] * col[:, SEG + k : SEG + k + 1]
        shifted.append(back)
        acc = acc + cw_ref[k : k + 1, lanes] * back
    return x, shifted, acc


def conv_state_kernel(
    x_ref, xp_ref, halo_ref, cw_ref, e_ref, hp_ref, mark_ref, u_ref, end_ref, col_ref, row_ref, et_ref
):
    q = pl.program_id(0)

    @pl.when(q == 0)
    def _():
        end_ref[...] = jnp.zeros_like(end_ref)

    e, marks = e_ref[...], mark_ref[...]
    lane = lanes_of()
    head = lane < HEADS
    raw = e + hp_ref[0:1, :]
    dt = jnp.where(head, jnp.maximum(raw, 0.0) + jnp.log1p(jnp.exp(-jnp.abs(raw))), 0.0)
    run = dot(jnp.where(triangle(), 1.0, 0.0), dt * hp_ref[1:2, :], highest)
    dec = jnp.where(head, jnp.exp(run) * marks[:, CONT : CONT + 1], 0.0)
    tail = jnp.where(head, jnp.exp(run[Q - 1 : Q, :] - run) * marks[:, LAST : LAST + 1], 0.0)
    log_dt = jnp.where(head, jnp.log(dt), 0.0)
    col = (
        run
        + pltpu.roll(dt, DT, 1)
        + pltpu.roll(dec, DEC, 1)
        + pltpu.roll(tail, TAIL, 1)
        + marks
        + pltpu.roll(log_dt, LOGDT, 1)
    )
    col_ref[...] = col
    row_ref[...] = col.T
    et = e.T
    et_ref[...] = et
    bt = et[COLB:COLC, :].astype(bf16)
    left = lane < HEADDIM
    for j in range(x_ref.shape[1] // 128):
        lanes = slice(128 * j, 128 * j + 128)
        _, _, acc = conv_rows(x_ref, xp_ref, halo_ref, cw_ref, col, q, lanes)
        u = acc * sigmoid(acc)
        u_ref[:, lanes] = u
        scaled = (u * (pair_cols(col, DT, j, left) * pair_cols(col, TAIL, j, left))).astype(bf16)
        keep = pair_cols(col[Q - 1 : Q, :], DEC, j, left[:1])
        end_ref[:, lanes] = keep * end_ref[:, lanes] + dot(bt, scaled)


def scan_kernel(
    u_ref, z_ref, col_ref, row_ref, e_ref, et_ref, s0_ref, cw_ref, gated_ref, y_ref, st_ref, S
):
    @pl.when(pl.program_id(0) == 0)
    def _():
        S[...] = s0_ref[...]

    col, row = col_ref[...], row_ref[...]
    left = lanes_of() < HEADDIM
    c = e_ref[:, COLC : COLC + STATES]
    bt = et_ref[COLB:COLC, :]
    scores = dot(c, bt, highest)
    neg = jnp.where((col[:, SEG : SEG + 1] == row[SEG : SEG + 1, :]) & triangle(), 0.0, NEG)
    c, bt = wide_left(c), bt.astype(bf16)
    for j in range(u_ref.shape[1] // 128):
        lanes = slice(128 * j, 128 * j + 128)
        uf = u_ref[:, lanes]
        u = uf.astype(bf16)
        state = S[:, lanes]
        st_ref[:, lanes] = state
        parts = []
        for h in (2 * j, 2 * j + 1):
            gap = col[:, h : h + 1] - (row[h : h + 1, :] - row[LOGDT + h : LOGDT + h + 1, :])
            parts.append((jnp.exp(gap + neg) * scores).astype(bf16))
        zero = jnp.zeros_like(u)
        both = jnp.concatenate([jnp.where(left, u, zero), jnp.where(left, zero, u)], axis=0)
        y = dot(jnp.concatenate(parts, axis=1), both)
        y = y + dot(c, stack_right(state)) * pair_cols(col, DEC, j, left) + cw_ref[5:6, lanes] * uf
        z = z_ref[:, lanes]
        y_ref[:, lanes] = y
        gated_ref[:, lanes] = (y * (z * sigmoid(z))).astype(bf16)
        scaled = (uf * (pair_cols(col, DT, j, left) * pair_cols(col, TAIL, j, left))).astype(bf16)
        keep = pair_cols(col[Q - 1 : Q, :], DEC, j, left[:1])
        S[:, lanes] = keep * state + dot(bt, scaled)


def gate_back_kernel(gg_ref, z_ref, y_ref, col_ref, et_ref, dy_ref, dz_ref, ds_ref):
    @pl.when(pl.program_id(0) == 0)
    def _():
        ds_ref[...] = jnp.zeros_like(ds_ref)

    col = col_ref[...]
    left = lanes_of() < HEADDIM
    ct = et_ref[COLC : COLC + STATES, :].astype(bf16)
    for j in range(z_ref.shape[1] // 128):
        lanes = slice(128 * j, 128 * j + 128)
        z = z_ref[:, lanes]
        gg = gg_ref[:, lanes]
        sig = sigmoid(z)
        dy = gg * (z * sig)
        dy_ref[:, lanes] = dy
        dz_ref[:, lanes] = (gg * y_ref[:, lanes] * (sig * (1.0 + z * (1.0 - sig)))).astype(bf16)
        scaled = (dy * pair_cols(col, DEC, j, left)).astype(bf16)
        keep = pair_cols(col[Q - 1 : Q, :], DEC, j, left[:1])
        ds_ref[:, lanes] = keep * ds_ref[:, lanes] + dot(ct, scaled)


def scan_back_kernel(
    u_ref, dy_ref, x_ref, xp_ref, halo_ref, cw_ref, col_ref, row_ref, e_ref, et_ref, st_ref, de_ref, hp_ref,
    lw_ref, sm_ref, pick_ref, head_ref,
    dx_ref, de_out_ref, cg_ref, edge_ref, hg_ref,
    D, WA, CONST, TAILS, DECS, DS, ST, SUMS, DG,
):
    step = pl.program_id(0)
    q = pl.num_programs(0) - 1 - step

    @pl.when(step == 0)
    def _():
        D[...] = de_ref[...]
        cg_ref[...] = jnp.zeros_like(cg_ref)
        edge_ref[...] = jnp.zeros_like(edge_ref)
        hg_ref[...] = jnp.zeros_like(hg_ref)
        WA[...] = jnp.zeros_like(WA)
        CONST[...] = jnp.zeros_like(CONST)
        DS[...] = jnp.zeros_like(DS)
        ST[...] = jnp.zeros_like(ST)

    col, row = col_ref[...], row_ref[...]
    lane = lanes_of()
    left = lane < HEADDIM
    e = e_ref[...]
    b, ct = e[:, COLB:COLC], et_ref[COLC : COLC + STATES, :]
    scores = dot(b, ct, highest)
    neg = jnp.where((col[:, SEG : SEG + 1] == row[SEG : SEG + 1, :]) & triangle(transposed=True), 0.0, NEG)
    b, ct, c = wide_left(b), ct.astype(bf16), wide_left(e[:, COLC : COLC + STATES])
    DG[...] = jnp.zeros_like(DG)
    SUMS[...] = jnp.zeros_like(SUMS)
    for j in range(u_ref.shape[1] // 128):
        lanes = slice(128 * j, 128 * j + 128)
        u = u_ref[:, lanes]
        dyf = dy_ref[:, lanes]
        dy = dyf.astype(bf16)
        dt = pair_cols(col, DT, j, left)
        dec = pair_cols(col, DEC, j, left)
        tail = pair_cols(col, TAIL, j, left)
        keep = pair_cols(col[Q - 1 : Q, :], DEC, j, left[:1])
        state, grad_state = st_ref[:, lanes], D[:, lanes]
        DS[COLB:COLC, lanes] = grad_state
        ST[COLC : COLC + STATES, lanes] = state
        xs = u * dt
        zero = jnp.zeros_like(dy)
        both = jnp.concatenate([jnp.where(left, dy, zero), jnp.where(left, zero, dy)], axis=0)
        d_mat = dot_t(xs.astype(bf16), both)
        mats, pairs, d_scores = [], [], None
        for i, h in enumerate((2 * j, 2 * j + 1)):
            decay = jnp.exp((row[h : h + 1, :] - col[:, h : h + 1]) + neg)
            mat = decay * scores
            dm = d_mat[:, Q * i : Q * i + Q]
            d_scores = decay * dm if d_scores is None else d_scores + decay * dm
            mats.append(mat.astype(bf16))
            pairs.append((mat * dm).astype(bf16))
        DG[...] += d_scores
        dxs = dot(jnp.concatenate(mats, axis=1), both)
        spans = dot(jnp.concatenate(pairs, axis=1), lw_ref[...]) * sm_ref[...]
        sums = jnp.sum(spans, axis=0, keepdims=True)
        WA[2 * j : 2 * j + 1, :] = sums[:, :Q]
        WA[2 * j + 1 : 2 * j + 2, :] = sums[:, Q:]
        from_tail = tail * dot(b, stack_right(grad_state))
        dxs = dxs + from_tail
        ydec = dyf * dec
        found = [u * dxs, ydec * dot(c, stack_right(state)), xs * from_tail]
        SUMS[...] += dot(jnp.concatenate([v.astype(bf16) for v in found], axis=1), pick_ref[j])
        TAILS[:, lanes] = (xs * tail).astype(bf16)
        low_dec = ydec.astype(bf16)
        DECS[:, lanes] = low_dec
        CONST[0:1, lanes] = keep * jnp.sum(state * grad_state, axis=0, keepdims=True)
        D[:, lanes] = keep * grad_state + dot(ct, low_dec)

        x, shifted, acc = conv_rows(x_ref, xp_ref, halo_ref, cw_ref, col, q, lanes)
        sig = sigmoid(acc)
        dconv = (dxs * dt + cw_ref[5:6, lanes] * dyf) * (sig * (1.0 + acc * (1.0 - sig)))
        dx = cw_ref[0:1, lanes] * dconv
        cg_ref[0:1, lanes] += jnp.sum(dconv * x, axis=0, keepdims=True)
        for k in (1, 2, 3):
            masked = dconv * col[:, SEG + k : SEG + k + 1]
            after = edge_ref[8 * (k - 1) : 8 * k, lanes]
            cat = jnp.concatenate([masked, after], axis=0)
            dx = dx + cw_ref[k : k + 1, lanes] * pltpu.roll(cat, Q + 8 - k, 0)[:Q, :]
            edge_ref[8 * (k - 1) : 8 * k, lanes] = masked[:8, :]
            cg_ref[k : k + 1, lanes] += jnp.sum(dconv * shifted[k - 1], axis=0, keepdims=True)
        cg_ref[4:5, lanes] += jnp.sum(dconv, axis=0, keepdims=True)
        cg_ref[5:6, lanes] += jnp.sum(dyf * u, axis=0, keepdims=True)
        dx_ref[:, lanes] = dx.astype(bf16)

    head = lane < HEADS
    found = SUMS[...]
    suffix = jnp.where(triangle(transposed=True), 1.0, 0.0)
    prefix = jnp.where(triangle(strict=True), 1.0, 0.0)
    d_step = (
        WA[...].T
        + dot(suffix, pltpu.roll(found, 128 - HEADS, 1), highest)
        + dot(prefix, pltpu.roll(found, 128 - 2 * HEADS, 1), highest)
        + dot(CONST[...], head_ref[...], highest)[0:1, :]
    )
    d_dt = d_step * hp_ref[1:2, :] + found
    d_raw = jnp.where(head, d_dt * sigmoid(e + hp_ref[0:1, :]), 0.0)
    step_dt = jnp.where(head, pltpu.roll(col, 128 - DT, 1), 0.0)
    hg_ref[0:1, :] += jnp.sum(d_raw, axis=0, keepdims=True)
    hg_ref[1:2, :] += jnp.sum(jnp.where(head, d_step, 0.0) * step_dt, axis=0, keepdims=True) * hp_ref[1:2, :]
    total = DG[...]
    b_part = jnp.where((lane >= COLB) & (lane < COLC), e, 0.0)
    c_part = jnp.where((lane >= COLC) & (lane < COLC + STATES), e, 0.0)
    de_out_ref[...] = (
        d_raw
        + dot_t(TAILS[...], DS[...].astype(bf16))
        + dot_t(DECS[...], ST[...].astype(bf16))
        + dot(total, pltpu.roll(c_part, 128 - STATES, 1), highest)
        + dot(total.T, pltpu.roll(b_part, STATES, 1), highest)
    )


def norm_kernel(*refs):
    *row_refs, gain_ref, hidden_ref, out_ref, turned_ref = refs
    rows = row_refs[0][...]
    for r in row_refs[1:]:
        rows = rows + r[...]
    hidden_ref[...] = rows
    scale = lax.rsqrt(jnp.mean(rows * rows, axis=-1, keepdims=True) + epsilon)
    normed = rows * scale * gain_ref[...]
    out_ref[...] = normed.astype(bf16)
    turned_ref[...] = normed.T.astype(bf16)


def norm_back_kernel(grad_ref, rows_ref, gain_ref, *refs):
    *base_refs, high_ref, low_ref, part_ref, turned_ref = refs

    @pl.when(pl.program_id(0) == 0)
    def _():
        part_ref[...] = jnp.zeros_like(part_ref)

    rows, grad = rows_ref[...], grad_ref[...]
    scale = lax.rsqrt(jnp.mean(rows * rows, axis=-1, keepdims=True) + epsilon)
    unit = rows * scale
    part_ref[0:1, :] += jnp.sum(grad * unit, axis=0, keepdims=True)
    unit_grad = grad * gain_ref[...]
    total = scale * (unit_grad - unit * jnp.mean(unit_grad * unit, axis=-1, keepdims=True))
    for r in base_refs:
        total = total + r[...].astype(f32)
    high = total.astype(bf16)
    high_ref[...] = high
    low_ref[...] = (total - high.astype(f32)).astype(bf16)
    turned_ref[...] = total.T.astype(bf16)


def flip(i, mask):
    bit = 1
    while bit <= mask:
        if mask & bit:
            i = i + bit * (1 - 2 * ((i // bit) % 2))
        bit *= 2
    return i


class Load:
    def __init__(self, *movers):
        self.reads, self.updates, self.news, self.copies = {}, {}, {}, []
        self.movers = movers
        for mover in movers:
            reads, updates, news, copies = mover.moves()
            self.reads.update(reads)
            self.updates.update(updates)
            self.news.update(news)
            self.copies += copies

    def arrive(self, got):
        for mover in self.movers:
            mover.take(got)


IDS = {}


def run(body, grid, in_specs, out_specs, out_shape, scratch, args, name, estimate=None, load=None, vmem=56):
    params = dict(dimension_semantics=("arbitrary",) * len(grid), vmem_limit_bytes=vmem * 1024 * 1024)
    if load is None:
        return pl.pallas_call(
            body, name=name, grid=grid, in_specs=in_specs, out_specs=out_specs, out_shape=out_shape,
            scratch_shapes=scratch, compiler_params=pltpu.CompilerParams(**params), cost_estimate=estimate,
        )(*args)
    cid = IDS.setdefault(name, len(IDS) + 1)
    reads, updates, news = list(load.reads), list(load.updates), list(load.news)
    n_in, n_out, n_scratch, n_copies = len(args), len(out_shape), len(scratch), len(load.copies)
    routes = []
    for c in load.copies:
        if c[4] is not None and c[4] not in routes:
            routes.append(c[4])

    def kernel(*refs):
        ins, rest = refs[:n_in], refs[n_in:]
        held = dict(zip(reads, rest))
        rest = rest[len(reads) + len(updates) :]
        outs, rest = rest[:n_out], rest[n_out:]
        held.update(zip(updates + news, rest))
        rest = rest[len(updates) + len(news) :]
        mine, (send, recv) = rest[:n_scratch], rest[n_scratch:]

        def device(route):
            return {route[0]: flip(lax.axis_index(route[0]), route[1])}

        def make(i, c):
            src, dst = held[c[0]].at[c[1]], held[c[2]].at[c[3]]
            if c[4] is None:
                return pltpu.make_async_copy(src, dst, recv.at[i])
            return pltpu.make_async_remote_copy(
                src_ref=src, dst_ref=dst, send_sem=send.at[i], recv_sem=recv.at[i],
                device_id=device(c[4]), device_id_type=pl.DeviceIdType.MESH,
            )

        first, last = pl.program_id(0) == 0, pl.program_id(0) == grid[0] - 1
        for axis in range(1, len(grid)):
            first = first & (pl.program_id(axis) == 0)
            last = last & (pl.program_id(axis) == grid[axis] - 1)

        @pl.when(first)
        def _():
            barrier = pltpu.get_barrier_semaphore()
            for route in routes:
                pl.semaphore_signal(
                    barrier, inc=1, device_id=device(route), device_id_type=pl.DeviceIdType.MESH
                )
            pl.semaphore_wait(barrier, len(routes))
            for i, c in enumerate(load.copies):
                make(i, c).start()

        if body is not None:
            body(*ins, *outs, *mine)

        @pl.when(last)
        def _():
            for i, c in enumerate(load.copies):
                make(i, c).wait()

    hbm = pl.BlockSpec(memory_space=pltpu.HBM)
    result = pl.pallas_call(
        kernel,
        name=name,
        grid=grid,
        in_specs=list(in_specs) + [hbm] * (len(reads) + len(updates)),
        out_specs=list(out_specs) + [hbm] * (len(updates) + len(news)),
        out_shape=list(out_shape)
        + [jax.ShapeDtypeStruct(load.updates[k].shape, load.updates[k].dtype) for k in updates]
        + [load.news[k] for k in news],
        scratch_shapes=list(scratch) + [pltpu.SemaphoreType.DMA((n_copies,)), pltpu.SemaphoreType.DMA((n_copies,))],
        input_output_aliases={n_in + len(reads) + i: n_out + i for i in range(len(updates))},
        compiler_params=pltpu.CompilerParams(collective_id=cid, has_side_effects=True, **params),
        cost_estimate=estimate,
    )(*args, *[load.reads[k] for k in reads], *[load.updates[k] for k in updates])
    load.arrive(dict(zip(updates + news, result[n_out:])))
    return result[:n_out]


def matmul(jobs, dtype, tile, name, load=None, nt=False, turned=False):
    n_jobs, n_pairs = len(jobs), len(jobs[0])
    rows = jobs[0][0][0].shape[0]
    columns = jobs[0][0][1].shape[0 if nt else 1]
    tiles = columns // tile

    def at(job):
        def place(j, t):
            return jnp.where(j == job, t, jnp.where(j < job, 0, tiles - 1))

        return place

    args, in_specs = [], []
    for job, pairs in enumerate(jobs):
        for left, right in pairs:
            args += [left, right]
            k = left.shape[1]
            in_specs.append(pl.BlockSpec((rows, k), lambda j, t: (0, 0), pipeline_mode=pl.Buffered(1)))
            if nt:
                in_specs.append(pl.BlockSpec((tile, k), lambda j, t, p=at(job): (p(j, t), 0)))
            else:
                in_specs.append(pl.BlockSpec((k, tile), lambda j, t, p=at(job): (0, p(j, t))))
    out_specs = [pl.BlockSpec((rows, tile), lambda j, t, p=at(job): (0, p(j, t))) for job in range(n_jobs)]
    out_shape = [jax.ShapeDtypeStruct((rows, columns), dtype)] * n_jobs
    if turned:
        out_specs += [pl.BlockSpec((tile, rows), lambda j, t, p=at(job): (p(j, t), 0)) for job in range(n_jobs)]
        out_shape += [jax.ShapeDtypeStruct((columns, rows), dtype)] * n_jobs

    def body(*refs):
        ins, outs = refs[: 2 * n_jobs * n_pairs], refs[2 * n_jobs * n_pairs :]
        for job in range(n_jobs):

            @pl.when(pl.program_id(0) == job)
            def _(job=job):
                total = None
                for p in range(n_pairs):
                    left, right = ins[2 * (job * n_pairs + p)], ins[2 * (job * n_pairs + p) + 1]
                    term = (dot_t if nt else dot)(left[...], right[...])
                    total = term if total is None else total + term
                outs[job][...] = total.astype(dtype)
                if turned:
                    outs[n_jobs + job][...] = total.T.astype(dtype)

    depth = sum(p[0].shape[1] for p in jobs[0])
    return run(
        body, (n_jobs, tiles), in_specs, out_specs, out_shape, [], args, name,
        pl.CostEstimate(
            flops=2 * n_jobs * rows * columns * depth, bytes_accessed=4 * n_jobs * rows * columns, transcendentals=0
        ),
        load,
    )


def feed_forward(normed, cot, gate_w, up_w, down_w):
    tokens, width = normed.shape
    cols, tile, step = gate_w[0].shape[1], 512, 256
    tiles = cols // tile

    def at(job):
        def place(j, t):
            return jnp.where(j == job, t, jnp.where(j < job, 0, tiles - 1))

        return place

    whole = pl.BlockSpec((tokens, width), lambda j, t: (0, 0), pipeline_mode=pl.Buffered(1))
    args, in_specs, out_specs = [normed, cot], [whole, whole], []
    for b in (0, 1):
        args += [gate_w[b], up_w[b], down_w[b]]
        in_specs += [pl.BlockSpec((width, tile), lambda j, t, p=at(b): (0, p(j, t)))] * 3
        out_specs += [pl.BlockSpec((tokens, tile), lambda j, t, p=at(b): (0, p(j, t)))] * 3

    def body(n_ref, c_ref, *refs):
        for b in (0, 1):
            wg, wu, wd = refs[3 * b : 3 * b + 3]
            act, gg, ug = refs[6 + 3 * b : 9 + 3 * b]

            @pl.when(pl.program_id(0) == b)
            def _(wg=wg, wu=wu, wd=wd, act=act, gg=gg, ug=ug):
                for i in range(tokens // step):
                    rows = slice(step * i, step * i + step)
                    gate, up, back = dot(n_ref[rows, :], wg[...]), dot(n_ref[rows, :], wu[...]), dot(c_ref[rows, :], wd[...])
                    sig = sigmoid(gate)
                    silu = gate * sig
                    act[rows, :] = (silu * up).astype(bf16)
                    gg[rows, :] = (back * up * sig * (1.0 + gate * (1.0 - sig))).astype(bf16)
                    ug[rows, :] = (back * silu).astype(bf16)

    out = run(
        body, (2, tiles), in_specs, out_specs, [jax.ShapeDtypeStruct((tokens, cols), bf16)] * 6, [], args,
        "feed_forward", pl.CostEstimate(flops=12 * tokens * cols * width, bytes_accessed=12 * tokens * cols, transcendentals=0),
    )
    return [out[0], out[3]], [out[1], out[4]], [out[2], out[5]]


def carry_only(load, name):
    run(None, (1,), [], [], [], [], [], name, None, load)


ALL = (slice(None),)


def low_sum(a, b):
    return (a.astype(f32) + b.astype(f32)).astype(bf16)


class Gather:
    def __init__(self, key, shard, n):
        rows, cols = shard.shape
        self.n, self.key, self.phase = n, key, 0
        self.shard = shard.reshape(2, rows // 2, cols)
        self.cols = cols

    def moves(self):
        k, n = self.key, self.n
        q = n // 4
        s, a, b = k + "s", k + "0", k + "1"
        if self.phase == 0:
            whole = jax.ShapeDtypeStruct((2, n) + self.shard.shape[1:], bf16)
            copies = [
                (s, (i,), a, (i, m), ("fsdp", m << 2) if m else None) for m in range(q) for i in (0, 1)
            ]
            return {s: self.shard}, {}, {a: whole, b: whole}, copies
        near, far, both = slice(0, q), slice(q, 2 * q), slice(0, 2 * q)
        if self.phase == 1:
            copies = [(a, (0, near), b, (0, near), ("tp", 1)), (a, (1, near), a, (1, far), ("fsdp", 2))]
        elif self.phase == 2:
            copies = [
                (a, (0, near), a, (0, far), ("fsdp", 2)),
                (b, (0, near), b, (0, far), ("fsdp", 2)),
                (a, (1, both), b, (1, both), ("tp", 1)),
            ]
        else:
            copies = [(h, (i, both), h, (i, slice(2 * q, 4 * q)), ("fsdp", 1)) for h in (a, b) for i in (0, 1)]
        return {}, {a: self.halves[0], b: self.halves[1]}, {}, copies

    def take(self, got):
        self.halves = [got[self.key + "0"], got[self.key + "1"]]
        self.phase += 1
        if self.phase == 4:
            self.full = [h.reshape(-1, self.cols) for h in self.halves]


class Scatter:
    def __init__(self, key, grads, n, piece=0, pieces=1):
        self.n, self.key, self.phase = n, f"{key}{piece}_", 0
        cols = grads[0].shape[1]
        self.cols = cols // pieces
        self.rows = grads[0].shape[0] // n
        self.now = [g.reshape(2, n, self.rows // 2, cols) for g in grads]
        self.range = slice(piece * self.cols, (piece + 1) * self.cols)

    def moves(self):
        n, v = self.n, self.now
        q = n // 4
        part = (self.rows // 2, self.cols)
        far, rest = slice(q, 2 * q), slice(2 * q, 4 * q)

        def name(i):
            return f"{self.key}{i}"

        def new(*dims):
            return jax.ShapeDtypeStruct(dims + part, bf16)

        if self.phase == 0:
            news = [new(2, 2 * q), new(2, 2 * q)]
            copies = [
                (b, (i, rest, slice(None), self.range), b, (i,), ("fsdp", 1)) for b in (0, 1) for i in (0, 1)
            ]
        elif self.phase == 1:
            news = [new(q), new(q), new(2 * q)]
            copies = [
                (0, (0, far), 0, ALL, ("fsdp", 2)),
                (1, (0, far), 1, ALL, ("fsdp", 2)),
                (1, (1,), 2, ALL, ("tp", 1)),
            ]
        elif self.phase == 2:
            news = [new(q), new(q)]
            copies = [(1, ALL, 0, ALL, ("tp", 1)), (2, (far,), 1, ALL, ("fsdp", 2))]
        else:
            news = [new(2) for _ in range(1, q)]
            copies = [(i, (m,), m - 1, (i,), ("fsdp", m << 2)) for m in range(1, q) for i in (0, 1)]
        reads = {name(f"v{i}"): a for i, a in enumerate(v) if any(c[0] == i for c in copies)}
        self.names = [name(f"r{i}") for i in range(len(news))]
        copies = [(name(f"v{c[0]}"), c[1], self.names[c[2]], c[3], c[4]) for c in copies]
        return reads, {}, dict(zip(self.names, news)), copies

    def take(self, got):
        r, v = [got[k] for k in self.names], self.now
        q = self.n // 4
        if self.phase == 0:
            self.now = [low_sum(p[:, : 2 * q, :, self.range], a) for p, a in zip(v, r)]
        elif self.phase == 1:
            self.now = [low_sum(v[0][0, :q], r[0]), low_sum(v[1][0, :q], r[1]), low_sum(v[0][1], r[2])]
        elif self.phase == 2:
            self.now = [low_sum(v[0], r[0]), low_sum(v[2][:q], r[1])]
        else:
            total = jnp.stack([v[0][0], v[1][0]]).astype(f32)
            for p in r:
                total = total + p.astype(f32)
            self.out = total.reshape(self.rows, self.cols)
        self.phase += 1


def specs(blocks, ch, reverse):
    def at(q):
        return blocks - 1 - q if reverse else q

    def whole(rows, cols):
        return pl.BlockSpec((rows, cols), lambda q: (0, 0))

    return dict(
        main=pl.BlockSpec((Q, ch), lambda q: (at(q), 0)),
        prev=pl.BlockSpec((HALO, ch), lambda q: (jnp.maximum(at(q) * (Q // HALO) - 1, 0), 0)),
        tile=pl.BlockSpec((Q, 128), lambda q: (at(q), 0)),
        state=pl.BlockSpec((STATES, ch), lambda q: (at(q), 0)),
        halo=whole(HALO, ch), row8=whole(8, ch), row24=whole(24, ch), row16=whole(STATES, ch), small=whole(8, 128),
    )


def shape(dims, dtype):
    return jax.ShapeDtypeStruct(dims, dtype)


def cost(flops, moved):
    return pl.CostEstimate(flops=int(flops), bytes_accessed=int(moved), transcendentals=0)


def conv_state(x, halo, cw, e, hp, marks, tag="", load=None):
    tokens, ch = x.shape
    s = specs(tokens // Q, ch, False)
    return run(
        conv_state_kernel,
        (tokens // Q,),
        [s["main"], s["prev"], s["halo"], s["row8"], s["tile"], s["small"], s["tile"]],
        [s["main"], s["row16"], s["tile"], s["tile"], s["tile"]],
        [shape((tokens, ch), f32), shape((STATES, ch), f32)] + [shape((tokens, 128), f32)] * 3,
        [],
        [x, x, halo, cw, e, hp, marks],
        "conv_state" + tag,
        cost(tokens * ch * 5000, 4 * tokens * ch),
        load,
    )


def scan_forward(u, z, col, row, e, et, s0, cw, tag="", load=None):
    tokens, ch = u.shape
    s = specs(tokens // Q, ch, False)
    return run(
        scan_kernel,
        (tokens // Q,),
        [s["main"], s["main"], s["tile"], s["tile"], s["tile"], s["tile"], s["row16"], s["row8"]],
        [s["main"], s["main"], s["state"]],
        [shape((tokens, ch), bf16), shape((tokens, ch), f32), shape((tokens // Q * STATES, ch), f32)],
        [pltpu.VMEM((STATES, ch), f32)],
        [u, z, col, row, e, et, s0, cw],
        "scan_forward" + tag,
        cost(tokens * ch * 10000, 8 * tokens * ch),
        load,
    )


def gate_backward(gg, z, y, col, et, tag="", load=None):
    tokens, ch = z.shape
    s = specs(tokens // Q, ch, True)
    return run(
        gate_back_kernel,
        (tokens // Q,),
        [s["main"], s["main"], s["main"], s["tile"], s["tile"]],
        [s["main"], s["main"], s["row16"]],
        [shape((tokens, ch), f32), shape((tokens, ch), bf16), shape((STATES, ch), f32)],
        [],
        [gg, z, y, col, et],
        "gate_backward" + tag,
        cost(tokens * ch * 5000, 10 * tokens * ch),
        load,
    )


def scan_backward(u, dy, x, halo, cw, col, row, e, et, st, de, hp, tag="", load=None):
    tokens, ch = u.shape
    s = specs(tokens // Q, ch, True)
    place = jnp.arange(2 * Q)
    lower = ((place[:, None] >= place[None, :]) & (place[:, None] // Q == place[None, :] // Q)).astype(bf16)
    strict = (jnp.arange(Q)[:, None] < (place % Q)[None, :]).astype(f32)
    pairs = ch // 128
    lane = jnp.arange(3 * 128)
    target = (lane // 128) * HEADS + 2 * jnp.arange(pairs)[:, None] + ((lane % 128) // HEADDIM)[None, :]
    pick = (target[:, :, None] == jnp.arange(128)[None, None, :]).astype(bf16)
    by_head = (jnp.arange(ch)[:, None] // HEADDIM == jnp.arange(128)[None, :]).astype(f32)
    return run(
        scan_back_kernel,
        (tokens // Q,),
        [
            s["main"], s["main"], s["main"], s["prev"], s["halo"], s["row8"], s["tile"], s["tile"], s["tile"],
            s["tile"], s["state"], s["row16"], s["small"],
            pl.BlockSpec((2 * Q, 2 * Q), lambda q: (0, 0)), pl.BlockSpec((Q, 2 * Q), lambda q: (0, 0)),
            pl.BlockSpec((pairs, 3 * 128, 128), lambda q: (0, 0, 0)), pl.BlockSpec((ch, 128), lambda q: (0, 0)),
        ],
        [s["main"], s["tile"], s["row8"], s["row24"], s["small"]],
        [
            shape((tokens, ch), bf16), shape((tokens, 128), f32), shape((8, ch), f32), shape((24, ch), f32),
            shape((8, 128), f32),
        ],
        [
            pltpu.VMEM((STATES, ch), f32), pltpu.VMEM((128, Q), f32), pltpu.VMEM((8, ch), f32),
            pltpu.VMEM((Q, ch), bf16), pltpu.VMEM((Q, ch), bf16), pltpu.VMEM((128, ch), f32),
            pltpu.VMEM((128, ch), f32), pltpu.VMEM((Q, 128), f32), pltpu.VMEM((Q, Q), f32),
        ],
        [u, dy, x, x, halo, cw, col, row, e, et, st, de, hp, lower, strict, pick, by_head],
        "scan_backward" + tag,
        cost(tokens * ch * 25000, 12 * tokens * ch),
        load,
    )


def norm_specs(width):
    main = pl.BlockSpec((Q, width), lambda q: (q, 0))
    return main, pl.BlockSpec((width, Q), lambda q: (0, q)), pl.BlockSpec((1, width), lambda q: (0, 0))


def norm_forward(rows, gain_row, name, load=None):
    tokens, width = rows[0].shape
    main, turned, one = norm_specs(width)
    return run(
        norm_kernel,
        (tokens // Q,),
        [main] * len(rows) + [one],
        [main, main, turned],
        [shape((tokens, width), f32), shape((tokens, width), bf16), shape((width, tokens), bf16)],
        [],
        [*rows, gain_row],
        name,
        cost(tokens * width * 20, 12 * tokens * width),
        load,
    )


def norm_back(grad, rows, gain_row, bases, name, load=None):
    tokens, width = rows.shape
    main, turned, one = norm_specs(width)
    high, low, part, high_t = run(
        norm_back_kernel,
        (tokens // Q,),
        [main, main, one] + [main] * len(bases),
        [main, main, pl.BlockSpec((8, width), lambda q: (0, 0)), turned],
        [
            shape((tokens, width), bf16), shape((tokens, width), bf16), shape((8, width), f32),
            shape((width, tokens), bf16),
        ],
        [],
        [grad, rows, gain_row, *bases],
        name,
        cost(tokens * width * 20, 16 * tokens * width),
        load,
    )
    return high, low, high_t, part[0]


def token_marks(seg, seg_before):
    tokens = seg.shape[0]
    by_block = seg.reshape(tokens // Q, Q)
    before = jnp.concatenate([seg_before[2:3], by_block[:-1, Q - 1]])
    padded = jnp.concatenate([seg_before, seg])
    found = [seg.astype(f32)] + [(padded[3 - k : 3 - k + tokens] == seg).astype(f32) for k in (1, 2, 3)]
    found.append((by_block == before[:, None]).astype(f32).reshape(-1))
    found.append((by_block == by_block[:, Q - 1 :]).astype(f32).reshape(-1))
    lane = jnp.arange(128)[None, :]
    out = jnp.zeros((tokens, 128), f32)
    for i, v in enumerate(found):
        out = jnp.where(lane == SEG + i, v[:, None], out)
    return out


def swap(x, axis, n, mask):
    return lax.ppermute(x, axis, [(i, i ^ mask) for i in range(n)])


def sum_all(x, n):
    bit = 1
    while bit < n:
        x = x + swap(x, "fsdp", n, bit)
        bit *= 2
    return x


def bf_dot(a, b):
    return jnp.dot(a, b, preferred_element_type=f32)


def make_local(n):
    def local(
        layer_in, seg_ids, gain_one, x_weight, z_weight, dt_weight, bc_weight, conv_weight, conv_bias,
        dt_bias, a_log, d_skip, out_weight, gain_two, gate_weight, up_weight, down_weight, cotangent,
    ):
        tokens, width = layer_in.shape
        rows, ch = x_weight.shape
        heads = dt_weight.shape[1]
        states = bc_weight.shape[1] // 2
        me, half = lax.axis_index("fsdp"), lax.axis_index("tp")

        epack = jnp.concatenate([dt_weight, bc_weight, jnp.zeros((rows, EXTRA - heads - 2 * states), bf16)], axis=1)
        X, E = Gather("x", x_weight, n), Gather("e", epack, n)
        Z, O = Gather("z", z_weight, n), Gather("o", out_weight, n)
        G, U, D = Gather("g", gate_weight, n), Gather("u", up_weight, n), Gather("d", down_weight, n)

        rate = -jnp.exp(a_log)
        pad = jnp.zeros((128 - heads,), f32)
        by_head = jnp.stack([jnp.concatenate([dt_bias, pad]), jnp.concatenate([rate, pad])])
        small = jnp.concatenate(
            [
                conv_weight,
                conv_bias[None, :],
                jnp.repeat(d_skip, HEADDIM)[None, :],
                jnp.pad(by_head, ((0, 0), (0, ch - 128))),
            ],
            axis=0,
        )
        smalls = [small, swap(small, "tp", 2, 1)]
        head_rows = [jnp.pad(v[6:8, :128], ((0, 6), (0, 0))) for v in smalls]
        before_rows = lax.ppermute(layer_in[tokens - HALO :], "tp", [(0, 1)])
        seg = lax.dynamic_slice(seg_ids, (half * tokens,), (tokens,))
        seg_before = jnp.where(half == 0, -1, seg_ids[tokens - 3 : tokens])

        part = rows // 2
        place = jnp.arange(2 * n)
        q = n // 4
        p = place % n
        part_at = (me ^ (p // (2 * q) + 2 * ((p // q) % 2) + 4 * (p % q))) * 2 + place // n
        seek = (place // 2) ^ me
        place_of = (place % 2) * n + (seek % 2) * 2 * q + ((seek // 2) % 2) * q + seek // 4
        col_at = (part_at[:, None] * part + jnp.arange(part)[None, :]).reshape(-1)
        turn = (jnp.arange(width)[:, None] == col_at[None, :]).astype(bf16)

        def to_local(v):
            return jnp.take(v.reshape(2 * n, part), part_at, axis=0).reshape(-1)

        def to_global(v):
            return jnp.take(v.reshape(2 * n, part), place_of, axis=0).reshape(-1)

        gain_one, gain_two = to_local(gain_one)[None, :], to_local(gain_two)[None, :]
        (rows_in,) = matmul([[(layer_in, turn)]], f32, 512, "turn_rows", Load(X, E))
        rows_in, normed, normed_t = norm_forward([rows_in], gain_one, "norm_one", Load(X, E, Z))
        cot_low, cot_t = matmul([[(cotangent, turn)]], bf16, 512, "turn_cotangent", Load(X, E, O), turned=True)
        carry_only(Load(X, E, Z), "carry_one")
        halo_rows = bf_dot(before_rows, turn)
        halo_scale = lax.rsqrt(jnp.mean(halo_rows * halo_rows, axis=-1, keepdims=True) + epsilon)
        normed_before = (halo_rows * halo_scale * gain_one).astype(bf16)
        marks = token_marks(seg, seg_before)

        xs = matmul([[(normed, w)] for w in X.full], f32, 512, "project_x", Load(Z, O, G))
        saved = []
        for b in (0, 1):
            v = dict(x=xs[b], cw=smalls[b], hp=head_rows[b])
            v["e"] = bf_dot(normed, E.full[b])
            v["halo"] = bf_dot(normed_before, X.full[b])
            load = Load(Z, O, U) if b == 0 else Load(G, O, D)
            v["u"], v["end"], v["col"], v["row"], v["et"] = conv_state(
                v["x"], v["halo"], v["cw"], v["e"], v["hp"], marks, tag=str(b), load=load
            )
            saved.append(v)
        starts = lax.ppermute(jnp.stack([v["end"] for v in saved]), "tp", [(0, 1)])[::-1]
        zs = matmul([[(normed, w)] for w in Z.full], f32, 512, "project_z", Load(G))
        for b in (0, 1):
            v = saved[b]
            v["z"] = zs[b]
            v["gated"], v["y"], v["states"] = scan_forward(
                v["u"], v["z"], v["col"], v["row"], v["e"], v["et"], starts[b], v["cw"],
                tag=str(b), load=Load(G, U, D) if b == 0 else Load(U),
            )
        (mixed,) = matmul(
            [[(v["gated"], w) for v, w in zip(saved, O.full)]], f32, 512, "project_out", Load(U, D), nt=True
        )
        hidden, normed_two, two_t = norm_forward([rows_in, mixed], gain_two, "norm_two", Load(D))

        acts, gate_grads, up_grads = feed_forward(normed_two, cot_low, G.full, U.full, D.full)
        def halves(key, grads):
            return [Scatter(key, grads, n, i, 2) for i in (0, 1)]

        da, db = halves("d", matmul([[(cot_t, a)] for a in acts], bf16, 512, "down_grad"))
        ga, gb = halves("g", matmul([[(two_t, a)] for a in gate_grads], bf16, 512, "gate_grad", Load(da, db)))
        ua, ub = halves("u", matmul([[(two_t, a)] for a in up_grads], bf16, 512, "up_grad", Load(da, ga, gb)))
        (fed,) = matmul([list(zip(acts, D.full))], f32, 512, "project_down", Load(db, da, ua, ub), nt=True)
        layer_out = matmul([[((hidden + fed).astype(bf16), turn)]], bf16, 512, "turn_out", nt=True)[0]
        (grad_two,) = matmul(
            [list(zip(gate_grads, G.full)) + list(zip(up_grads, U.full))], f32, 256, "two_back",
            Load(ga, gb, db, da), nt=True,
        )
        mixed_grad, mixed_low, mixed_t, gain_two_part = norm_back(
            grad_two, hidden, gain_two, [cot_low], "norm_two_back", Load(ga, db)
        )

        so = Scatter("o", matmul([[(mixed_t, v["gated"])] for v in saved], bf16, 512, "out_grad", Load(ua, ga)), n)
        gg = matmul([[(mixed_grad, w)] for w in O.full], f32, 512, "gated_back", Load(gb, so))
        for b in (0, 1):
            v = saved[b]
            v["dy"], v["dz"], v["ds"] = gate_backward(
                gg[b], v["z"], v["y"], v["col"], v["et"], tag=str(b), load=Load(ua, gb) if b == 0 else None
            )
        ends = lax.ppermute(jnp.stack([v["ds"] for v in saved]), "tp", [(1, 0)])[::-1]
        sz = Scatter("z", matmul([[(normed_t, v["dz"])] for v in saved], bf16, 512, "z_grad", Load(ub, ua)), n)
        for b in (0, 1):
            v = saved[b]
            v["dx"], v["de"], v["cg"], v["edge"], v["hg"] = scan_backward(
                v["u"], v["dy"], v["x"], v["halo"], v["cw"], v["col"], v["row"], v["e"], v["et"], v["states"],
                ends[b], v["hp"], tag=str(b), load=Load(sz, so, ub) if b else Load(so, ub, sz),
            )
        edges = lax.ppermute(jnp.stack([v["edge"] for v in saved]), "tp", [(1, 0)])[::-1]
        shared = 0.5 * (saved[0]["de"] + saved[1]["de"])
        own_lane = jnp.arange(EXTRA)[None, :] < heads
        for b in (0, 1):
            v = saved[b]
            cw, edge = v["cw"], edges[b].reshape(3, 8, ch)
            fix = [jnp.zeros((HALO - 3, ch), f32)]
            for j in (3, 2, 1):
                fix.append(sum(cw[k : k + 1] * edge[k - 1, k - j : k - j + 1] for k in range(j, 4)))
            last = v["dx"][tokens - HALO :].astype(f32) + jnp.concatenate(fix, axis=0)
            v["dx"] = lax.dynamic_update_slice(v["dx"], last.astype(bf16), (tokens - HALO, 0))
            v["de"] = jnp.where(own_lane, v["de"], shared).astype(bf16)
        xa, xb = halves("x", matmul([[(normed_t, v["dx"])] for v in saved], bf16, 512, "x_grad", Load(sz, so)))
        se = Scatter("e", matmul([[(normed_t, v["de"])] for v in saved], bf16, 128, "e_grad"), n)
        pairs = [(v["dx"], w) for v, w in zip(saved, X.full)] + [(v["de"], w) for v, w in zip(saved, E.full)]
        (grad_x,) = matmul([pairs], f32, 512, "x_back", Load(xa, xb, se, sz), nt=True)
        (grad_z,) = matmul([[(v["dz"], w) for v, w in zip(saved, Z.full)]], f32, 512, "z_back", Load(xa, xb, se), nt=True)
        high, low, _, gain_one_part = norm_back(
            grad_x + grad_z, rows_in, gain_one, [mixed_grad, mixed_low], "norm_one_back", Load(xa, xb, se)
        )
        (input_grad,) = matmul([[(high, turn), (low, turn)]], f32, 512, "turn_back", Load(xa, xb, se), nt=True)

        def small_row(v):
            cg, hg = v["cg"], v["hg"]
            skip = jnp.sum(cg[5].reshape(heads, HEADDIM), axis=1)
            return jnp.concatenate([cg[:5].reshape(-1), hg[0, :heads], hg[1, :heads], skip])

        gains = jnp.concatenate([to_global(gain_one_part), to_global(gain_two_part)])
        own = jnp.concatenate([small_row(saved[0]), gains])
        other = jnp.concatenate([small_row(saved[1]), gains])
        total = sum_all(own + swap(other, "tp", 2, 1), n)
        base = 5 * ch
        dt_b_total, a_total, skip_total = (total[base + heads * i : base + heads * (i + 1)] for i in range(3))
        base += 3 * heads
        return (
            layer_out,
            input_grad,
            total[base : base + width],
            jnp.concatenate([xa.out, xb.out], axis=1),
            sz.out,
            se.out[:, :heads],
            2.0 * se.out[:, heads : heads + 2 * states],
            total[: 4 * ch].reshape(4, ch),
            total[4 * ch : 5 * ch],
            dt_b_total,
            a_total,
            skip_total,
            so.out,
            total[base + width :],
            jnp.concatenate([ga.out, gb.out], axis=1),
            jnp.concatenate([ua.out, ub.out], axis=1),
            jnp.concatenate([da.out, db.out], axis=1),
        )

    return local


def solution(mesh):
    rows = P(("fsdp", "tp"), None)
    weight = P("fsdp", "tp")
    in_specs = (
        rows, P("fsdp"), P(), weight, weight, weight, P("fsdp", None), P(None, "tp"), P("tp"), P("tp"), P("tp"),
        P("tp"), weight, P(), weight, weight, weight, rows,
    )
    out_specs = (
        rows, rows, P(), weight, weight, weight, P("fsdp", None), P(None, "tp"), P("tp"), P("tp"), P("tp"), P("tp"),
        weight, P(), weight, weight, weight,
    )
    return jax.shard_map(
        make_local(mesh.shape["fsdp"]), mesh=mesh, in_specs=in_specs, out_specs=out_specs, check_vma=False
    )
```

```python
import functools

import jax
import jax.numpy as jnp
from jax import lax
from jax.experimental import pallas as pl
from jax.experimental.pallas import tpu as pltpu
from jax.sharding import PartitionSpec as P

HEADDIM = 64
HEADS = 24
STATES = 16
Q = 128
HALO = 16
EXTRA = 128
RUN, DT, DEC, TAIL, SEG, CONT, LAST, LOGDT = 0, 24, 48, 72, 96, 100, 101, 104
COLB, COLC = HEADS, HEADS + STATES

f32 = jnp.float32
bf16 = jnp.bfloat16
highest = lax.Precision.HIGHEST
epsilon = 1e-05
NEG = -1e30


def dot(a, b, precision=None):
    return jnp.dot(a, b, preferred_element_type=f32, precision=precision)


def dot_t(a, b):
    return lax.dot_general(a, b, (((1,), (1,)), ((), ())), preferred_element_type=f32)


def split(v):
    high = v.astype(bf16)
    return high, (v - high.astype(f32)).astype(bf16)


def wide_left(v):
    high, low = split(v)
    return jnp.concatenate([high, low, high], axis=1)


def stack_right(v):
    high, low = split(v)
    return jnp.concatenate([high, high, low], axis=0)


def sigmoid(v):
    return 0.5 * jnp.tanh(0.5 * v) + 0.5


def lanes_of(rows=Q):
    return lax.broadcasted_iota(jnp.int32, (rows, 128), 1)


def pair_cols(col, first, j, left):
    a = col[:, first + 2 * j : first + 2 * j + 1]
    b = col[:, first + 2 * j + 1 : first + 2 * j + 2]
    return jnp.where(left, a, b)


def triangle(strict=False, transposed=False):
    i = lax.broadcasted_iota(jnp.int32, (Q, Q), 1 if transposed else 0)
    k = lax.broadcasted_iota(jnp.int32, (Q, Q), 0 if transposed else 1)
    return (i > k) if strict else (i >= k)


def conv_rows(x_ref, xp_ref, halo_ref, cw_ref, col, q, lanes):
    x = x_ref[:, lanes]
    prev = jnp.where(q == 0, halo_ref[:, lanes], xp_ref[:, lanes])
    cat = jnp.concatenate([prev, x], axis=0)
    acc = cw_ref[4:5, lanes] + cw_ref[0:1, lanes] * x
    shifted = []
    for k in (1, 2, 3):
        back = pltpu.roll(cat, k, 0)[HALO:, :] * col[:, SEG + k : SEG + k + 1]
        shifted.append(back)
        acc = acc + cw_ref[k : k + 1, lanes] * back
    return x, shifted, acc


def conv_state_kernel(
    x_ref, xp_ref, halo_ref, cw_ref, e_ref, hp_ref, mark_ref, u_ref, end_ref, col_ref, row_ref, et_ref
):
    q = pl.program_id(0)

    @pl.when(q == 0)
    def _():
        end_ref[...] = jnp.zeros_like(end_ref)

    e, marks = e_ref[...], mark_ref[...]
    lane = lanes_of()
    head = lane < HEADS
    raw = e + hp_ref[0:1, :]
    dt = jnp.where(head, jnp.maximum(raw, 0.0) + jnp.log1p(jnp.exp(-jnp.abs(raw))), 0.0)
    run = dot(jnp.where(triangle(), 1.0, 0.0), dt * hp_ref[1:2, :], highest)
    dec = jnp.where(head, jnp.exp(run) * marks[:, CONT : CONT + 1], 0.0)
    tail = jnp.where(head, jnp.exp(run[Q - 1 : Q, :] - run) * marks[:, LAST : LAST + 1], 0.0)
    log_dt = jnp.where(head, jnp.log(dt), 0.0)
    col = (
        run
        + pltpu.roll(dt, DT, 1)
        + pltpu.roll(dec, DEC, 1)
        + pltpu.roll(tail, TAIL, 1)
        + marks
        + pltpu.roll(log_dt, LOGDT, 1)
    )
    col_ref[...] = col
    row_ref[...] = col.T
    et = e.T
    et_ref[...] = et
    bt = wide_left(et[COLB:COLC, :])
    left = lane < HEADDIM
    for j in range(x_ref.shape[1] // 128):
        lanes = slice(128 * j, 128 * j + 128)
        _, _, acc = conv_rows(x_ref, xp_ref, halo_ref, cw_ref, col, q, lanes)
        u = acc * sigmoid(acc)
        u_ref[:, lanes] = u
        scaled = u * (pair_cols(col, DT, j, left) * pair_cols(col, TAIL, j, left))
        keep = pair_cols(col[Q - 1 : Q, :], DEC, j, left[:1])
        end_ref[:, lanes] = keep * end_ref[:, lanes] + dot(bt, stack_right(scaled))


def scan_kernel(
    u_ref, z_ref, col_ref, row_ref, e_ref, et_ref, s0_ref, cw_ref, gated_ref, y_ref, st_ref, S
):
    @pl.when(pl.program_id(0) == 0)
    def _():
        S[...] = s0_ref[...]

    col, row = col_ref[...], row_ref[...]
    left = lanes_of() < HEADDIM
    c = e_ref[:, COLC : COLC + STATES]
    bt = et_ref[COLB:COLC, :]
    scores = dot(c, bt, highest)
    neg = jnp.where((col[:, SEG : SEG + 1] == row[SEG : SEG + 1, :]) & triangle(), 0.0, NEG)
    c, bt = wide_left(c), wide_left(bt)
    for j in range(u_ref.shape[1] // 128):
        lanes = slice(128 * j, 128 * j + 128)
        uf = u_ref[:, lanes]
        u, u_low = split(uf)
        state = S[:, lanes]
        st_ref[:, lanes] = state
        parts, rest = [], []
        for h in (2 * j, 2 * j + 1):
            gap = col[:, h : h + 1] - (row[h : h + 1, :] - row[LOGDT + h : LOGDT + h + 1, :])
            high, low = split(jnp.exp(gap + neg) * scores)
            parts.append(high)
            rest.append(low)
        zero = jnp.zeros_like(u)
        both = [jnp.where(left, u, zero), jnp.where(left, zero, u)]
        both_low = [jnp.where(left, u_low, zero), jnp.where(left, zero, u_low)]
        y = dot(jnp.concatenate(parts + rest + parts, axis=1), jnp.concatenate(both + both + both_low, axis=0))
        y = y + dot(c, stack_right(state)) * pair_cols(col, DEC, j, left) + cw_ref[5:6, lanes] * uf
        z = z_ref[:, lanes]
        y_ref[:, lanes] = y
        gated_ref[:, lanes] = (y * (z * sigmoid(z))).astype(bf16)
        scaled = uf * (pair_cols(col, DT, j, left) * pair_cols(col, TAIL, j, left))
        keep = pair_cols(col[Q - 1 : Q, :], DEC, j, left[:1])
        S[:, lanes] = keep * state + dot(bt, stack_right(scaled))


def gate_back_kernel(gg_ref, z_ref, y_ref, col_ref, et_ref, dy_ref, dz_ref, ds_ref):
    @pl.when(pl.program_id(0) == 0)
    def _():
        ds_ref[...] = jnp.zeros_like(ds_ref)

    col = col_ref[...]
    left = lanes_of() < HEADDIM
    ct = et_ref[COLC : COLC + STATES, :].astype(bf16)
    for j in range(z_ref.shape[1] // 128):
        lanes = slice(128 * j, 128 * j + 128)
        z = z_ref[:, lanes]
        gg = gg_ref[:, lanes]
        sig = sigmoid(z)
        dy = gg * (z * sig)
        dy_ref[:, lanes] = dy
        dz_ref[:, lanes] = (gg * y_ref[:, lanes] * (sig * (1.0 + z * (1.0 - sig)))).astype(bf16)
        scaled = (dy * pair_cols(col, DEC, j, left)).astype(bf16)
        keep = pair_cols(col[Q - 1 : Q, :], DEC, j, left[:1])
        ds_ref[:, lanes] = keep * ds_ref[:, lanes] + dot(ct, scaled)


def scan_back_kernel(
    u_ref, dy_ref, x_ref, xp_ref, halo_ref, cw_ref, col_ref, row_ref, e_ref, et_ref, st_ref, de_ref, hp_ref,
    lw_ref, sm_ref, pick_ref, head_ref,
    dx_ref, de_out_ref, cg_ref, edge_ref, hg_ref,
    D, WA, CONST, TAILS, DECS, DS, ST, SUMS, DG,
):
    step = pl.program_id(0)
    q = pl.num_programs(0) - 1 - step

    @pl.when(step == 0)
    def _():
        D[...] = de_ref[...]
        cg_ref[...] = jnp.zeros_like(cg_ref)
        edge_ref[...] = jnp.zeros_like(edge_ref)
        hg_ref[...] = jnp.zeros_like(hg_ref)
        WA[...] = jnp.zeros_like(WA)
        CONST[...] = jnp.zeros_like(CONST)
        DS[...] = jnp.zeros_like(DS)
        ST[...] = jnp.zeros_like(ST)

    col, row = col_ref[...], row_ref[...]
    lane = lanes_of()
    left = lane < HEADDIM
    e = e_ref[...]
    b, ct = e[:, COLB:COLC], et_ref[COLC : COLC + STATES, :]
    scores = dot(b, ct, highest)
    neg = jnp.where((col[:, SEG : SEG + 1] == row[SEG : SEG + 1, :]) & triangle(transposed=True), 0.0, NEG)
    b, ct, c = wide_left(b), ct.astype(bf16), wide_left(e[:, COLC : COLC + STATES])
    DG[...] = jnp.zeros_like(DG)
    SUMS[...] = jnp.zeros_like(SUMS)
    for j in range(u_ref.shape[1] // 128):
        lanes = slice(128 * j, 128 * j + 128)
        u = u_ref[:, lanes]
        dyf = dy_ref[:, lanes]
        dy = dyf.astype(bf16)
        dt = pair_cols(col, DT, j, left)
        dec = pair_cols(col, DEC, j, left)
        tail = pair_cols(col, TAIL, j, left)
        keep = pair_cols(col[Q - 1 : Q, :], DEC, j, left[:1])
        state, grad_state = st_ref[:, lanes], D[:, lanes]
        DS[COLB:COLC, lanes] = grad_state
        ST[COLC : COLC + STATES, lanes] = state
        xs = u * dt
        zero = jnp.zeros_like(dy)
        both = jnp.concatenate([jnp.where(left, dy, zero), jnp.where(left, zero, dy)], axis=0)
        d_mat = dot_t(xs.astype(bf16), both)
        mats, pairs, d_scores = [], [], None
        for i, h in enumerate((2 * j, 2 * j + 1)):
            decay = jnp.exp((row[h : h + 1, :] - col[:, h : h + 1]) + neg)
            mat = decay * scores
            dm = d_mat[:, Q * i : Q * i + Q]
            d_scores = decay * dm if d_scores is None else d_scores + decay * dm
            mats.append(mat.astype(bf16))
            pairs.append((mat * dm).astype(bf16))
        DG[...] += d_scores
        dxs = dot(jnp.concatenate(mats, axis=1), both)
        spans = dot(jnp.concatenate(pairs, axis=1), lw_ref[...]) * sm_ref[...]
        sums = jnp.sum(spans, axis=0, keepdims=True)
        WA[2 * j : 2 * j + 1, :] = sums[:, :Q]
        WA[2 * j + 1 : 2 * j + 2, :] = sums[:, Q:]
        from_tail = tail * dot(b, stack_right(grad_state))
        dxs = dxs + from_tail
        ydec = dyf * dec
        found = [u * dxs, ydec * dot(c, stack_right(state)), xs * from_tail]
        SUMS[...] += dot(jnp.concatenate([v.astype(bf16) for v in found], axis=1), pick_ref[j])
        TAILS[:, lanes] = (xs * tail).astype(bf16)
        low_dec = ydec.astype(bf16)
        DECS[:, lanes] = low_dec
        CONST[0:1, lanes] = keep * jnp.sum(state * grad_state, axis=0, keepdims=True)
        D[:, lanes] = keep * grad_state + dot(ct, low_dec)

        x, shifted, acc = conv_rows(x_ref, xp_ref, halo_ref, cw_ref, col, q, lanes)
        sig = sigmoid(acc)
        dconv = (dxs * dt + cw_ref[5:6, lanes] * dyf) * (sig * (1.0 + acc * (1.0 - sig)))
        dx = cw_ref[0:1, lanes] * dconv
        cg_ref[0:1, lanes] += jnp.sum(dconv * x, axis=0, keepdims=True)
        for k in (1, 2, 3):
            masked = dconv * col[:, SEG + k : SEG + k + 1]
            after = edge_ref[8 * (k - 1) : 8 * k, lanes]
            cat = jnp.concatenate([masked, after], axis=0)
            dx = dx + cw_ref[k : k + 1, lanes] * pltpu.roll(cat, Q + 8 - k, 0)[:Q, :]
            edge_ref[8 * (k - 1) : 8 * k, lanes] = masked[:8, :]
            cg_ref[k : k + 1, lanes] += jnp.sum(dconv * shifted[k - 1], axis=0, keepdims=True)
        cg_ref[4:5, lanes] += jnp.sum(dconv, axis=0, keepdims=True)
        cg_ref[5:6, lanes] += jnp.sum(dyf * u, axis=0, keepdims=True)
        dx_ref[:, lanes] = dx.astype(bf16)

    head = lane < HEADS
    found = SUMS[...]
    suffix = jnp.where(triangle(transposed=True), 1.0, 0.0)
    prefix = jnp.where(triangle(strict=True), 1.0, 0.0)
    d_step = (
        WA[...].T
        + dot(suffix, pltpu.roll(found, 128 - HEADS, 1), highest)
        + dot(prefix, pltpu.roll(found, 128 - 2 * HEADS, 1), highest)
        + dot(CONST[...], head_ref[...], highest)[0:1, :]
    )
    d_dt = d_step * hp_ref[1:2, :] + found
    d_raw = jnp.where(head, d_dt * sigmoid(e + hp_ref[0:1, :]), 0.0)
    step_dt = jnp.where(head, pltpu.roll(col, 128 - DT, 1), 0.0)
    hg_ref[0:1, :] += jnp.sum(d_raw, axis=0, keepdims=True)
    hg_ref[1:2, :] += jnp.sum(jnp.where(head, d_step, 0.0) * step_dt, axis=0, keepdims=True) * hp_ref[1:2, :]
    total = DG[...]
    b_part = jnp.where((lane >= COLB) & (lane < COLC), e, 0.0)
    c_part = jnp.where((lane >= COLC) & (lane < COLC + STATES), e, 0.0)
    de_out_ref[...] = (
        d_raw
        + dot_t(TAILS[...], DS[...].astype(bf16))
        + dot_t(DECS[...], ST[...].astype(bf16))
        + dot(total, pltpu.roll(c_part, 128 - STATES, 1), highest)
        + dot(total.T, pltpu.roll(b_part, STATES, 1), highest)
    )


def norm_kernel(*refs):
    *row_refs, gain_ref, hidden_ref, out_ref, turned_ref = refs
    rows = row_refs[0][...]
    for r in row_refs[1:]:
        rows = rows + r[...]
    hidden_ref[...] = rows
    scale = lax.rsqrt(jnp.mean(rows * rows, axis=-1, keepdims=True) + epsilon)
    normed = rows * scale * gain_ref[...]
    out_ref[...] = normed.astype(bf16)
    turned_ref[...] = normed.T.astype(bf16)


def norm_back_kernel(n_grads, rows_ref, gain_ref, *refs):
    *given, high_ref, low_ref, part_ref, turned_ref = refs

    @pl.when(pl.program_id(0) == 0)
    def _():
        part_ref[...] = jnp.zeros_like(part_ref)

    rows, grad = rows_ref[...], given[0][...]
    for r in given[1:n_grads]:
        grad = grad + r[...]
    scale = lax.rsqrt(jnp.mean(rows * rows, axis=-1, keepdims=True) + epsilon)
    unit = rows * scale
    part_ref[0:1, :] += jnp.sum(grad * unit, axis=0, keepdims=True)
    unit_grad = grad * gain_ref[...]
    total = scale * (unit_grad - unit * jnp.mean(unit_grad * unit, axis=-1, keepdims=True))
    for r in given[n_grads:]:
        total = total + r[...].astype(f32)
    high = total.astype(bf16)
    high_ref[...] = high
    low_ref[...] = (total - high.astype(f32)).astype(bf16)
    turned_ref[...] = total.T.astype(bf16)


def flip(i, mask):
    bit = 1
    while bit <= mask:
        if mask & bit:
            i = i + bit * (1 - 2 * ((i // bit) % 2))
        bit *= 2
    return i


class Load:
    def __init__(self, *movers):
        self.reads, self.updates, self.news, self.copies = {}, {}, {}, []
        self.movers = movers
        for mover in movers:
            reads, updates, news, copies = mover.moves()
            self.reads.update(reads)
            self.updates.update(updates)
            self.news.update(news)
            self.copies += copies

    def arrive(self, got):
        for mover in self.movers:
            mover.take(got)


IDS = {}


def run(body, grid, in_specs, out_specs, out_shape, scratch, args, name, estimate=None, load=None, vmem=56):
    params = dict(dimension_semantics=("arbitrary",) * len(grid), vmem_limit_bytes=vmem * 1024 * 1024)
    if load is None:
        return pl.pallas_call(
            body, name=name, grid=grid, in_specs=in_specs, out_specs=out_specs, out_shape=out_shape,
            scratch_shapes=scratch, compiler_params=pltpu.CompilerParams(**params), cost_estimate=estimate,
        )(*args)
    cid = IDS.setdefault(name, len(IDS) + 1)
    reads, updates, news = list(load.reads), list(load.updates), list(load.news)
    n_in, n_out, n_scratch, n_copies = len(args), len(out_shape), len(scratch), len(load.copies)
    routes = []
    for c in load.copies:
        if c[4] is not None and c[4] not in routes:
            routes.append(c[4])

    def kernel(*refs):
        ins, rest = refs[:n_in], refs[n_in:]
        held = dict(zip(reads, rest))
        rest = rest[len(reads) + len(updates) :]
        outs, rest = rest[:n_out], rest[n_out:]
        held.update(zip(updates + news, rest))
        rest = rest[len(updates) + len(news) :]
        mine, (send, recv) = rest[:n_scratch], rest[n_scratch:]

        def device(route):
            return {route[0]: flip(lax.axis_index(route[0]), route[1])}

        def make(i, c):
            src, dst = held[c[0]].at[c[1]], held[c[2]].at[c[3]]
            if c[4] is None:
                return pltpu.make_async_copy(src, dst, recv.at[i])
            return pltpu.make_async_remote_copy(
                src_ref=src, dst_ref=dst, send_sem=send.at[i], recv_sem=recv.at[i],
                device_id=device(c[4]), device_id_type=pl.DeviceIdType.MESH,
            )

        first, last = pl.program_id(0) == 0, pl.program_id(0) == grid[0] - 1
        for axis in range(1, len(grid)):
            first = first & (pl.program_id(axis) == 0)
            last = last & (pl.program_id(axis) == grid[axis] - 1)

        @pl.when(first)
        def _():
            barrier = pltpu.get_barrier_semaphore()
            for route in routes:
                pl.semaphore_signal(
                    barrier, inc=1, device_id=device(route), device_id_type=pl.DeviceIdType.MESH
                )
            pl.semaphore_wait(barrier, len(routes))
            for i, c in enumerate(load.copies):
                make(i, c).start()

        if body is not None:
            body(*ins, *outs, *mine)

        @pl.when(last)
        def _():
            for i, c in enumerate(load.copies):
                make(i, c).wait()

    hbm = pl.BlockSpec(memory_space=pltpu.HBM)
    result = pl.pallas_call(
        kernel,
        name=name,
        grid=grid,
        in_specs=list(in_specs) + [hbm] * (len(reads) + len(updates)),
        out_specs=list(out_specs) + [hbm] * (len(updates) + len(news)),
        out_shape=list(out_shape)
        + [jax.ShapeDtypeStruct(load.updates[k].shape, load.updates[k].dtype) for k in updates]
        + [load.news[k] for k in news],
        scratch_shapes=list(scratch) + [pltpu.SemaphoreType.DMA((n_copies,)), pltpu.SemaphoreType.DMA((n_copies,))],
        input_output_aliases={n_in + len(reads) + i: n_out + i for i in range(len(updates))},
        compiler_params=pltpu.CompilerParams(collective_id=cid, has_side_effects=True, **params),
        cost_estimate=estimate,
    )(*args, *[load.reads[k] for k in reads], *[load.updates[k] for k in updates])
    load.arrive(dict(zip(updates + news, result[n_out:])))
    return result[:n_out]


def matmul(jobs, dtype, tile, name, load=None, nt=False, turned=False):
    n_jobs, n_pairs = len(jobs), len(jobs[0])
    rows = jobs[0][0][0].shape[0]
    columns = jobs[0][0][1].shape[0 if nt else 1]
    tiles = columns // tile

    def at(job):
        def place(j, t):
            return jnp.where(j == job, t, jnp.where(j < job, 0, tiles - 1))

        return place

    args, in_specs = [], []
    for job, pairs in enumerate(jobs):
        for left, right in pairs:
            args += [left, right]
            k = left.shape[1]
            in_specs.append(pl.BlockSpec((rows, k), lambda j, t: (0, 0), pipeline_mode=pl.Buffered(1)))
            if nt:
                in_specs.append(pl.BlockSpec((tile, k), lambda j, t, p=at(job): (p(j, t), 0)))
            else:
                in_specs.append(pl.BlockSpec((k, tile), lambda j, t, p=at(job): (0, p(j, t))))
    out_specs = [pl.BlockSpec((rows, tile), lambda j, t, p=at(job): (0, p(j, t))) for job in range(n_jobs)]
    out_shape = [jax.ShapeDtypeStruct((rows, columns), dtype)] * n_jobs
    if turned:
        out_specs += [pl.BlockSpec((tile, rows), lambda j, t, p=at(job): (p(j, t), 0)) for job in range(n_jobs)]
        out_shape += [jax.ShapeDtypeStruct((columns, rows), dtype)] * n_jobs

    def body(*refs):
        ins, outs = refs[: 2 * n_jobs * n_pairs], refs[2 * n_jobs * n_pairs :]
        for job in range(n_jobs):

            @pl.when(pl.program_id(0) == job)
            def _(job=job):
                total = None
                for p in range(n_pairs):
                    left, right = ins[2 * (job * n_pairs + p)], ins[2 * (job * n_pairs + p) + 1]
                    term = (dot_t if nt else dot)(left[...], right[...])
                    total = term if total is None else total + term
                outs[job][...] = total.astype(dtype)
                if turned:
                    outs[n_jobs + job][...] = total.T.astype(dtype)

    depth = sum(p[0].shape[1] for p in jobs[0])
    return run(
        body, (n_jobs, tiles), in_specs, out_specs, out_shape, [], args, name,
        pl.CostEstimate(
            flops=2 * n_jobs * rows * columns * depth, bytes_accessed=4 * n_jobs * rows * columns, transcendentals=0
        ),
        load,
    )


def feed_forward(normed, cot, gate_w, up_w, down_w):
    tokens, width = normed.shape
    cols, tile, step = gate_w[0].shape[1], 512, 256
    tiles = cols // tile

    def at(job):
        def place(j, t):
            return jnp.where(j == job, t, jnp.where(j < job, 0, tiles - 1))

        return place

    whole = pl.BlockSpec((tokens, width), lambda j, t: (0, 0), pipeline_mode=pl.Buffered(1))
    args, in_specs, out_specs = [normed, cot], [whole, whole], []
    for b in (0, 1):
        args += [gate_w[b], up_w[b], down_w[b]]
        in_specs += [pl.BlockSpec((width, tile), lambda j, t, p=at(b): (0, p(j, t)))] * 3
        out_specs += [pl.BlockSpec((tokens, tile), lambda j, t, p=at(b): (0, p(j, t)))] * 3

    def body(n_ref, c_ref, *refs):
        for b in (0, 1):
            wg, wu, wd = refs[3 * b : 3 * b + 3]
            act, gg, ug = refs[6 + 3 * b : 9 + 3 * b]

            @pl.when(pl.program_id(0) == b)
            def _(wg=wg, wu=wu, wd=wd, act=act, gg=gg, ug=ug):
                for i in range(tokens // step):
                    rows = slice(step * i, step * i + step)
                    gate, up, back = dot(n_ref[rows, :], wg[...]), dot(n_ref[rows, :], wu[...]), dot(c_ref[rows, :], wd[...])
                    sig = sigmoid(gate)
                    silu = gate * sig
                    act[rows, :] = (silu * up).astype(bf16)
                    gg[rows, :] = (back * up * sig * (1.0 + gate * (1.0 - sig))).astype(bf16)
                    ug[rows, :] = (back * silu).astype(bf16)

    out = run(
        body, (2, tiles), in_specs, out_specs, [jax.ShapeDtypeStruct((tokens, cols), bf16)] * 6, [], args,
        "feed_forward", pl.CostEstimate(flops=12 * tokens * cols * width, bytes_accessed=12 * tokens * cols, transcendentals=0),
    )
    return [out[0], out[3]], [out[1], out[4]], [out[2], out[5]]


def carry_only(load, name):
    run(None, (1,), [], [], [], [], [], name, None, load)


ALL = (slice(None),)


def low_sum(a, b):
    return (a.astype(f32) + b.astype(f32)).astype(bf16)


class Gather:
    def __init__(self, key, shard, n):
        rows, cols = shard.shape
        self.n, self.key, self.phase = n, key, 0
        self.shard = shard.reshape(2, rows // 2, cols)
        self.cols = cols

    def moves(self):
        k, n = self.key, self.n
        q = n // 4
        s, a, b = k + "s", k + "0", k + "1"
        if self.phase == 0:
            whole = jax.ShapeDtypeStruct((2, n) + self.shard.shape[1:], bf16)
            copies = [
                (s, (i,), a, (i, m), ("fsdp", m << 2) if m else None) for m in range(q) for i in (0, 1)
            ]
            return {s: self.shard}, {}, {a: whole, b: whole}, copies
        near, far, both = slice(0, q), slice(q, 2 * q), slice(0, 2 * q)
        if self.phase == 1:
            copies = [(a, (0, near), b, (0, near), ("tp", 1)), (a, (1, near), a, (1, far), ("fsdp", 2))]
        elif self.phase == 2:
            copies = [
                (a, (0, near), a, (0, far), ("fsdp", 2)),
                (b, (0, near), b, (0, far), ("fsdp", 2)),
                (a, (1, both), b, (1, both), ("tp", 1)),
            ]
        else:
            copies = [(h, (i, both), h, (i, slice(2 * q, 4 * q)), ("fsdp", 1)) for h in (a, b) for i in (0, 1)]
        return {}, {a: self.halves[0], b: self.halves[1]}, {}, copies

    def take(self, got):
        self.halves = [got[self.key + "0"], got[self.key + "1"]]
        self.phase += 1
        if self.phase == 4:
            self.full = [h.reshape(-1, self.cols) for h in self.halves]


class Scatter:
    def __init__(self, key, grads, n, piece=0, pieces=1):
        self.n, self.key, self.phase = n, f"{key}{piece}_", 0
        cols = grads[0].shape[1]
        self.cols = cols // pieces
        self.rows = grads[0].shape[0] // n
        self.now = [g.reshape(2, n, self.rows // 2, cols) for g in grads]
        self.range = slice(piece * self.cols, (piece + 1) * self.cols)

    def moves(self):
        n, v = self.n, self.now
        q = n // 4
        part = (self.rows // 2, self.cols)
        far, rest = slice(q, 2 * q), slice(2 * q, 4 * q)

        def name(i):
            return f"{self.key}{i}"

        def new(*dims):
            return jax.ShapeDtypeStruct(dims + part, bf16)

        if self.phase == 0:
            news = [new(2, 2 * q), new(2, 2 * q)]
            copies = [
                (b, (i, rest, slice(None), self.range), b, (i,), ("fsdp", 1)) for b in (0, 1) for i in (0, 1)
            ]
        elif self.phase == 1:
            news = [new(q), new(q), new(2 * q)]
            copies = [
                (0, (0, far), 0, ALL, ("fsdp", 2)),
                (1, (0, far), 1, ALL, ("fsdp", 2)),
                (1, (1,), 2, ALL, ("tp", 1)),
            ]
        elif self.phase == 2:
            news = [new(q), new(q)]
            copies = [(1, ALL, 0, ALL, ("tp", 1)), (2, (far,), 1, ALL, ("fsdp", 2))]
        else:
            news = [new(2) for _ in range(1, q)]
            copies = [(i, (m,), m - 1, (i,), ("fsdp", m << 2)) for m in range(1, q) for i in (0, 1)]
        reads = {name(f"v{i}"): a for i, a in enumerate(v) if any(c[0] == i for c in copies)}
        self.names = [name(f"r{i}") for i in range(len(news))]
        copies = [(name(f"v{c[0]}"), c[1], self.names[c[2]], c[3], c[4]) for c in copies]
        return reads, {}, dict(zip(self.names, news)), copies

    def take(self, got):
        r, v = [got[k] for k in self.names], self.now
        q = self.n // 4
        if self.phase == 0:
            self.now = [low_sum(p[:, : 2 * q, :, self.range], a) for p, a in zip(v, r)]
        elif self.phase == 1:
            self.now = [low_sum(v[0][0, :q], r[0]), low_sum(v[1][0, :q], r[1]), low_sum(v[0][1], r[2])]
        elif self.phase == 2:
            self.now = [low_sum(v[0], r[0]), low_sum(v[2][:q], r[1])]
        else:
            total = jnp.stack([v[0][0], v[1][0]]).astype(f32)
            for p in r:
                total = total + p.astype(f32)
            self.out = total.reshape(self.rows, self.cols)
        self.phase += 1


def specs(blocks, ch, reverse):
    def at(q):
        return blocks - 1 - q if reverse else q

    def whole(rows, cols):
        return pl.BlockSpec((rows, cols), lambda q: (0, 0))

    return dict(
        main=pl.BlockSpec((Q, ch), lambda q: (at(q), 0)),
        prev=pl.BlockSpec((HALO, ch), lambda q: (jnp.maximum(at(q) * (Q // HALO) - 1, 0), 0)),
        tile=pl.BlockSpec((Q, 128), lambda q: (at(q), 0)),
        state=pl.BlockSpec((STATES, ch), lambda q: (at(q), 0)),
        halo=whole(HALO, ch), row8=whole(8, ch), row24=whole(24, ch), row16=whole(STATES, ch), small=whole(8, 128),
    )


def shape(dims, dtype):
    return jax.ShapeDtypeStruct(dims, dtype)


def cost(flops, moved):
    return pl.CostEstimate(flops=int(flops), bytes_accessed=int(moved), transcendentals=0)


def conv_state(x, halo, cw, e, hp, marks, tag="", load=None):
    tokens, ch = x.shape
    s = specs(tokens // Q, ch, False)
    return run(
        conv_state_kernel,
        (tokens // Q,),
        [s["main"], s["prev"], s["halo"], s["row8"], s["tile"], s["small"], s["tile"]],
        [s["main"], s["row16"], s["tile"], s["tile"], s["tile"]],
        [shape((tokens, ch), f32), shape((STATES, ch), f32)] + [shape((tokens, 128), f32)] * 3,
        [],
        [x, x, halo, cw, e, hp, marks],
        "conv_state" + tag,
        cost(tokens * ch * 5000, 4 * tokens * ch),
        load,
    )


def scan_forward(u, z, col, row, e, et, s0, cw, tag="", load=None):
    tokens, ch = u.shape
    s = specs(tokens // Q, ch, False)
    return run(
        scan_kernel,
        (tokens // Q,),
        [s["main"], s["main"], s["tile"], s["tile"], s["tile"], s["tile"], s["row16"], s["row8"]],
        [s["main"], s["main"], s["state"]],
        [shape((tokens, ch), bf16), shape((tokens, ch), f32), shape((tokens // Q * STATES, ch), f32)],
        [pltpu.VMEM((STATES, ch), f32)],
        [u, z, col, row, e, et, s0, cw],
        "scan_forward" + tag,
        cost(tokens * ch * 10000, 8 * tokens * ch),
        load,
    )


def gate_backward(gg, z, y, col, et, tag="", load=None):
    tokens, ch = z.shape
    s = specs(tokens // Q, ch, True)
    return run(
        gate_back_kernel,
        (tokens // Q,),
        [s["main"], s["main"], s["main"], s["tile"], s["tile"]],
        [s["main"], s["main"], s["row16"]],
        [shape((tokens, ch), f32), shape((tokens, ch), bf16), shape((STATES, ch), f32)],
        [],
        [gg, z, y, col, et],
        "gate_backward" + tag,
        cost(tokens * ch * 5000, 10 * tokens * ch),
        load,
    )


def scan_backward(u, dy, x, halo, cw, col, row, e, et, st, de, hp, tag="", load=None):
    tokens, ch = u.shape
    s = specs(tokens // Q, ch, True)
    place = jnp.arange(2 * Q)
    lower = ((place[:, None] >= place[None, :]) & (place[:, None] // Q == place[None, :] // Q)).astype(bf16)
    strict = (jnp.arange(Q)[:, None] < (place % Q)[None, :]).astype(f32)
    pairs = ch // 128
    lane = jnp.arange(3 * 128)
    target = (lane // 128) * HEADS + 2 * jnp.arange(pairs)[:, None] + ((lane % 128) // HEADDIM)[None, :]
    pick = (target[:, :, None] == jnp.arange(128)[None, None, :]).astype(bf16)
    by_head = (jnp.arange(ch)[:, None] // HEADDIM == jnp.arange(128)[None, :]).astype(f32)
    return run(
        scan_back_kernel,
        (tokens // Q,),
        [
            s["main"], s["main"], s["main"], s["prev"], s["halo"], s["row8"], s["tile"], s["tile"], s["tile"],
            s["tile"], s["state"], s["row16"], s["small"],
            pl.BlockSpec((2 * Q, 2 * Q), lambda q: (0, 0)), pl.BlockSpec((Q, 2 * Q), lambda q: (0, 0)),
            pl.BlockSpec((pairs, 3 * 128, 128), lambda q: (0, 0, 0)), pl.BlockSpec((ch, 128), lambda q: (0, 0)),
        ],
        [s["main"], s["tile"], s["row8"], s["row24"], s["small"]],
        [
            shape((tokens, ch), bf16), shape((tokens, 128), f32), shape((8, ch), f32), shape((24, ch), f32),
            shape((8, 128), f32),
        ],
        [
            pltpu.VMEM((STATES, ch), f32), pltpu.VMEM((128, Q), f32), pltpu.VMEM((8, ch), f32),
            pltpu.VMEM((Q, ch), bf16), pltpu.VMEM((Q, ch), bf16), pltpu.VMEM((128, ch), f32),
            pltpu.VMEM((128, ch), f32), pltpu.VMEM((Q, 128), f32), pltpu.VMEM((Q, Q), f32),
        ],
        [u, dy, x, x, halo, cw, col, row, e, et, st, de, hp, lower, strict, pick, by_head],
        "scan_backward" + tag,
        cost(tokens * ch * 25000, 12 * tokens * ch),
        load,
    )


def norm_specs(width):
    main = pl.BlockSpec((Q, width), lambda q: (q, 0))
    return main, pl.BlockSpec((width, Q), lambda q: (0, q)), pl.BlockSpec((1, width), lambda q: (0, 0))


def norm_forward(rows, gain_row, name, load=None):
    tokens, width = rows[0].shape
    main, turned, one = norm_specs(width)
    return run(
        norm_kernel,
        (tokens // Q,),
        [main] * len(rows) + [one],
        [main, main, turned],
        [shape((tokens, width), f32), shape((tokens, width), bf16), shape((width, tokens), bf16)],
        [],
        [*rows, gain_row],
        name,
        cost(tokens * width * 20, 12 * tokens * width),
        load,
    )


def norm_back(grads, rows, gain_row, bases, name, load=None):
    tokens, width = rows.shape
    main, turned, one = norm_specs(width)
    high, low, part, high_t = run(
        functools.partial(norm_back_kernel, len(grads)),
        (tokens // Q,),
        [main, one] + [main] * (len(grads) + len(bases)),
        [main, main, pl.BlockSpec((8, width), lambda q: (0, 0)), turned],
        [
            shape((tokens, width), bf16), shape((tokens, width), bf16), shape((8, width), f32),
            shape((width, tokens), bf16),
        ],
        [],
        [rows, gain_row, *grads, *bases],
        name,
        cost(tokens * width * 20, 16 * tokens * width),
        load,
    )
    return high, low, high_t, part[0]


def token_marks(seg, seg_before):
    tokens = seg.shape[0]
    by_block = seg.reshape(tokens // Q, Q)
    before = jnp.concatenate([seg_before[2:3], by_block[:-1, Q - 1]])
    padded = jnp.concatenate([seg_before, seg])
    found = [seg.astype(f32)] + [(padded[3 - k : 3 - k + tokens] == seg).astype(f32) for k in (1, 2, 3)]
    found.append((by_block == before[:, None]).astype(f32).reshape(-1))
    found.append((by_block == by_block[:, Q - 1 :]).astype(f32).reshape(-1))
    lane = jnp.arange(128)[None, :]
    out = jnp.zeros((tokens, 128), f32)
    for i, v in enumerate(found):
        out = jnp.where(lane == SEG + i, v[:, None], out)
    return out


def swap(x, axis, n, mask):
    return lax.ppermute(x, axis, [(i, i ^ mask) for i in range(n)])


def sum_all(x, n, over_tp=False):
    if over_tp:
        x = x + swap(x, "tp", 2, 1)
    bit = 1
    while bit < n:
        x = x + swap(x, "fsdp", n, bit)
        bit *= 2
    return x


def bf_dot(a, b):
    return jnp.dot(a, b, preferred_element_type=f32)


def make_local(n):
    def local(
        layer_in, seg_ids, gain_one, x_weight, z_weight, dt_weight, bc_weight, conv_weight, conv_bias,
        dt_bias, a_log, d_skip, out_weight, gain_two, gate_weight, up_weight, down_weight, cotangent,
    ):
        tokens, width = layer_in.shape
        rows, ch = x_weight.shape
        heads = dt_weight.shape[1]
        states = bc_weight.shape[1] // 2
        me, half = lax.axis_index("fsdp"), lax.axis_index("tp")

        epack = jnp.concatenate([dt_weight, bc_weight, jnp.zeros((rows, EXTRA - heads - 2 * states), bf16)], axis=1)
        X, E = Gather("x", x_weight, n), Gather("e", epack, n)
        Z, O = Gather("z", z_weight, n), Gather("o", out_weight, n)
        G, U, D = Gather("g", gate_weight, n), Gather("u", up_weight, n), Gather("d", down_weight, n)

        rate = -jnp.exp(a_log)
        pad = jnp.zeros((128 - heads,), f32)
        by_head = jnp.stack([jnp.concatenate([dt_bias, pad]), jnp.concatenate([rate, pad])])
        small = jnp.concatenate(
            [
                conv_weight,
                conv_bias[None, :],
                jnp.repeat(d_skip, HEADDIM)[None, :],
                jnp.pad(by_head, ((0, 0), (0, ch - 128))),
            ],
            axis=0,
        )
        smalls = [small, swap(small, "tp", 2, 1)]
        head_rows = [jnp.pad(v[6:8, :128], ((0, 6), (0, 0))) for v in smalls]
        before_rows = lax.ppermute(layer_in[tokens - HALO :], "tp", [(0, 1)])
        seg = lax.dynamic_slice(seg_ids, (half * tokens,), (tokens,))
        seg_before = jnp.where(half == 0, -1, seg_ids[tokens - 3 : tokens])

        part = rows // 2
        place = jnp.arange(2 * n)
        q = n // 4
        p = place % n
        part_at = (me ^ (p // (2 * q) + 2 * ((p // q) % 2) + 4 * (p % q))) * 2 + place // n
        seek = (place // 2) ^ me
        place_of = (place % 2) * n + (seek % 2) * 2 * q + ((seek // 2) % 2) * q + seek // 4
        col_at = (part_at[:, None] * part + jnp.arange(part)[None, :]).reshape(-1)
        turn = (jnp.arange(width)[:, None] == col_at[None, :]).astype(bf16)

        def to_local(v):
            return jnp.take(v.reshape(2 * n, part), part_at, axis=0).reshape(-1)

        def to_global(v):
            return jnp.take(v.reshape(2 * n, part), place_of, axis=0).reshape(-1)

        gain_one, gain_two = to_local(gain_one)[None, :], to_local(gain_two)[None, :]
        (rows_in,) = matmul([[(layer_in, turn)]], f32, 512, "turn_rows", Load(X, E))
        rows_in, normed, normed_t = norm_forward([rows_in], gain_one, "norm_one", Load(X, E, Z))
        cot_low, cot_t = matmul([[(cotangent, turn)]], bf16, 512, "turn_cotangent", Load(X, E, O), turned=True)
        carry_only(Load(X, E, Z), "carry_one")
        halo_rows = bf_dot(before_rows, turn)
        halo_scale = lax.rsqrt(jnp.mean(halo_rows * halo_rows, axis=-1, keepdims=True) + epsilon)
        normed_before = (halo_rows * halo_scale * gain_one).astype(bf16)
        marks = token_marks(seg, seg_before)

        xs = matmul([[(normed, w)] for w in X.full], f32, 512, "project_x", Load(Z, O, G))
        saved = []
        for b in (0, 1):
            v = dict(x=xs[b], cw=smalls[b], hp=head_rows[b])
            v["e"] = bf_dot(normed, E.full[b])
            v["halo"] = bf_dot(normed_before, X.full[b])
            load = Load(Z, O, G, U) if b == 0 else Load(G, O, D)
            v["u"], v["end"], v["col"], v["row"], v["et"] = conv_state(
                v["x"], v["halo"], v["cw"], v["e"], v["hp"], marks, tag=str(b), load=load
            )
            saved.append(v)
        starts = lax.ppermute(jnp.stack([v["end"] for v in saved]), "tp", [(0, 1)])[::-1]
        zs = matmul([[(normed, w)] for w in Z.full], f32, 512, "project_z", Load(G, U, D))
        for b in (0, 1):
            v = saved[b]
            v["z"] = zs[b]
            v["gated"], v["y"], v["states"] = scan_forward(
                v["u"], v["z"], v["col"], v["row"], v["e"], v["et"], starts[b], v["cw"],
                tag=str(b), load=Load(U) if b == 0 else Load(U, D),
            )
        (mixed,) = matmul(
            [[(v["gated"], w) for v, w in zip(saved, O.full)]], f32, 512, "project_out", Load(D), nt=True
        )
        hidden, normed_two, two_t = norm_forward([rows_in, mixed], gain_two, "norm_two")

        acts, gate_grads, up_grads = feed_forward(normed_two, cot_low, G.full, U.full, D.full)
        def halves(key, grads):
            return [Scatter(key, grads, n, i, 2) for i in (0, 1)]

        da, db = halves("d", matmul([[(cot_t, a)] for a in acts], bf16, 512, "down_grad"))
        ga, gb = halves("g", matmul([[(two_t, a)] for a in gate_grads], bf16, 512, "gate_grad", Load(da, db)))
        ua, ub = halves("u", matmul([[(two_t, a)] for a in up_grads], bf16, 512, "up_grad", Load(da, ga, gb)))
        (fed,) = matmul([list(zip(acts, D.full))], f32, 512, "project_down", Load(db, da, ua, ub), nt=True)
        out_low = (hidden + fed).astype(bf16)
        (grad_two,) = matmul(
            [list(zip(gate_grads, G.full)) + list(zip(up_grads, U.full))], f32, 256, "two_back",
            Load(ga, gb, db, da), nt=True,
        )
        mixed_grad, mixed_low, mixed_t, gain_two_part = norm_back(
            [grad_two], hidden, gain_two, [cot_low], "norm_two_back", Load(ga, db)
        )

        so = Scatter("o", matmul([[(mixed_t, v["gated"])] for v in saved], bf16, 512, "out_grad", Load(ua, ga)), n)
        gg = matmul([[(mixed_grad, w)] for w in O.full], f32, 512, "gated_back", Load(gb, so))
        for b in (0, 1):
            v = saved[b]
            v["dy"], v["dz"], v["ds"] = gate_backward(
                gg[b], v["z"], v["y"], v["col"], v["et"], tag=str(b), load=Load(ua, gb) if b == 0 else None
            )
        ends = lax.ppermute(jnp.stack([v["ds"] for v in saved]), "tp", [(1, 0)])[::-1]
        sz = Scatter("z", matmul([[(normed_t, v["dz"])] for v in saved], bf16, 512, "z_grad", Load(ua)), n)
        (grad_z,) = matmul([[(v["dz"], w) for v, w in zip(saved, Z.full)]], f32, 512, "z_back", Load(sz), nt=True)
        for b in (0, 1):
            v = saved[b]
            v["dx"], v["de"], v["cg"], v["edge"], v["hg"] = scan_backward(
                v["u"], v["dy"], v["x"], v["halo"], v["cw"], v["col"], v["row"], v["e"], v["et"], v["states"],
                ends[b], v["hp"], tag=str(b), load=Load(ub, so, sz) if b else Load(ub, so),
            )
        edges = lax.ppermute(jnp.stack([v["edge"] for v in saved]), "tp", [(1, 0)])[::-1]
        own, other = ([v["cg"][:6].reshape(-1), v["hg"][:2].reshape(-1)] for v in saved)
        gain_two_part = to_global(gain_two_part)
        own, other = jnp.concatenate(own + [gain_two_part]), jnp.concatenate(other + [gain_two_part])
        total = sum_all(own + swap(other, "tp", 2, 1), n)
        cg, hg = total[: 6 * ch].reshape(6, ch), total[6 * ch : 6 * ch + 256].reshape(2, 128)
        gain_two_total = total[6 * ch + 256 :]

        shared = 0.5 * (saved[0]["de"] + saved[1]["de"])
        own_lane = jnp.arange(EXTRA)[None, :] < heads
        for b in (0, 1):
            v = saved[b]
            cw, edge = v["cw"], edges[b].reshape(3, 8, ch)
            fix = [jnp.zeros((HALO - 3, ch), f32)]
            for j in (3, 2, 1):
                fix.append(sum(cw[k : k + 1] * edge[k - 1, k - j : k - j + 1] for k in range(j, 4)))
            last = v["dx"][tokens - HALO :].astype(f32) + jnp.concatenate(fix, axis=0)
            v["dx"] = lax.dynamic_update_slice(v["dx"], last.astype(bf16), (tokens - HALO, 0))
            v["de"] = jnp.where(own_lane, v["de"], shared).astype(bf16)
        sx = Scatter("x", matmul([[(normed_t, v["dx"])] for v in saved], bf16, 512, "x_grad", Load(sz, ub)), n)
        se = Scatter("e", matmul([[(normed_t, v["de"])] for v in saved], bf16, 128, "e_grad"), n)
        pairs = [(v["dx"], w) for v, w in zip(saved, X.full)] + [(v["de"], w) for v, w in zip(saved, E.full)]
        (grad_x,) = matmul([pairs], f32, 512, "x_back", Load(sx, se, so), nt=True)
        high, low, _, gain_one_part = norm_back(
            [grad_x, grad_z], rows_in, gain_one, [mixed_grad, mixed_low], "norm_one_back", Load(sx, se, sz)
        )
        (layer_out,) = matmul([[(out_low, turn)]], bf16, 512, "turn_out", Load(sx, se), nt=True)
        (input_grad,) = matmul([[(high, turn), (low, turn)]], f32, 512, "turn_back", Load(sx, se), nt=True)

        gain_one_total = sum_all(to_global(gain_one_part), n, True)
        dt_b_total, a_total = hg[0, :heads], hg[1, :heads]
        skip_total = jnp.sum(cg[5].reshape(heads, HEADDIM), axis=1)
        return (
            layer_out,
            input_grad,
            gain_one_total,
            sx.out,
            sz.out,
            se.out[:, :heads],
            2.0 * se.out[:, heads : heads + 2 * states],
            cg[:4],
            cg[4],
            dt_b_total,
            a_total,
            skip_total,
            so.out,
            gain_two_total,
            jnp.concatenate([ga.out, gb.out], axis=1),
            jnp.concatenate([ua.out, ub.out], axis=1),
            jnp.concatenate([da.out, db.out], axis=1),
        )

    return local


def solution(mesh):
    rows = P(("fsdp", "tp"), None)
    weight = P("fsdp", "tp")
    in_specs = (
        rows, P("fsdp"), P(), weight, weight, weight, P("fsdp", None), P(None, "tp"), P("tp"), P("tp"), P("tp"),
        P("tp"), weight, P(), weight, weight, weight, rows,
    )
    out_specs = (
        rows, rows, P(), weight, weight, weight, P("fsdp", None), P(None, "tp"), P("tp"), P("tp"), P("tp"), P("tp"),
        weight, P(), weight, weight, weight,
    )
    return jax.shard_map(
        make_local(mesh.shape["fsdp"]), mesh=mesh, in_specs=in_specs, out_specs=out_specs, check_vma=False
    )
```

```python
import functools

import jax
import jax.numpy as jnp
from jax import lax
from jax.experimental import pallas as pl
from jax.experimental.pallas import tpu as pltpu
from jax.sharding import PartitionSpec as P

HEADDIM = 64
HEADS = 24
STATES = 16
Q = 128
HALO = 16
EXTRA = 128
RUN, DT, DEC, TAIL, SEG, CONT, LAST, LOGDT = 0, 24, 48, 72, 96, 100, 101, 104
COLB, COLC = HEADS, HEADS + STATES

f32 = jnp.float32
bf16 = jnp.bfloat16
highest = lax.Precision.HIGHEST
epsilon = 1e-05
NEG = -1e30


def dot(a, b, precision=None):
    return jnp.dot(a, b, preferred_element_type=f32, precision=precision)


def dot_t(a, b):
    return lax.dot_general(a, b, (((1,), (1,)), ((), ())), preferred_element_type=f32)


def split(v):
    high = v.astype(bf16)
    return high, (v - high.astype(f32)).astype(bf16)


def wide_left(v):
    high, low = split(v)
    return jnp.concatenate([high, low, high], axis=1)


def stack_right(v):
    high, low = split(v)
    return jnp.concatenate([high, high, low], axis=0)


def sigmoid(v):
    return 0.5 * jnp.tanh(0.5 * v) + 0.5


def lanes_of(rows=Q):
    return lax.broadcasted_iota(jnp.int32, (rows, 128), 1)


def pair_cols(col, first, j, left):
    a = col[:, first + 2 * j : first + 2 * j + 1]
    b = col[:, first + 2 * j + 1 : first + 2 * j + 2]
    return jnp.where(left, a, b)


def triangle(strict=False, transposed=False):
    i = lax.broadcasted_iota(jnp.int32, (Q, Q), 1 if transposed else 0)
    k = lax.broadcasted_iota(jnp.int32, (Q, Q), 0 if transposed else 1)
    return (i > k) if strict else (i >= k)


def spread_marks(col):
    return [jnp.broadcast_to(col[:, SEG + k : SEG + k + 1], (Q, 128)) for k in (1, 2, 3)]


def conv_rows(x_ref, xp_ref, halo_ref, cw_ref, marks, q, lanes):
    x = x_ref[:, lanes]
    prev = jnp.where(q == 0, halo_ref[:, lanes], xp_ref[:, lanes])
    cat = jnp.concatenate([prev, x], axis=0)
    acc = cw_ref[4:5, lanes] + cw_ref[0:1, lanes] * x
    shifted = []
    for k in (1, 2, 3):
        back = pltpu.roll(cat, k, 0)[HALO:, :] * marks[k - 1]
        shifted.append(back)
        acc = acc + cw_ref[k : k + 1, lanes] * back
    return x, shifted, acc


def conv_state_kernel(
    x_ref, xp_ref, halo_ref, cw_ref, e_ref, hp_ref, mark_ref, u_ref, end_ref, col_ref, row_ref, et_ref
):
    q = pl.program_id(0)

    @pl.when(q == 0)
    def _():
        end_ref[...] = jnp.zeros_like(end_ref)

    e, marks = e_ref[...], mark_ref[...]
    lane = lanes_of()
    head = lane < HEADS
    raw = e + hp_ref[0:1, :]
    dt = jnp.where(head, jnp.maximum(raw, 0.0) + jnp.log1p(jnp.exp(-jnp.abs(raw))), 0.0)
    run = dot(jnp.where(triangle(), 1.0, 0.0), dt * hp_ref[1:2, :], highest)
    dec = jnp.where(head, jnp.exp(run) * marks[:, CONT : CONT + 1], 0.0)
    tail = jnp.where(head, jnp.exp(run[Q - 1 : Q, :] - run) * marks[:, LAST : LAST + 1], 0.0)
    log_dt = jnp.where(head, jnp.log(dt), 0.0)
    col = (
        run
        + pltpu.roll(dt, DT, 1)
        + pltpu.roll(dec, DEC, 1)
        + pltpu.roll(tail, TAIL, 1)
        + marks
        + pltpu.roll(log_dt, LOGDT, 1)
    )
    col_ref[...] = col
    row_ref[...] = col.T
    et = e.T
    et_ref[...] = et
    bt = wide_left(et[COLB:COLC, :])
    left = lane < HEADDIM
    spread = spread_marks(col)
    for j in range(x_ref.shape[1] // 128):
        lanes = slice(128 * j, 128 * j + 128)
        _, _, acc = conv_rows(x_ref, xp_ref, halo_ref, cw_ref, spread, q, lanes)
        u = acc * sigmoid(acc)
        u_ref[:, lanes] = u
        scaled = u * (pair_cols(col, DT, j, left) * pair_cols(col, TAIL, j, left))
        keep = pair_cols(col[Q - 1 : Q, :], DEC, j, left[:1])
        end_ref[:, lanes] = keep * end_ref[:, lanes] + dot(bt, stack_right(scaled))


def scan_kernel(
    u_ref, z_ref, col_ref, row_ref, e_ref, et_ref, s0_ref, cw_ref, gated_ref, y_ref, st_ref, S
):
    @pl.when(pl.program_id(0) == 0)
    def _():
        S[...] = s0_ref[...]

    col, row = col_ref[...], row_ref[...]
    left = lanes_of() < HEADDIM
    c = e_ref[:, COLC : COLC + STATES]
    bt = et_ref[COLB:COLC, :]
    scores = dot(c, bt, highest)
    neg = jnp.where((col[:, SEG : SEG + 1] == row[SEG : SEG + 1, :]) & triangle(), 0.0, NEG)
    c, bt = wide_left(c), wide_left(bt)
    for j in range(u_ref.shape[1] // 128):
        lanes = slice(128 * j, 128 * j + 128)
        uf = u_ref[:, lanes]
        u, u_low = split(uf)
        state = S[:, lanes]
        st_ref[:, lanes] = state
        parts, rest = [], []
        for h in (2 * j, 2 * j + 1):
            gap = col[:, h : h + 1] - (row[h : h + 1, :] - row[LOGDT + h : LOGDT + h + 1, :])
            high, low = split(jnp.exp(gap + neg) * scores)
            parts.append(high)
            rest.append(low)
        zero = jnp.zeros_like(u)
        both = [jnp.where(left, u, zero), jnp.where(left, zero, u)]
        both_low = [jnp.where(left, u_low, zero), jnp.where(left, zero, u_low)]
        y = dot(jnp.concatenate(parts + rest + parts, axis=1), jnp.concatenate(both + both + both_low, axis=0))
        y = y + dot(c, stack_right(state)) * pair_cols(col, DEC, j, left) + cw_ref[5:6, lanes] * uf
        z = z_ref[:, lanes]
        y_ref[:, lanes] = y
        gated_ref[:, lanes] = (y * (z * sigmoid(z))).astype(bf16)
        scaled = uf * (pair_cols(col, DT, j, left) * pair_cols(col, TAIL, j, left))
        keep = pair_cols(col[Q - 1 : Q, :], DEC, j, left[:1])
        S[:, lanes] = keep * state + dot(bt, stack_right(scaled))


def gate_back_kernel(gg_ref, z_ref, y_ref, col_ref, et_ref, dy_ref, dz_ref, ds_ref):
    @pl.when(pl.program_id(0) == 0)
    def _():
        ds_ref[...] = jnp.zeros_like(ds_ref)

    col = col_ref[...]
    left = lanes_of() < HEADDIM
    ct = et_ref[COLC : COLC + STATES, :].astype(bf16)
    for j in range(z_ref.shape[1] // 128):
        lanes = slice(128 * j, 128 * j + 128)
        z = z_ref[:, lanes]
        gg = gg_ref[:, lanes]
        sig = sigmoid(z)
        dy = gg * (z * sig)
        dy_ref[:, lanes] = dy
        dz_ref[:, lanes] = (gg * y_ref[:, lanes] * (sig * (1.0 + z * (1.0 - sig)))).astype(bf16)
        scaled = (dy * pair_cols(col, DEC, j, left)).astype(bf16)
        keep = pair_cols(col[Q - 1 : Q, :], DEC, j, left[:1])
        ds_ref[:, lanes] = keep * ds_ref[:, lanes] + dot(ct, scaled)


def scan_back_kernel(
    u_ref, dy_ref, x_ref, xp_ref, halo_ref, cw_ref, col_ref, row_ref, e_ref, et_ref, st_ref, de_ref, hp_ref,
    lw_ref, sm_ref, pick_ref, head_ref,
    dx_ref, de_out_ref, cg_ref, edge_ref, hg_ref,
    D, WA, CONST, TAILS, DECS, DS, ST, SUMS, DG,
):
    step = pl.program_id(0)
    q = pl.num_programs(0) - 1 - step

    @pl.when(step == 0)
    def _():
        D[...] = de_ref[...]
        cg_ref[...] = jnp.zeros_like(cg_ref)
        edge_ref[...] = jnp.zeros_like(edge_ref)
        hg_ref[...] = jnp.zeros_like(hg_ref)
        WA[...] = jnp.zeros_like(WA)
        CONST[...] = jnp.zeros_like(CONST)
        DS[...] = jnp.zeros_like(DS)
        ST[...] = jnp.zeros_like(ST)

    col, row = col_ref[...], row_ref[...]
    lane = lanes_of()
    left = lane < HEADDIM
    e = e_ref[...]
    b, ct = e[:, COLB:COLC], et_ref[COLC : COLC + STATES, :]
    scores = dot(b, ct, highest)
    neg = jnp.where((col[:, SEG : SEG + 1] == row[SEG : SEG + 1, :]) & triangle(transposed=True), 0.0, NEG)
    b, ct, c = wide_left(b), ct.astype(bf16), wide_left(e[:, COLC : COLC + STATES])
    spread = spread_marks(col)
    DG[...] = jnp.zeros_like(DG)
    SUMS[...] = jnp.zeros_like(SUMS)
    for j in range(u_ref.shape[1] // 128):
        lanes = slice(128 * j, 128 * j + 128)
        u = u_ref[:, lanes]
        dyf = dy_ref[:, lanes]
        dy = dyf.astype(bf16)
        dt = pair_cols(col, DT, j, left)
        dec = pair_cols(col, DEC, j, left)
        tail = pair_cols(col, TAIL, j, left)
        keep = pair_cols(col[Q - 1 : Q, :], DEC, j, left[:1])
        state, grad_state = st_ref[:, lanes], D[:, lanes]
        DS[COLB:COLC, lanes] = grad_state
        ST[COLC : COLC + STATES, lanes] = state
        xs = u * dt
        zero = jnp.zeros_like(dy)
        both = jnp.concatenate([jnp.where(left, dy, zero), jnp.where(left, zero, dy)], axis=0)
        d_mat = dot_t(xs.astype(bf16), both)
        mats, pairs, d_scores = [], [], None
        for i, h in enumerate((2 * j, 2 * j + 1)):
            decay = jnp.exp((row[h : h + 1, :] - col[:, h : h + 1]) + neg)
            mat = decay * scores
            dm = d_mat[:, Q * i : Q * i + Q]
            d_scores = decay * dm if d_scores is None else d_scores + decay * dm
            mats.append(mat.astype(bf16))
            pairs.append((mat * dm).astype(bf16))
        DG[...] += d_scores
        dxs = dot(jnp.concatenate(mats, axis=1), both)
        spans = dot(jnp.concatenate(pairs, axis=1), lw_ref[...]) * sm_ref[...]
        sums = jnp.sum(spans, axis=0, keepdims=True)
        WA[2 * j : 2 * j + 1, :] = sums[:, :Q]
        WA[2 * j + 1 : 2 * j + 2, :] = sums[:, Q:]
        from_tail = tail * dot(b, stack_right(grad_state))
        dxs = dxs + from_tail
        ydec = dyf * dec
        found = [u * dxs, ydec * dot(c, stack_right(state)), xs * from_tail]
        SUMS[...] += dot(jnp.concatenate([v.astype(bf16) for v in found], axis=1), pick_ref[j])
        TAILS[:, lanes] = (xs * tail).astype(bf16)
        low_dec = ydec.astype(bf16)
        DECS[:, lanes] = low_dec
        CONST[0:1, lanes] = keep * jnp.sum(state * grad_state, axis=0, keepdims=True)
        D[:, lanes] = keep * grad_state + dot(ct, low_dec)

        x, shifted, acc = conv_rows(x_ref, xp_ref, halo_ref, cw_ref, spread, q, lanes)
        sig = sigmoid(acc)
        dconv = (dxs * dt + cw_ref[5:6, lanes] * dyf) * (sig * (1.0 + acc * (1.0 - sig)))
        dx = cw_ref[0:1, lanes] * dconv
        cg_ref[0:1, lanes] += jnp.sum(dconv * x, axis=0, keepdims=True)
        for k in (1, 2, 3):
            masked = dconv * spread[k - 1]
            after = edge_ref[8 * (k - 1) : 8 * k, lanes]
            cat = jnp.concatenate([masked, after], axis=0)
            dx = dx + cw_ref[k : k + 1, lanes] * pltpu.roll(cat, Q + 8 - k, 0)[:Q, :]
            edge_ref[8 * (k - 1) : 8 * k, lanes] = masked[:8, :]
            cg_ref[k : k + 1, lanes] += jnp.sum(dconv * shifted[k - 1], axis=0, keepdims=True)
        cg_ref[4:5, lanes] += jnp.sum(dconv, axis=0, keepdims=True)
        cg_ref[5:6, lanes] += jnp.sum(dyf * u, axis=0, keepdims=True)
        dx_ref[:, lanes] = dx.astype(bf16)

    head = lane < HEADS
    found = SUMS[...]
    suffix = jnp.where(triangle(transposed=True), 1.0, 0.0)
    prefix = jnp.where(triangle(strict=True), 1.0, 0.0)
    d_step = (
        WA[...].T
        + dot(suffix, pltpu.roll(found, 128 - HEADS, 1), highest)
        + dot(prefix, pltpu.roll(found, 128 - 2 * HEADS, 1), highest)
        + dot(CONST[...], head_ref[...], highest)[0:1, :]
    )
    d_dt = d_step * hp_ref[1:2, :] + found
    d_raw = jnp.where(head, d_dt * sigmoid(e + hp_ref[0:1, :]), 0.0)
    step_dt = jnp.where(head, pltpu.roll(col, 128 - DT, 1), 0.0)
    hg_ref[0:1, :] += jnp.sum(d_raw, axis=0, keepdims=True)
    hg_ref[1:2, :] += jnp.sum(jnp.where(head, d_step, 0.0) * step_dt, axis=0, keepdims=True) * hp_ref[1:2, :]
    total = DG[...]
    b_part = jnp.where((lane >= COLB) & (lane < COLC), e, 0.0)
    c_part = jnp.where((lane >= COLC) & (lane < COLC + STATES), e, 0.0)
    de_out_ref[...] = (
        d_raw
        + dot_t(TAILS[...], DS[...].astype(bf16))
        + dot_t(DECS[...], ST[...].astype(bf16))
        + dot(total, pltpu.roll(c_part, 128 - STATES, 1), highest)
        + dot(total.T, pltpu.roll(b_part, STATES, 1), highest)
    )


def norm_kernel(*refs):
    *row_refs, gain_ref, hidden_ref, out_ref, turned_ref = refs
    rows = row_refs[0][...]
    for r in row_refs[1:]:
        rows = rows + r[...]
    hidden_ref[...] = rows
    scale = lax.rsqrt(jnp.mean(rows * rows, axis=-1, keepdims=True) + epsilon)
    normed = rows * scale * gain_ref[...]
    out_ref[...] = normed.astype(bf16)
    turned_ref[...] = normed.T.astype(bf16)


def norm_back_kernel(n_grads, rows_ref, gain_ref, *refs):
    *given, high_ref, low_ref, part_ref, turned_ref = refs

    @pl.when(pl.program_id(0) == 0)
    def _():
        part_ref[...] = jnp.zeros_like(part_ref)

    rows, grad = rows_ref[...], given[0][...]
    for r in given[1:n_grads]:
        grad = grad + r[...]
    scale = lax.rsqrt(jnp.mean(rows * rows, axis=-1, keepdims=True) + epsilon)
    unit = rows * scale
    part_ref[0:1, :] += jnp.sum(grad * unit, axis=0, keepdims=True)
    unit_grad = grad * gain_ref[...]
    total = scale * (unit_grad - unit * jnp.mean(unit_grad * unit, axis=-1, keepdims=True))
    for r in given[n_grads:]:
        total = total + r[...].astype(f32)
    high = total.astype(bf16)
    high_ref[...] = high
    low_ref[...] = (total - high.astype(f32)).astype(bf16)
    turned_ref[...] = total.T.astype(bf16)


def flip(i, mask):
    bit = 1
    while bit <= mask:
        if mask & bit:
            i = i + bit * (1 - 2 * ((i // bit) % 2))
        bit *= 2
    return i


class Load:
    def __init__(self, *movers):
        self.reads, self.updates, self.news, self.copies = {}, {}, {}, []
        self.movers = movers
        for mover in movers:
            reads, updates, news, copies = mover.moves()
            self.reads.update(reads)
            self.updates.update(updates)
            self.news.update(news)
            self.copies += copies

    def arrive(self, got):
        for mover in self.movers:
            mover.take(got)


IDS = {}


def run(body, grid, in_specs, out_specs, out_shape, scratch, args, name, estimate=None, load=None, vmem=56):
    params = dict(dimension_semantics=("arbitrary",) * len(grid), vmem_limit_bytes=vmem * 1024 * 1024)
    if load is None:
        return pl.pallas_call(
            body, name=name, grid=grid, in_specs=in_specs, out_specs=out_specs, out_shape=out_shape,
            scratch_shapes=scratch, compiler_params=pltpu.CompilerParams(**params), cost_estimate=estimate,
        )(*args)
    cid = IDS.setdefault(name, len(IDS) + 1)
    reads, updates, news = list(load.reads), list(load.updates), list(load.news)
    n_in, n_out, n_scratch, n_copies = len(args), len(out_shape), len(scratch), len(load.copies)
    routes = []
    for c in load.copies:
        if c[4] is not None and c[4] not in routes:
            routes.append(c[4])

    def kernel(*refs):
        ins, rest = refs[:n_in], refs[n_in:]
        held = dict(zip(reads, rest))
        rest = rest[len(reads) + len(updates) :]
        outs, rest = rest[:n_out], rest[n_out:]
        held.update(zip(updates + news, rest))
        rest = rest[len(updates) + len(news) :]
        mine, (send, recv) = rest[:n_scratch], rest[n_scratch:]

        def device(route):
            return {route[0]: flip(lax.axis_index(route[0]), route[1])}

        def make(i, c):
            src, dst = held[c[0]].at[c[1]], held[c[2]].at[c[3]]
            if c[4] is None:
                return pltpu.make_async_copy(src, dst, recv.at[i])
            return pltpu.make_async_remote_copy(
                src_ref=src, dst_ref=dst, send_sem=send.at[i], recv_sem=recv.at[i],
                device_id=device(c[4]), device_id_type=pl.DeviceIdType.MESH,
            )

        first, last = pl.program_id(0) == 0, pl.program_id(0) == grid[0] - 1
        for axis in range(1, len(grid)):
            first = first & (pl.program_id(axis) == 0)
            last = last & (pl.program_id(axis) == grid[axis] - 1)

        @pl.when(first)
        def _():
            barrier = pltpu.get_barrier_semaphore()
            for route in routes:
                pl.semaphore_signal(
                    barrier, inc=1, device_id=device(route), device_id_type=pl.DeviceIdType.MESH
                )
            pl.semaphore_wait(barrier, len(routes))
            for i, c in enumerate(load.copies):
                make(i, c).start()

        if body is not None:
            body(*ins, *outs, *mine)

        @pl.when(last)
        def _():
            for i, c in enumerate(load.copies):
                make(i, c).wait()

    hbm = pl.BlockSpec(memory_space=pltpu.HBM)
    result = pl.pallas_call(
        kernel,
        name=name,
        grid=grid,
        in_specs=list(in_specs) + [hbm] * (len(reads) + len(updates)),
        out_specs=list(out_specs) + [hbm] * (len(updates) + len(news)),
        out_shape=list(out_shape)
        + [jax.ShapeDtypeStruct(load.updates[k].shape, load.updates[k].dtype) for k in updates]
        + [load.news[k] for k in news],
        scratch_shapes=list(scratch) + [pltpu.SemaphoreType.DMA((n_copies,)), pltpu.SemaphoreType.DMA((n_copies,))],
        input_output_aliases={n_in + len(reads) + i: n_out + i for i in range(len(updates))},
        compiler_params=pltpu.CompilerParams(collective_id=cid, has_side_effects=True, **params),
        cost_estimate=estimate,
    )(*args, *[load.reads[k] for k in reads], *[load.updates[k] for k in updates])
    load.arrive(dict(zip(updates + news, result[n_out:])))
    return result[:n_out]


def matmul(jobs, dtype, tile, name, load=None, nt=False, turned=False, beside=None):
    n_jobs, n_pairs = len(jobs), len(jobs[0])
    rows = jobs[0][0][0].shape[0]
    columns = jobs[0][0][1].shape[0 if nt else 1]
    tiles = columns // tile

    def at(job):
        def place(j, t):
            return jnp.where(j == job, t, jnp.where(j < job, 0, tiles - 1))

        return place

    args, in_specs = [], []
    for job, pairs in enumerate(jobs):
        for left, right in pairs:
            args += [left, right]
            k = left.shape[1]
            in_specs.append(pl.BlockSpec((rows, k), lambda j, t: (0, 0), pipeline_mode=pl.Buffered(1)))
            if nt:
                in_specs.append(pl.BlockSpec((tile, k), lambda j, t, p=at(job): (p(j, t), 0)))
            else:
                in_specs.append(pl.BlockSpec((k, tile), lambda j, t, p=at(job): (0, p(j, t))))
    out_specs = [pl.BlockSpec((rows, tile), lambda j, t, p=at(job): (0, p(j, t))) for job in range(n_jobs)]
    out_shape = [jax.ShapeDtypeStruct((rows, columns), dtype)] * n_jobs
    if turned:
        out_specs += [pl.BlockSpec((tile, rows), lambda j, t, p=at(job): (p(j, t), 0)) for job in range(n_jobs)]
        out_shape += [jax.ShapeDtypeStruct((columns, rows), dtype)] * n_jobs
    if beside:
        few, narrow = beside
        args += [few, *narrow]
        in_specs += [pl.BlockSpec(v.shape, lambda j, t: (0, 0), pipeline_mode=pl.Buffered(1)) for v in (few, *narrow)]
        out_specs += [pl.BlockSpec((few.shape[0], tile), lambda j, t, p=at(job): (0, p(j, t))) for job in range(n_jobs)]
        out_shape += [jax.ShapeDtypeStruct((few.shape[0], columns), dtype)] * n_jobs
        out_specs += [pl.BlockSpec((rows, v.shape[1]), lambda j, t: (0, 0)) for v in narrow]
        out_shape += [jax.ShapeDtypeStruct((rows, v.shape[1]), dtype) for v in narrow]
    n_in = len(args)

    def body(*refs):
        ins, outs = refs[:n_in], refs[n_in:]
        for job in range(n_jobs):

            @pl.when(pl.program_id(0) == job)
            def _(job=job):
                total = None
                for p in range(n_pairs):
                    left, right = ins[2 * (job * n_pairs + p)], ins[2 * (job * n_pairs + p) + 1]
                    term = (dot_t if nt else dot)(left[...], right[...])
                    total = term if total is None else total + term
                outs[job][...] = total.astype(dtype)
                if turned:
                    outs[n_jobs + job][...] = total.T.astype(dtype)
                if beside:
                    left, right, few = ins[2 * job * n_pairs], ins[2 * job * n_pairs + 1], ins[2 * n_jobs * n_pairs]
                    outs[n_jobs + job][...] = dot(few[...], right[...]).astype(dtype)

                    @pl.when(pl.program_id(1) == 0)
                    def _():
                        narrow = ins[2 * n_jobs * n_pairs + 1 + job]
                        outs[2 * n_jobs + job][...] = dot(left[...], narrow[...]).astype(dtype)

    depth = sum(p[0].shape[1] for p in jobs[0])
    return run(
        body, (n_jobs, tiles), in_specs, out_specs, out_shape, [], args, name,
        pl.CostEstimate(
            flops=2 * n_jobs * rows * columns * depth, bytes_accessed=4 * n_jobs * rows * columns, transcendentals=0
        ),
        load,
    )


class LateScatter:
    def __init__(self, key, n, other):
        self.key, self.n, self.phase = key, n, 0
        self.given(other)

    def given(self, grad):
        self.rows, self.cols = grad.shape[0] // self.n, grad.shape[1]
        self.now = grad.reshape(2, self.n, self.rows // 2, self.cols)

    def moves(self):
        k, q, v = self.key, self.n // 4, self.now
        far, rest = slice(q, 2 * q), slice(2 * q, 4 * q)

        def new(*dims):
            return jax.ShapeDtypeStruct(dims + (self.rows // 2, self.cols), bf16)

        core = [(k + "v", (i, rest), k + "r", (i,), ("fsdp", 1)) for i in (0, 1)]
        if self.phase == 0:
            return {k + "v": v}, {}, {k + "r": new(2, 2 * q)}, core
        if self.phase == 1:
            copies = [(k + "v", (0, far), k + "r", ALL, ("fsdp", 2)), (k + "v", (1,), k + "s", ALL, ("tp", 1))]
            return {k + "v": v}, {}, {k + "r": new(q), k + "s": new(2 * q)}, copies
        if self.phase == 2:
            copies = core + [(k + "a", ALL, k + "s", ALL, ("tp", 1))]
            return {k + "v": v, k + "a": self.other}, {}, {k + "r": new(2, 2 * q), k + "s": new(q)}, copies
        if self.phase == 3:
            copies = [(k + "v", (far,), k + "r", ALL, ("fsdp", 2)), (k + "a", (far,), k + "s", ALL, ("fsdp", 2))]
            return {k + "v": v[0], k + "a": v[1]}, {}, {k + "r": new(q), k + "s": new(q)}, copies
        news = {f"{k}r{m}": new(2) for m in range(1, q)}
        copies = [(f"{k}v{i}", (m,), f"{k}r{m}", (i,), ("fsdp", m << 2)) for m in range(1, q) for i in (0, 1)]
        return {k + "v0": v[0], k + "v1": v[1]}, {}, news, copies

    def take(self, got):
        k, q, v = self.key, self.n // 4, self.now
        if self.phase == 0:
            self.now = low_sum(v[:, : 2 * q], got[k + "r"])
        elif self.phase == 1:
            self.other, self.lower = low_sum(v[0, :q], got[k + "r"]), got[k + "s"]
        elif self.phase == 2:
            own = [v[i, : 2 * q].astype(f32) + got[k + "r"][i].astype(f32) for i in (0, 1)]
            self.now = [own[0].astype(bf16), (own[1] + self.lower.astype(f32)).astype(bf16)]
            self.other = got[k + "s"]
        elif self.phase == 3:
            upper = v[0][:q].astype(f32) + got[k + "r"].astype(f32) + self.other.astype(f32)
            self.now = [upper.astype(bf16), low_sum(v[1][:q], got[k + "s"])]
        else:
            total = jnp.stack([v[0][0], v[1][0]]).astype(f32)
            for m in range(1, q):
                total = total + got[f"{k}r{m}"].astype(f32)
            self.out = total.reshape(self.rows, self.cols)
        self.phase += 1


def feed_forward(normed, cot, gate_w, up_w, down_w):
    tokens, width = normed.shape
    cols, tile, step = gate_w[0].shape[1], 512, 256
    tiles = cols // tile

    def at(job):
        def place(j, t):
            return jnp.where(j == job, t, jnp.where(j < job, 0, tiles - 1))

        return place

    whole = pl.BlockSpec((tokens, width), lambda j, t: (0, 0), pipeline_mode=pl.Buffered(1))
    args, in_specs, out_specs = [normed, cot], [whole, whole], []
    for b in (0, 1):
        args += [gate_w[b], up_w[b], down_w[b]]
        in_specs += [pl.BlockSpec((width, tile), lambda j, t, p=at(b): (0, p(j, t)))] * 3
        out_specs += [pl.BlockSpec((tokens, tile), lambda j, t, p=at(b): (0, p(j, t)))] * 3

    def body(n_ref, c_ref, *refs):
        for b in (0, 1):
            wg, wu, wd = refs[3 * b : 3 * b + 3]
            act, gg, ug = refs[6 + 3 * b : 9 + 3 * b]

            @pl.when(pl.program_id(0) == b)
            def _(wg=wg, wu=wu, wd=wd, act=act, gg=gg, ug=ug):
                for i in range(tokens // step):
                    rows = slice(step * i, step * i + step)
                    gate, up, back = dot(n_ref[rows, :], wg[...]), dot(n_ref[rows, :], wu[...]), dot(c_ref[rows, :], wd[...])
                    sig = sigmoid(gate)
                    silu = gate * sig
                    act[rows, :] = (silu * up).astype(bf16)
                    gg[rows, :] = (back * up * sig * (1.0 + gate * (1.0 - sig))).astype(bf16)
                    ug[rows, :] = (back * silu).astype(bf16)

    out = run(
        body, (2, tiles), in_specs, out_specs, [jax.ShapeDtypeStruct((tokens, cols), bf16)] * 6, [], args,
        "feed_forward", pl.CostEstimate(flops=12 * tokens * cols * width, bytes_accessed=12 * tokens * cols, transcendentals=0),
    )
    return [out[0], out[3]], [out[1], out[4]], [out[2], out[5]]


def carry_only(load, name):
    run(None, (1,), [], [], [], [], [], name, None, load)


ALL = (slice(None),)


def low_sum(a, b):
    return a + b


class Gather:
    def __init__(self, key, shard, n):
        rows, cols = shard.shape
        self.n, self.key, self.phase = n, key, 0
        self.shard = shard.reshape(2, rows // 2, cols)
        self.cols = cols

    def moves(self):
        k, n = self.key, self.n
        q = n // 4
        s, a, b = k + "s", k + "0", k + "1"
        if self.phase == 0:
            whole = jax.ShapeDtypeStruct((2, n) + self.shard.shape[1:], bf16)
            copies = [
                (s, (i,), a, (i, m), ("fsdp", m << 2) if m else None) for m in range(q) for i in (0, 1)
            ]
            return {s: self.shard}, {}, {a: whole, b: whole}, copies
        near, far, both = slice(0, q), slice(q, 2 * q), slice(0, 2 * q)
        if self.phase == 1:
            copies = [(a, (0, near), b, (0, near), ("tp", 1)), (a, (1, near), a, (1, far), ("fsdp", 2))]
        elif self.phase == 2:
            copies = [
                (a, (0, near), a, (0, far), ("fsdp", 2)),
                (b, (0, near), b, (0, far), ("fsdp", 2)),
                (a, (1, both), b, (1, both), ("tp", 1)),
            ]
        else:
            copies = [(h, (i, both), h, (i, slice(2 * q, 4 * q)), ("fsdp", 1)) for h in (a, b) for i in (0, 1)]
        return {}, {a: self.halves[0], b: self.halves[1]}, {}, copies

    def take(self, got):
        self.halves = [got[self.key + "0"], got[self.key + "1"]]
        self.phase += 1
        if self.phase == 4:
            self.full = [h.reshape(-1, self.cols) for h in self.halves]


class Scatter:
    def __init__(self, key, grads, n, piece=0, pieces=1):
        self.n, self.key, self.phase = n, f"{key}{piece}_", 0
        cols = grads[0].shape[1]
        self.cols = cols // pieces
        self.rows = grads[0].shape[0] // n
        self.now = [g.reshape(2, n, self.rows // 2, cols) for g in grads]
        self.range = slice(piece * self.cols, (piece + 1) * self.cols)

    def moves(self):
        n, v = self.n, self.now
        q = n // 4
        part = (self.rows // 2, self.cols)
        far, rest = slice(q, 2 * q), slice(2 * q, 4 * q)

        def name(i):
            return f"{self.key}{i}"

        def new(*dims):
            return jax.ShapeDtypeStruct(dims + part, bf16)

        if self.phase == 0:
            news = [new(2, 2 * q), new(2, 2 * q)]
            copies = [
                (b, (i, rest, slice(None), self.range), b, (i,), ("fsdp", 1)) for b in (0, 1) for i in (0, 1)
            ]
        elif self.phase == 1:
            news = [new(q), new(q), new(2 * q)]
            copies = [
                (0, (0, far), 0, ALL, ("fsdp", 2)),
                (1, (0, far), 1, ALL, ("fsdp", 2)),
                (1, (1,), 2, ALL, ("tp", 1)),
            ]
        elif self.phase == 2:
            news = [new(q), new(q)]
            copies = [(1, ALL, 0, ALL, ("tp", 1)), (2, (far,), 1, ALL, ("fsdp", 2))]
        else:
            news = [new(2) for _ in range(1, q)]
            copies = [(i, (m,), m - 1, (i,), ("fsdp", m << 2)) for m in range(1, q) for i in (0, 1)]
        reads = {name(f"v{i}"): a for i, a in enumerate(v) if any(c[0] == i for c in copies)}
        self.names = [name(f"r{i}") for i in range(len(news))]
        copies = [(name(f"v{c[0]}"), c[1], self.names[c[2]], c[3], c[4]) for c in copies]
        return reads, {}, dict(zip(self.names, news)), copies

    def take(self, got):
        r, v = [got[k] for k in self.names], self.now
        q = self.n // 4
        if self.phase == 0:
            self.now = [low_sum(p[:, : 2 * q, :, self.range], a) for p, a in zip(v, r)]
        elif self.phase == 1:
            self.now = [low_sum(v[0][0, :q], r[0]), low_sum(v[1][0, :q], r[1]), low_sum(v[0][1], r[2])]
        elif self.phase == 2:
            self.now = [low_sum(v[0], r[0]), low_sum(v[2][:q], r[1])]
        else:
            total = jnp.stack([v[0][0], v[1][0]]).astype(f32)
            for p in r:
                total = total + p.astype(f32)
            self.out = total.reshape(self.rows, self.cols)
        self.phase += 1


def specs(blocks, ch, reverse):
    def at(q):
        return blocks - 1 - q if reverse else q

    def whole(rows, cols):
        return pl.BlockSpec((rows, cols), lambda q: (0, 0))

    return dict(
        main=pl.BlockSpec((Q, ch), lambda q: (at(q), 0)),
        prev=pl.BlockSpec((HALO, ch), lambda q: (jnp.maximum(at(q) * (Q // HALO) - 1, 0), 0)),
        tile=pl.BlockSpec((Q, 128), lambda q: (at(q), 0)),
        state=pl.BlockSpec((STATES, ch), lambda q: (at(q), 0)),
        halo=whole(HALO, ch), row8=whole(8, ch), row24=whole(24, ch), row16=whole(STATES, ch), small=whole(8, 128),
    )


def shape(dims, dtype):
    return jax.ShapeDtypeStruct(dims, dtype)


def cost(flops, moved):
    return pl.CostEstimate(flops=int(flops), bytes_accessed=int(moved), transcendentals=0)


def conv_state(x, halo, cw, e, hp, marks, tag="", load=None):
    tokens, ch = x.shape
    s = specs(tokens // Q, ch, False)
    return run(
        conv_state_kernel,
        (tokens // Q,),
        [s["main"], s["prev"], s["halo"], s["row8"], s["tile"], s["small"], s["tile"]],
        [s["main"], s["row16"], s["tile"], s["tile"], s["tile"]],
        [shape((tokens, ch), f32), shape((STATES, ch), f32)] + [shape((tokens, 128), f32)] * 3,
        [],
        [x, x, halo, cw, e, hp, marks],
        "conv_state" + tag,
        cost(tokens * ch * 5000, 4 * tokens * ch),
        load,
    )


def scan_forward(u, z, col, row, e, et, s0, cw, tag="", load=None):
    tokens, ch = u.shape
    s = specs(tokens // Q, ch, False)
    return run(
        scan_kernel,
        (tokens // Q,),
        [s["main"], s["main"], s["tile"], s["tile"], s["tile"], s["tile"], s["row16"], s["row8"]],
        [s["main"], s["main"], s["state"]],
        [shape((tokens, ch), bf16), shape((tokens, ch), f32), shape((tokens // Q * STATES, ch), f32)],
        [pltpu.VMEM((STATES, ch), f32)],
        [u, z, col, row, e, et, s0, cw],
        "scan_forward" + tag,
        cost(tokens * ch * 10000, 8 * tokens * ch),
        load,
    )


def gate_backward(gg, z, y, col, et, tag="", load=None):
    tokens, ch = z.shape
    s = specs(tokens // Q, ch, True)
    return run(
        gate_back_kernel,
        (tokens // Q,),
        [s["main"], s["main"], s["main"], s["tile"], s["tile"]],
        [s["main"], s["main"], s["row16"]],
        [shape((tokens, ch), f32), shape((tokens, ch), bf16), shape((STATES, ch), f32)],
        [],
        [gg, z, y, col, et],
        "gate_backward" + tag,
        cost(tokens * ch * 5000, 10 * tokens * ch),
        load,
    )


def scan_backward(u, dy, x, halo, cw, col, row, e, et, st, de, hp, tag="", load=None):
    tokens, ch = u.shape
    s = specs(tokens // Q, ch, True)
    place = jnp.arange(2 * Q)
    lower = ((place[:, None] >= place[None, :]) & (place[:, None] // Q == place[None, :] // Q)).astype(bf16)
    strict = (jnp.arange(Q)[:, None] < (place % Q)[None, :]).astype(f32)
    pairs = ch // 128
    lane = jnp.arange(3 * 128)
    target = (lane // 128) * HEADS + 2 * jnp.arange(pairs)[:, None] + ((lane % 128) // HEADDIM)[None, :]
    pick = (target[:, :, None] == jnp.arange(128)[None, None, :]).astype(bf16)
    by_head = (jnp.arange(ch)[:, None] // HEADDIM == jnp.arange(128)[None, :]).astype(f32)
    return run(
        scan_back_kernel,
        (tokens // Q,),
        [
            s["main"], s["main"], s["main"], s["prev"], s["halo"], s["row8"], s["tile"], s["tile"], s["tile"],
            s["tile"], s["state"], s["row16"], s["small"],
            pl.BlockSpec((2 * Q, 2 * Q), lambda q: (0, 0)), pl.BlockSpec((Q, 2 * Q), lambda q: (0, 0)),
            pl.BlockSpec((pairs, 3 * 128, 128), lambda q: (0, 0, 0)), pl.BlockSpec((ch, 128), lambda q: (0, 0)),
        ],
        [s["main"], s["tile"], s["row8"], s["row24"], s["small"]],
        [
            shape((tokens, ch), bf16), shape((tokens, 128), f32), shape((8, ch), f32), shape((24, ch), f32),
            shape((8, 128), f32),
        ],
        [
            pltpu.VMEM((STATES, ch), f32), pltpu.VMEM((128, Q), f32), pltpu.VMEM((8, ch), f32),
            pltpu.VMEM((Q, ch), bf16), pltpu.VMEM((Q, ch), bf16), pltpu.VMEM((128, ch), f32),
            pltpu.VMEM((128, ch), f32), pltpu.VMEM((Q, 128), f32), pltpu.VMEM((Q, Q), f32),
        ],
        [u, dy, x, x, halo, cw, col, row, e, et, st, de, hp, lower, strict, pick, by_head],
        "scan_backward" + tag,
        cost(tokens * ch * 25000, 12 * tokens * ch),
        load,
    )


def norm_specs(width):
    main = pl.BlockSpec((Q, width), lambda q: (q, 0))
    return main, pl.BlockSpec((width, Q), lambda q: (0, q)), pl.BlockSpec((1, width), lambda q: (0, 0))


def norm_forward(rows, gain_row, name, load=None):
    tokens, width = rows[0].shape
    main, turned, one = norm_specs(width)
    return run(
        norm_kernel,
        (tokens // Q,),
        [main] * len(rows) + [one],
        [main, main, turned],
        [shape((tokens, width), f32), shape((tokens, width), bf16), shape((width, tokens), bf16)],
        [],
        [*rows, gain_row],
        name,
        cost(tokens * width * 20, 12 * tokens * width),
        load,
    )


def norm_back(grads, rows, gain_row, bases, name, load=None):
    tokens, width = rows.shape
    main, turned, one = norm_specs(width)
    high, low, part, high_t = run(
        functools.partial(norm_back_kernel, len(grads)),
        (tokens // Q,),
        [main, one] + [main] * (len(grads) + len(bases)),
        [main, main, pl.BlockSpec((8, width), lambda q: (0, 0)), turned],
        [
            shape((tokens, width), bf16), shape((tokens, width), bf16), shape((8, width), f32),
            shape((width, tokens), bf16),
        ],
        [],
        [rows, gain_row, *grads, *bases],
        name,
        cost(tokens * width * 20, 16 * tokens * width),
        load,
    )
    return high, low, high_t, part[0]


def token_marks(seg, seg_before):
    tokens = seg.shape[0]
    by_block = seg.reshape(tokens // Q, Q)
    before = jnp.concatenate([seg_before[2:3], by_block[:-1, Q - 1]])
    padded = jnp.concatenate([seg_before, seg])
    found = [seg.astype(f32)] + [(padded[3 - k : 3 - k + tokens] == seg).astype(f32) for k in (1, 2, 3)]
    found.append((by_block == before[:, None]).astype(f32).reshape(-1))
    found.append((by_block == by_block[:, Q - 1 :]).astype(f32).reshape(-1))
    lane = jnp.arange(128)[None, :]
    out = jnp.zeros((tokens, 128), f32)
    for i, v in enumerate(found):
        out = jnp.where(lane == SEG + i, v[:, None], out)
    return out


def swap(x, axis, n, mask):
    return lax.ppermute(x, axis, [(i, i ^ mask) for i in range(n)])


def sum_all(x, n, over_tp=False):
    if over_tp:
        x = x + swap(x, "tp", 2, 1)
    bit = 1
    while bit < n:
        x = x + swap(x, "fsdp", n, bit)
        bit *= 2
    return x


def bf_dot(a, b):
    return jnp.dot(a, b, preferred_element_type=f32)


def make_local(n):
    def local(
        layer_in, seg_ids, gain_one, x_weight, z_weight, dt_weight, bc_weight, conv_weight, conv_bias,
        dt_bias, a_log, d_skip, out_weight, gain_two, gate_weight, up_weight, down_weight, cotangent,
    ):
        tokens, width = layer_in.shape
        rows, ch = x_weight.shape
        heads = dt_weight.shape[1]
        states = bc_weight.shape[1] // 2
        me, half = lax.axis_index("fsdp"), lax.axis_index("tp")

        epack = jnp.concatenate([dt_weight, bc_weight, jnp.zeros((rows, EXTRA - heads - 2 * states), bf16)], axis=1)
        X, E = Gather("x", x_weight, n), Gather("e", epack, n)
        Z, O = Gather("z", z_weight, n), Gather("o", out_weight, n)
        G, U, D = Gather("g", gate_weight, n), Gather("u", up_weight, n), Gather("d", down_weight, n)

        rate = -jnp.exp(a_log)
        pad = jnp.zeros((128 - heads,), f32)
        by_head = jnp.stack([jnp.concatenate([dt_bias, pad]), jnp.concatenate([rate, pad])])
        small = jnp.concatenate(
            [
                conv_weight,
                conv_bias[None, :],
                jnp.repeat(d_skip, HEADDIM)[None, :],
                jnp.pad(by_head, ((0, 0), (0, ch - 128))),
            ],
            axis=0,
        )
        smalls = [small, swap(small, "tp", 2, 1)]
        head_rows = [jnp.pad(v[6:8, :128], ((0, 6), (0, 0))) for v in smalls]
        before_rows = lax.ppermute(layer_in[tokens - HALO :], "tp", [(0, 1)])
        seg = lax.dynamic_slice(seg_ids, (half * tokens,), (tokens,))
        seg_before = jnp.where(half == 0, -1, seg_ids[tokens - 3 : tokens])

        part = rows // 2
        place = jnp.arange(2 * n)
        q = n // 4
        p = place % n
        part_at = (me ^ (p // (2 * q) + 2 * ((p // q) % 2) + 4 * (p % q))) * 2 + place // n
        seek = (place // 2) ^ me
        place_of = (place % 2) * n + (seek % 2) * 2 * q + ((seek // 2) % 2) * q + seek // 4
        col_at = (part_at[:, None] * part + jnp.arange(part)[None, :]).reshape(-1)
        turn = (jnp.arange(width)[:, None] == col_at[None, :]).astype(bf16)

        def to_local(v):
            return jnp.take(v.reshape(2 * n, part), part_at, axis=0).reshape(-1)

        def to_global(v):
            return jnp.take(v.reshape(2 * n, part), place_of, axis=0).reshape(-1)

        gain_one, gain_two = to_local(gain_one)[None, :], to_local(gain_two)[None, :]
        (rows_in,) = matmul([[(layer_in, turn)]], f32, 512, "turn_rows", Load(X, E))
        rows_in, normed, normed_t = norm_forward([rows_in], gain_one, "norm_one", Load(X, E, Z))
        cot_low, cot_t = matmul([[(cotangent, turn)]], bf16, 512, "turn_cotangent", Load(X, E, O), turned=True)
        carry_only(Load(X, E, Z), "carry_one")
        halo_rows = bf_dot(before_rows, turn)
        halo_scale = lax.rsqrt(jnp.mean(halo_rows * halo_rows, axis=-1, keepdims=True) + epsilon)
        normed_before = (halo_rows * halo_scale * gain_one).astype(bf16)
        marks = token_marks(seg, seg_before)

        found = matmul(
            [[(normed, w)] for w in X.full], f32, 512, "project_x", Load(Z, O, G), beside=(normed_before, E.full)
        )
        xs, halos, es = found[:2], found[2:4], found[4:]
        saved = []
        for b in (0, 1):
            v = dict(x=xs[b], cw=smalls[b], hp=head_rows[b])
            v["e"], v["halo"] = es[b], halos[b]
            load = Load(Z, O, G, U) if b == 0 else Load(G, O, D)
            v["u"], v["end"], v["col"], v["row"], v["et"] = conv_state(
                v["x"], v["halo"], v["cw"], v["e"], v["hp"], marks, tag=str(b), load=load
            )
            saved.append(v)
        starts = lax.ppermute(jnp.stack([v["end"] for v in saved]), "tp", [(0, 1)])[::-1]
        zs = matmul([[(normed, w)] for w in Z.full], f32, 512, "project_z", Load(G, U, D))
        for b in (0, 1):
            v = saved[b]
            v["z"] = zs[b]
            v["gated"], v["y"], v["states"] = scan_forward(
                v["u"], v["z"], v["col"], v["row"], v["e"], v["et"], starts[b], v["cw"],
                tag=str(b), load=Load(U) if b == 0 else Load(U, D),
            )
        (mixed,) = matmul(
            [[(v["gated"], w) for v, w in zip(saved, O.full)]], f32, 512, "project_out", Load(D), nt=True
        )
        hidden, normed_two, two_t = norm_forward([rows_in, mixed], gain_two, "norm_two")

        acts, gate_grads, up_grads = feed_forward(normed_two, cot_low, G.full, U.full, D.full)
        def halves(key, grads):
            return [Scatter(key, grads, n, i, 2) for i in (0, 1)]

        da, db = halves("d", matmul([[(cot_t, a)] for a in acts], bf16, 512, "down_grad"))
        ga, gb = halves("g", matmul([[(two_t, a)] for a in gate_grads], bf16, 512, "gate_grad", Load(da, db)))
        ua, ub = halves("u", matmul([[(two_t, a)] for a in up_grads], bf16, 512, "up_grad", Load(da, ga, gb)))
        (fed,) = matmul([list(zip(acts, D.full))], f32, 512, "project_down", Load(db, da, ua, ub), nt=True)
        out_low = (hidden + fed).astype(bf16)
        (grad_two,) = matmul(
            [list(zip(gate_grads, G.full)) + list(zip(up_grads, U.full))], f32, 256, "two_back",
            Load(ga, gb, db, da), nt=True,
        )
        mixed_grad, mixed_low, mixed_t, gain_two_part = norm_back(
            [grad_two], hidden, gain_two, [cot_low], "norm_two_back", Load(ga, db)
        )

        so = Scatter("o", matmul([[(mixed_t, v["gated"])] for v in saved], bf16, 512, "out_grad", Load(ua, ga)), n)
        gg = matmul([[(mixed_grad, w)] for w in O.full], f32, 512, "gated_back", Load(gb, so))
        for b in (0, 1):
            v = saved[b]
            v["dy"], v["dz"], v["ds"] = gate_backward(
                gg[b], v["z"], v["y"], v["col"], v["et"], tag=str(b), load=Load(ua, gb) if b == 0 else None
            )
        ends = lax.ppermute(jnp.stack([v["ds"] for v in saved]), "tp", [(1, 0)])[::-1]
        sz = Scatter("z", matmul([[(normed_t, v["dz"])] for v in saved], bf16, 512, "z_grad", Load(ua)), n)

        def back(b, load):
            v = saved[b]
            v["dx"], v["de"], v["cg"], v["edge"], v["hg"] = scan_backward(
                v["u"], v["dy"], v["x"], v["halo"], v["cw"], v["col"], v["row"], v["e"], v["et"], v["states"],
                ends[b], v["hp"], tag=str(b), load=load,
            )
            cw, edge = v["cw"], v["edge"].reshape(3, 8, ch)
            fix = [jnp.zeros((HALO - 3, ch), f32)]
            for j in (3, 2, 1):
                fix.append(sum(cw[k : k + 1] * edge[k - 1, k - j : k - j + 1] for k in range(j, 4)))
            v["fix"] = jnp.concatenate(fix, axis=0)

        def x_gradient(b, load):
            v = saved[b]
            return matmul(
                [[(normed_t, v["dx"]), (before_t, v["fix"].astype(bf16))]], bf16, 512, f"x_grad{b}", load
            )[0]

        before_t = normed_before.T
        back(1, Load(so, ub, sz))
        sx = LateScatter("x", n, x_gradient(1, Load(so)))
        (grad_z,) = matmul(
            [[(v["dz"], w) for v, w in zip(saved, Z.full)]], f32, 512, "z_back", Load(sx, ub), nt=True
        )
        back(0, Load(sz, sx, so, ub))
        sx.given(x_gradient(0, Load(sz)))
        fixes = lax.ppermute(jnp.stack([v["fix"] for v in saved]), "tp", [(1, 0)])[::-1]
        own, other = ([v["cg"][:6].reshape(-1), v["hg"][:2].reshape(-1)] for v in saved)
        gain_two_part = to_global(gain_two_part)
        own, other = jnp.concatenate(own + [gain_two_part]), jnp.concatenate(other + [gain_two_part])
        total = sum_all(own + swap(other, "tp", 2, 1), n)
        cg, hg = total[: 6 * ch].reshape(6, ch), total[6 * ch : 6 * ch + 256].reshape(2, 128)
        gain_two_total = total[6 * ch + 256 :]

        shared = 0.5 * (saved[0]["de"] + saved[1]["de"])
        own_lane = jnp.arange(EXTRA)[None, :] < heads
        for b in (0, 1):
            v = saved[b]
            last = v["dx"][tokens - HALO :].astype(f32) + fixes[b]
            v["dx"] = lax.dynamic_update_slice(v["dx"], last.astype(bf16), (tokens - HALO, 0))
            v["de"] = jnp.where(own_lane, v["de"], shared).astype(bf16)
        se = Scatter("e", matmul([[(normed_t, v["de"])] for v in saved], bf16, 128, "e_grad"), n)
        pairs = [(v["dx"], w) for v, w in zip(saved, X.full)] + [(v["de"], w) for v, w in zip(saved, E.full)]
        (grad_x,) = matmul([pairs], f32, 512, "x_back", Load(sx, se, sz), nt=True)
        high, low, _, gain_one_part = norm_back(
            [grad_x, grad_z], rows_in, gain_one, [mixed_grad, mixed_low], "norm_one_back", Load(se)
        )
        (layer_out,) = matmul([[(out_low, turn)]], bf16, 512, "turn_out", Load(sx, se), nt=True)
        (input_grad,) = matmul([[(high, turn), (low, turn)]], f32, 512, "turn_back", Load(sx, se), nt=True)

        gain_one_total = sum_all(to_global(gain_one_part), n, True)
        dt_b_total, a_total = hg[0, :heads], hg[1, :heads]
        skip_total = jnp.sum(cg[5].reshape(heads, HEADDIM), axis=1)
        return (
            layer_out,
            input_grad,
            gain_one_total,
            sx.out,
            sz.out,
            se.out[:, :heads],
            2.0 * se.out[:, heads : heads + 2 * states],
            cg[:4],
            cg[4],
            dt_b_total,
            a_total,
            skip_total,
            so.out,
            gain_two_total,
            jnp.concatenate([ga.out, gb.out], axis=1),
            jnp.concatenate([ua.out, ub.out], axis=1),
            jnp.concatenate([da.out, db.out], axis=1),
        )

    return local


def solution(mesh):
    rows = P(("fsdp", "tp"), None)
    weight = P("fsdp", "tp")
    in_specs = (
        rows, P("fsdp"), P(), weight, weight, weight, P("fsdp", None), P(None, "tp"), P("tp"), P("tp"), P("tp"),
        P("tp"), weight, P(), weight, weight, weight, rows,
    )
    out_specs = (
        rows, rows, P(), weight, weight, weight, P("fsdp", None), P(None, "tp"), P("tp"), P("tp"), P("tp"), P("tp"),
        weight, P(), weight, weight, weight,
    )
    return jax.shard_map(
        make_local(mesh.shape["fsdp"]), mesh=mesh, in_specs=in_specs, out_specs=out_specs, check_vma=False
    )
```

```python
import functools

import jax
import jax.numpy as jnp
from jax import lax
from jax.experimental import pallas as pl
from jax.experimental.pallas import tpu as pltpu
from jax.sharding import PartitionSpec as P

HEADDIM = 64
HEADS = 24
STATES = 16
Q = 128
HALO = 16
EXTRA = 128
RUN, DT, DEC, TAIL, SEG, CONT, LAST, LOGDT = 0, 24, 48, 72, 96, 100, 101, 104
COLB, COLC = HEADS, HEADS + STATES

f32 = jnp.float32
bf16 = jnp.bfloat16
highest = lax.Precision.HIGHEST
epsilon = 1e-05
NEG = -1e30


def dot(a, b, precision=None):
    return jnp.dot(a, b, preferred_element_type=f32, precision=precision)


def dot_t(a, b):
    return lax.dot_general(a, b, (((1,), (1,)), ((), ())), preferred_element_type=f32)


def split(v):
    high = v.astype(bf16)
    return high, (v - high.astype(f32)).astype(bf16)


def wide_left(v):
    high, low = split(v)
    return jnp.concatenate([high, low, high], axis=1)


def stack_right(v):
    high, low = split(v)
    return jnp.concatenate([high, high, low], axis=0)


def sigmoid(v):
    return 0.5 * jnp.tanh(0.5 * v) + 0.5


def lanes_of(rows=Q):
    return lax.broadcasted_iota(jnp.int32, (rows, 128), 1)


def pair_cols(col, first, j, left):
    a = col[:, first + 2 * j : first + 2 * j + 1]
    b = col[:, first + 2 * j + 1 : first + 2 * j + 2]
    return jnp.where(left, a, b)


def triangle(strict=False, transposed=False):
    i = lax.broadcasted_iota(jnp.int32, (Q, Q), 1 if transposed else 0)
    k = lax.broadcasted_iota(jnp.int32, (Q, Q), 0 if transposed else 1)
    return (i > k) if strict else (i >= k)


def spread_marks(col):
    return [jnp.broadcast_to(col[:, SEG + k : SEG + k + 1], (Q, 128)) for k in (1, 2, 3)]


def conv_rows(x_ref, xp_ref, halo_ref, cw_ref, marks, q, lanes):
    x = x_ref[:, lanes]
    prev = jnp.where(q == 0, halo_ref[:, lanes], xp_ref[:, lanes])
    cat = jnp.concatenate([prev, x], axis=0)
    acc = cw_ref[4:5, lanes] + cw_ref[0:1, lanes] * x
    shifted = []
    for k in (1, 2, 3):
        back = pltpu.roll(cat, k, 0)[HALO:, :] * marks[k - 1]
        shifted.append(back)
        acc = acc + cw_ref[k : k + 1, lanes] * back
    return x, shifted, acc


def conv_state_kernel(
    x_ref, xp_ref, halo_ref, cw_ref, e_ref, hp_ref, mark_ref, u_ref, end_ref, col_ref, row_ref, et_ref
):
    q = pl.program_id(0)

    @pl.when(q == 0)
    def _():
        end_ref[...] = jnp.zeros_like(end_ref)

    e, marks = e_ref[...], mark_ref[...]
    lane = lanes_of()
    head = lane < HEADS
    raw = e + hp_ref[0:1, :]
    dt = jnp.where(head, jnp.maximum(raw, 0.0) + jnp.log1p(jnp.exp(-jnp.abs(raw))), 0.0)
    run = dot(jnp.where(triangle(), 1.0, 0.0), dt * hp_ref[1:2, :], highest)
    dec = jnp.where(head, jnp.exp(run) * marks[:, CONT : CONT + 1], 0.0)
    tail = jnp.where(head, jnp.exp(run[Q - 1 : Q, :] - run) * marks[:, LAST : LAST + 1], 0.0)
    log_dt = jnp.where(head, jnp.log(dt), 0.0)
    col = (
        run
        + pltpu.roll(dt, DT, 1)
        + pltpu.roll(dec, DEC, 1)
        + pltpu.roll(tail, TAIL, 1)
        + marks
        + pltpu.roll(log_dt, LOGDT, 1)
    )
    col_ref[...] = col
    row_ref[...] = col.T
    et = e.T
    et_ref[...] = et
    bt = wide_left(et[COLB:COLC, :])
    left = lane < HEADDIM
    spread = spread_marks(col)
    for j in range(x_ref.shape[1] // 128):
        lanes = slice(128 * j, 128 * j + 128)
        _, _, acc = conv_rows(x_ref, xp_ref, halo_ref, cw_ref, spread, q, lanes)
        u = acc * sigmoid(acc)
        u_ref[:, lanes] = u
        scaled = u * (pair_cols(col, DT, j, left) * pair_cols(col, TAIL, j, left))
        keep = pair_cols(col[Q - 1 : Q, :], DEC, j, left[:1])
        end_ref[:, lanes] = keep * end_ref[:, lanes] + dot(bt, stack_right(scaled))


def scan_kernel(
    u_ref, z_ref, col_ref, row_ref, e_ref, et_ref, s0_ref, cw_ref, gated_ref, y_ref, st_ref, S
):
    @pl.when(pl.program_id(0) == 0)
    def _():
        S[...] = s0_ref[...]

    col, row = col_ref[...], row_ref[...]
    left = lanes_of() < HEADDIM
    c = e_ref[:, COLC : COLC + STATES]
    bt = et_ref[COLB:COLC, :]
    scores = dot(c, bt, highest)
    neg = jnp.where((col[:, SEG : SEG + 1] == row[SEG : SEG + 1, :]) & triangle(), 0.0, NEG)
    c, bt = wide_left(c), wide_left(bt)
    for j in range(u_ref.shape[1] // 128):
        lanes = slice(128 * j, 128 * j + 128)
        uf = u_ref[:, lanes]
        u, u_low = split(uf)
        state = S[:, lanes]
        st_ref[:, lanes] = state
        parts, rest = [], []
        for h in (2 * j, 2 * j + 1):
            gap = col[:, h : h + 1] - (row[h : h + 1, :] - row[LOGDT + h : LOGDT + h + 1, :])
            high, low = split(jnp.exp(gap + neg) * scores)
            parts.append(high)
            rest.append(low)
        zero = jnp.zeros_like(u)
        both = [jnp.where(left, u, zero), jnp.where(left, zero, u)]
        both_low = [jnp.where(left, u_low, zero), jnp.where(left, zero, u_low)]
        y = dot(jnp.concatenate(parts + rest + parts, axis=1), jnp.concatenate(both + both + both_low, axis=0))
        y = y + dot(c, stack_right(state)) * pair_cols(col, DEC, j, left) + cw_ref[5:6, lanes] * uf
        z = z_ref[:, lanes]
        y_ref[:, lanes] = y
        gated_ref[:, lanes] = (y * (z * sigmoid(z))).astype(bf16)
        scaled = uf * (pair_cols(col, DT, j, left) * pair_cols(col, TAIL, j, left))
        keep = pair_cols(col[Q - 1 : Q, :], DEC, j, left[:1])
        S[:, lanes] = keep * state + dot(bt, stack_right(scaled))


def gate_back_kernel(gg_ref, z_ref, y_ref, col_ref, et_ref, dy_ref, dz_ref, ds_ref):
    @pl.when(pl.program_id(0) == 0)
    def _():
        ds_ref[...] = jnp.zeros_like(ds_ref)

    col = col_ref[...]
    left = lanes_of() < HEADDIM
    ct = et_ref[COLC : COLC + STATES, :].astype(bf16)
    for j in range(z_ref.shape[1] // 128):
        lanes = slice(128 * j, 128 * j + 128)
        z = z_ref[:, lanes]
        gg = gg_ref[:, lanes]
        sig = sigmoid(z)
        dy = gg * (z * sig)
        dy_ref[:, lanes] = dy
        dz_ref[:, lanes] = (gg * y_ref[:, lanes] * (sig * (1.0 + z * (1.0 - sig)))).astype(bf16)
        scaled = (dy * pair_cols(col, DEC, j, left)).astype(bf16)
        keep = pair_cols(col[Q - 1 : Q, :], DEC, j, left[:1])
        ds_ref[:, lanes] = keep * ds_ref[:, lanes] + dot(ct, scaled)


def scan_back_kernel(
    u_ref, dy_ref, x_ref, xp_ref, halo_ref, cw_ref, col_ref, row_ref, e_ref, et_ref, st_ref, de_ref, hp_ref,
    lw_ref, sm_ref, pick_ref, head_ref,
    dx_ref, de_out_ref, cg_ref, edge_ref, hg_ref,
    D, WA, CONST, TAILS, DECS, DS, ST, SUMS, DG,
):
    step = pl.program_id(0)
    q = pl.num_programs(0) - 1 - step

    @pl.when(step == 0)
    def _():
        D[...] = de_ref[...]
        cg_ref[...] = jnp.zeros_like(cg_ref)
        edge_ref[...] = jnp.zeros_like(edge_ref)
        hg_ref[...] = jnp.zeros_like(hg_ref)
        WA[...] = jnp.zeros_like(WA)
        CONST[...] = jnp.zeros_like(CONST)
        DS[...] = jnp.zeros_like(DS)
        ST[...] = jnp.zeros_like(ST)

    col, row = col_ref[...], row_ref[...]
    lane = lanes_of()
    left = lane < HEADDIM
    e = e_ref[...]
    b, ct = e[:, COLB:COLC], et_ref[COLC : COLC + STATES, :]
    scores = dot(b, ct, highest)
    neg = jnp.where((col[:, SEG : SEG + 1] == row[SEG : SEG + 1, :]) & triangle(transposed=True), 0.0, NEG)
    b, ct, c = wide_left(b), ct.astype(bf16), wide_left(e[:, COLC : COLC + STATES])
    spread = spread_marks(col)
    DG[...] = jnp.zeros_like(DG)
    SUMS[...] = jnp.zeros_like(SUMS)
    for j in range(u_ref.shape[1] // 128):
        lanes = slice(128 * j, 128 * j + 128)
        u = u_ref[:, lanes]
        dyf = dy_ref[:, lanes]
        dy = dyf.astype(bf16)
        dt = pair_cols(col, DT, j, left)
        dec = pair_cols(col, DEC, j, left)
        tail = pair_cols(col, TAIL, j, left)
        keep = pair_cols(col[Q - 1 : Q, :], DEC, j, left[:1])
        state, grad_state = st_ref[:, lanes], D[:, lanes]
        DS[COLB:COLC, lanes] = grad_state
        ST[COLC : COLC + STATES, lanes] = state
        xs = u * dt
        zero = jnp.zeros_like(dy)
        both = jnp.concatenate([jnp.where(left, dy, zero), jnp.where(left, zero, dy)], axis=0)
        d_mat = dot_t(xs.astype(bf16), both)
        mats, pairs, d_scores = [], [], None
        for i, h in enumerate((2 * j, 2 * j + 1)):
            decay = jnp.exp((row[h : h + 1, :] - col[:, h : h + 1]) + neg)
            mat = decay * scores
            dm = d_mat[:, Q * i : Q * i + Q]
            d_scores = decay * dm if d_scores is None else d_scores + decay * dm
            mats.append(mat.astype(bf16))
            pairs.append((mat * dm).astype(bf16))
        DG[...] += d_scores
        dxs = dot(jnp.concatenate(mats, axis=1), both)
        spans = dot(jnp.concatenate(pairs, axis=1), lw_ref[...]) * sm_ref[...]
        sums = jnp.sum(spans, axis=0, keepdims=True)
        WA[2 * j : 2 * j + 1, :] = sums[:, :Q]
        WA[2 * j + 1 : 2 * j + 2, :] = sums[:, Q:]
        from_tail = tail * dot(b, stack_right(grad_state))
        dxs = dxs + from_tail
        ydec = dyf * dec
        found = [u * dxs, ydec * dot(c, stack_right(state)), xs * from_tail]
        SUMS[...] += dot(jnp.concatenate([v.astype(bf16) for v in found], axis=1), pick_ref[j])
        TAILS[:, lanes] = (xs * tail).astype(bf16)
        low_dec = ydec.astype(bf16)
        DECS[:, lanes] = low_dec
        CONST[0:1, lanes] = keep * jnp.sum(state * grad_state, axis=0, keepdims=True)
        D[:, lanes] = keep * grad_state + dot(ct, low_dec)

        x, shifted, acc = conv_rows(x_ref, xp_ref, halo_ref, cw_ref, spread, q, lanes)
        sig = sigmoid(acc)
        dconv = (dxs * dt + cw_ref[5:6, lanes] * dyf) * (sig * (1.0 + acc * (1.0 - sig)))
        dx = cw_ref[0:1, lanes] * dconv
        cg_ref[0:1, lanes] += jnp.sum(dconv * x, axis=0, keepdims=True)
        for k in (1, 2, 3):
            masked = dconv * spread[k - 1]
            after = edge_ref[8 * (k - 1) : 8 * k, lanes]
            cat = jnp.concatenate([masked, after], axis=0)
            dx = dx + cw_ref[k : k + 1, lanes] * pltpu.roll(cat, Q + 8 - k, 0)[:Q, :]
            edge_ref[8 * (k - 1) : 8 * k, lanes] = masked[:8, :]
            cg_ref[k : k + 1, lanes] += jnp.sum(dconv * shifted[k - 1], axis=0, keepdims=True)
        cg_ref[4:5, lanes] += jnp.sum(dconv, axis=0, keepdims=True)
        cg_ref[5:6, lanes] += jnp.sum(dyf * u, axis=0, keepdims=True)
        dx_ref[:, lanes] = dx.astype(bf16)

    head = lane < HEADS
    found = SUMS[...]
    suffix = jnp.where(triangle(transposed=True), 1.0, 0.0)
    prefix = jnp.where(triangle(strict=True), 1.0, 0.0)
    d_step = (
        WA[...].T
        + dot(suffix, pltpu.roll(found, 128 - HEADS, 1), highest)
        + dot(prefix, pltpu.roll(found, 128 - 2 * HEADS, 1), highest)
        + dot(CONST[...], head_ref[...], highest)[0:1, :]
    )
    d_dt = d_step * hp_ref[1:2, :] + found
    d_raw = jnp.where(head, d_dt * sigmoid(e + hp_ref[0:1, :]), 0.0)
    step_dt = jnp.where(head, pltpu.roll(col, 128 - DT, 1), 0.0)
    hg_ref[0:1, :] += jnp.sum(d_raw, axis=0, keepdims=True)
    hg_ref[1:2, :] += jnp.sum(jnp.where(head, d_step, 0.0) * step_dt, axis=0, keepdims=True) * hp_ref[1:2, :]
    total = DG[...]
    b_part = jnp.where((lane >= COLB) & (lane < COLC), e, 0.0)
    c_part = jnp.where((lane >= COLC) & (lane < COLC + STATES), e, 0.0)
    de_out_ref[...] = (
        d_raw
        + dot_t(TAILS[...], DS[...].astype(bf16))
        + dot_t(DECS[...], ST[...].astype(bf16))
        + dot(total, pltpu.roll(c_part, 128 - STATES, 1), highest)
        + dot(total.T, pltpu.roll(b_part, STATES, 1), highest)
    )


def norm_kernel(*refs):
    *row_refs, gain_ref, hidden_ref, out_ref, turned_ref = refs
    rows = row_refs[0][...]
    for r in row_refs[1:]:
        rows = rows + r[...]
    hidden_ref[...] = rows
    scale = lax.rsqrt(jnp.mean(rows * rows, axis=-1, keepdims=True) + epsilon)
    normed = rows * scale * gain_ref[...]
    out_ref[...] = normed.astype(bf16)
    turned_ref[...] = normed.T.astype(bf16)


def norm_back_kernel(n_grads, n_given, rows_ref, gain_ref, *refs):
    given, (high_ref, low_ref, part_ref), turned_refs = refs[:n_given], refs[n_given : n_given + 3], refs[n_given + 3 :]

    @pl.when(pl.program_id(0) == 0)
    def _():
        part_ref[...] = jnp.zeros_like(part_ref)

    rows, grad = rows_ref[...], given[0][...]
    for r in given[1:n_grads]:
        grad = grad + r[...]
    scale = lax.rsqrt(jnp.mean(rows * rows, axis=-1, keepdims=True) + epsilon)
    unit = rows * scale
    part_ref[0:1, :] += jnp.sum(grad * unit, axis=0, keepdims=True)
    unit_grad = grad * gain_ref[...]
    total = scale * (unit_grad - unit * jnp.mean(unit_grad * unit, axis=-1, keepdims=True))
    for r in given[n_grads:]:
        total = total + r[...].astype(f32)
    high = total.astype(bf16)
    high_ref[...] = high
    low_ref[...] = (total - high.astype(f32)).astype(bf16)
    for r in turned_refs:
        r[...] = total.T.astype(bf16)


def flip(i, mask):
    bit = 1
    while bit <= mask:
        if mask & bit:
            i = i + bit * (1 - 2 * ((i // bit) % 2))
        bit *= 2
    return i


class Load:
    def __init__(self, *movers):
        self.reads, self.updates, self.news, self.copies = {}, {}, {}, []
        self.movers = movers
        for mover in movers:
            reads, updates, news, copies = mover.moves()
            self.reads.update(reads)
            self.updates.update(updates)
            self.news.update(news)
            self.copies += copies

    def arrive(self, got):
        for mover in self.movers:
            mover.take(got)


IDS = {}


def run(body, grid, in_specs, out_specs, out_shape, scratch, args, name, estimate=None, load=None, vmem=56):
    params = dict(dimension_semantics=("arbitrary",) * len(grid), vmem_limit_bytes=vmem * 1024 * 1024)
    if load is None:
        return pl.pallas_call(
            body, name=name, grid=grid, in_specs=in_specs, out_specs=out_specs, out_shape=out_shape,
            scratch_shapes=scratch, compiler_params=pltpu.CompilerParams(**params), cost_estimate=estimate,
        )(*args)
    cid = IDS.setdefault(name, len(IDS) + 1)
    reads, updates, news = list(load.reads), list(load.updates), list(load.news)
    n_in, n_out, n_scratch, n_copies = len(args), len(out_shape), len(scratch), len(load.copies)
    routes = []
    for c in load.copies:
        if c[4] is not None and c[4] not in routes:
            routes.append(c[4])

    def kernel(*refs):
        ins, rest = refs[:n_in], refs[n_in:]
        held = dict(zip(reads, rest))
        rest = rest[len(reads) + len(updates) :]
        outs, rest = rest[:n_out], rest[n_out:]
        held.update(zip(updates + news, rest))
        rest = rest[len(updates) + len(news) :]
        mine, (send, recv) = rest[:n_scratch], rest[n_scratch:]

        def device(route):
            return {axis: flip(lax.axis_index(axis), mask) for axis, mask in zip(route[::2], route[1::2])}

        def make(i, c):
            src, dst = held[c[0]].at[c[1]], held[c[2]].at[c[3]]
            if c[4] is None:
                return pltpu.make_async_copy(src, dst, recv.at[i])
            return pltpu.make_async_remote_copy(
                src_ref=src, dst_ref=dst, send_sem=send.at[i], recv_sem=recv.at[i],
                device_id=device(c[4]), device_id_type=pl.DeviceIdType.MESH,
            )

        first, last = pl.program_id(0) == 0, pl.program_id(0) == grid[0] - 1
        for axis in range(1, len(grid)):
            first = first & (pl.program_id(axis) == 0)
            last = last & (pl.program_id(axis) == grid[axis] - 1)

        @pl.when(first)
        def _():
            barrier = pltpu.get_barrier_semaphore()
            for route in routes:
                pl.semaphore_signal(
                    barrier, inc=1, device_id=device(route), device_id_type=pl.DeviceIdType.MESH
                )
            pl.semaphore_wait(barrier, len(routes))
            for i, c in enumerate(load.copies):
                make(i, c).start()

        if body is not None:
            body(*ins, *outs, *mine)

        @pl.when(last)
        def _():
            for i, c in enumerate(load.copies):
                make(i, c).wait()

    hbm = pl.BlockSpec(memory_space=pltpu.HBM)
    result = pl.pallas_call(
        kernel,
        name=name,
        grid=grid,
        in_specs=list(in_specs) + [hbm] * (len(reads) + len(updates)),
        out_specs=list(out_specs) + [hbm] * (len(updates) + len(news)),
        out_shape=list(out_shape)
        + [jax.ShapeDtypeStruct(load.updates[k].shape, load.updates[k].dtype) for k in updates]
        + [load.news[k] for k in news],
        scratch_shapes=list(scratch) + [pltpu.SemaphoreType.DMA((n_copies,)), pltpu.SemaphoreType.DMA((n_copies,))],
        input_output_aliases={n_in + len(reads) + i: n_out + i for i in range(len(updates))},
        compiler_params=pltpu.CompilerParams(collective_id=cid, has_side_effects=True, **params),
        cost_estimate=estimate,
    )(*args, *[load.reads[k] for k in reads], *[load.updates[k] for k in updates])
    load.arrive(dict(zip(updates + news, result[n_out:])))
    return result[:n_out]


def matmul(jobs, dtype, tile, name, load=None, nt=False, turned=False, beside=None):
    n_jobs, n_pairs = len(jobs), len(jobs[0])
    rows = jobs[0][0][0].shape[0]
    columns = jobs[0][0][1].shape[0 if nt else 1]
    tiles = columns // tile

    def at(job):
        def place(j, t):
            return jnp.where(j == job, t, jnp.where(j < job, 0, tiles - 1))

        return place

    args, in_specs = [], []
    for job, pairs in enumerate(jobs):
        for left, right in pairs:
            args += [left, right]
            k = left.shape[1]
            in_specs.append(pl.BlockSpec((rows, k), lambda j, t: (0, 0), pipeline_mode=pl.Buffered(1)))
            if nt:
                in_specs.append(pl.BlockSpec((tile, k), lambda j, t, p=at(job): (p(j, t), 0)))
            else:
                in_specs.append(pl.BlockSpec((k, tile), lambda j, t, p=at(job): (0, p(j, t))))
    out_specs = [pl.BlockSpec((rows, tile), lambda j, t, p=at(job): (0, p(j, t))) for job in range(n_jobs)]
    out_shape = [jax.ShapeDtypeStruct((rows, columns), dtype)] * n_jobs
    if turned:
        out_specs += [pl.BlockSpec((tile, rows), lambda j, t, p=at(job): (p(j, t), 0)) for job in range(n_jobs)]
        out_shape += [jax.ShapeDtypeStruct((columns, rows), dtype)] * n_jobs
    if beside:
        few, narrow = beside
        args += [few, *narrow]
        in_specs += [pl.BlockSpec(v.shape, lambda j, t: (0, 0), pipeline_mode=pl.Buffered(1)) for v in (few, *narrow)]
        out_specs += [pl.BlockSpec((few.shape[0], tile), lambda j, t, p=at(job): (0, p(j, t))) for job in range(n_jobs)]
        out_shape += [jax.ShapeDtypeStruct((few.shape[0], columns), dtype)] * n_jobs
        out_specs += [pl.BlockSpec((rows, v.shape[1]), lambda j, t: (0, 0)) for v in narrow]
        out_shape += [jax.ShapeDtypeStruct((rows, v.shape[1]), dtype) for v in narrow]
    n_in = len(args)

    def body(*refs):
        ins, outs = refs[:n_in], refs[n_in:]
        for job in range(n_jobs):

            @pl.when(pl.program_id(0) == job)
            def _(job=job):
                total = None
                for p in range(n_pairs):
                    left, right = ins[2 * (job * n_pairs + p)], ins[2 * (job * n_pairs + p) + 1]
                    term = (dot_t if nt else dot)(left[...], right[...])
                    total = term if total is None else total + term
                outs[job][...] = total.astype(dtype)
                if turned:
                    outs[n_jobs + job][...] = total.T.astype(dtype)
                if beside:
                    left, right, few = ins[2 * job * n_pairs], ins[2 * job * n_pairs + 1], ins[2 * n_jobs * n_pairs]
                    outs[n_jobs + job][...] = dot(few[...], right[...]).astype(dtype)

                    @pl.when(pl.program_id(1) == 0)
                    def _():
                        narrow = ins[2 * n_jobs * n_pairs + 1 + job]
                        outs[2 * n_jobs + job][...] = dot(left[...], narrow[...]).astype(dtype)

    depth = sum(p[0].shape[1] for p in jobs[0])
    return run(
        body, (n_jobs, tiles), in_specs, out_specs, out_shape, [], args, name,
        pl.CostEstimate(
            flops=2 * n_jobs * rows * columns * depth, bytes_accessed=4 * n_jobs * rows * columns, transcendentals=0
        ),
        load,
    )


class LateScatter:
    def __init__(self, key, n, other):
        self.key, self.n, self.phase = key, n, 0
        self.given(other)

    def given(self, grad):
        self.rows, self.cols = grad.shape[0] // self.n, grad.shape[1]
        self.now = grad.reshape(2, self.n, self.rows // 2, self.cols)

    def moves(self):
        k, q, v = self.key, self.n // 4, self.now
        far, rest = slice(q, 2 * q), slice(2 * q, 4 * q)

        def new(*dims):
            return jax.ShapeDtypeStruct(dims + (self.rows // 2, self.cols), bf16)

        core = [(k + "v", (i, rest), k + "r", (i,), ("fsdp", 1)) for i in (0, 1)]
        if self.phase == 0:
            return {k + "v": v}, {}, {k + "r": new(2, 2 * q)}, core
        if self.phase == 1:
            copies = [(k + "v", (0, far), k + "r", ALL, ("fsdp", 2)), (k + "v", (1,), k + "s", ALL, ("tp", 1))]
            return {k + "v": v}, {}, {k + "r": new(q), k + "s": new(2 * q)}, copies
        if self.phase == 2:
            copies = core + [(k + "a", ALL, k + "s", ALL, ("tp", 1))]
            return {k + "v": v, k + "a": self.other}, {}, {k + "r": new(2, 2 * q), k + "s": new(q)}, copies
        if self.phase == 3:
            copies = [(k + "v", (far,), k + "r", ALL, ("fsdp", 2)), (k + "a", (far,), k + "s", ALL, ("fsdp", 2))]
            return {k + "v": v[0], k + "a": v[1]}, {}, {k + "r": new(q), k + "s": new(q)}, copies
        news = {f"{k}r{m}": new(2) for m in range(1, q)}
        copies = [(f"{k}v{i}", (m,), f"{k}r{m}", (i,), ("fsdp", m << 2)) for m in range(1, q) for i in (0, 1)]
        return {k + "v0": v[0], k + "v1": v[1]}, {}, news, copies

    def take(self, got):
        k, q, v = self.key, self.n // 4, self.now
        if self.phase == 0:
            self.now = low_sum(v[:, : 2 * q], got[k + "r"])
        elif self.phase == 1:
            self.other, self.lower = low_sum(v[0, :q], got[k + "r"]), got[k + "s"]
        elif self.phase == 2:
            own = [v[i, : 2 * q].astype(f32) + got[k + "r"][i].astype(f32) for i in (0, 1)]
            self.now = [own[0].astype(bf16), (own[1] + self.lower.astype(f32)).astype(bf16)]
            self.other = got[k + "s"]
        elif self.phase == 3:
            upper = v[0][:q].astype(f32) + got[k + "r"].astype(f32) + self.other.astype(f32)
            self.now = [upper.astype(bf16), low_sum(v[1][:q], got[k + "s"])]
        else:
            total = jnp.stack([v[0][0], v[1][0]]).astype(f32)
            for m in range(1, q):
                total = total + got[f"{k}r{m}"].astype(f32)
            self.out = total.reshape(self.rows, self.cols)
        self.phase += 1


class SumAll:
    def __init__(self, key, own, other, n):
        self.key, self.n, self.phase, self.size = key, n, 0, own.shape[0]
        rows = -(-self.size // 1024) * 8
        self.own, self.other = (jnp.pad(v, (0, rows * 128 - self.size)).reshape(rows, 128) for v in (own, other))

    def moves(self):
        k = self.key
        new = jax.ShapeDtypeStruct(self.own.shape, f32)
        if self.phase == 0:
            reads = {k + "v": self.own, k + "w": self.other}
            steps = [(m % 4, m // 4) for m in range(1, 8)]
            routes = [(("fsdp", f) if f else ()) + (("tp", t) if t else ()) for f, t in steps]
            sources = [k + ("w" if t else "v") for f, t in steps]
        else:
            reads, routes = {k + "v": self.own}, [("fsdp", m << 2) for m in range(1, self.n // 4)]
            sources = [k + "v"] * len(routes)
        names = [f"{k}r{i}" for i in range(len(routes))]
        copies = [(a, ALL, b, ALL, c) for a, b, c in zip(sources, names, routes)]
        return reads, {}, {b: new for b in names}, copies

    def take(self, got):
        count = 8 if self.phase == 0 else self.n // 4
        terms = [self.own] + [got[f"{self.key}r{i}"] for i in range(count - 1)]
        while len(terms) > 1:
            terms = [a + b for a, b in zip(terms[::2], terms[1::2])]
        self.own = terms[0]
        self.phase += 1
        self.out = self.own.reshape(-1)[: self.size]


def feed_forward(normed, cot, gate_w, up_w, down_w):
    tokens, width = normed.shape
    cols, tile, step = gate_w[0].shape[1], 512, 256
    tiles = cols // tile

    def at(job):
        def place(j, t):
            return jnp.where(j == job, t, jnp.where(j < job, 0, tiles - 1))

        return place

    whole = pl.BlockSpec((tokens, width), lambda j, t: (0, 0), pipeline_mode=pl.Buffered(1))
    args, in_specs, out_specs = [normed, cot], [whole, whole], []
    for b in (0, 1):
        args += [gate_w[b], up_w[b], down_w[b]]
        in_specs += [pl.BlockSpec((width, tile), lambda j, t, p=at(b): (0, p(j, t)))] * 3
        out_specs += [pl.BlockSpec((tokens, tile), lambda j, t, p=at(b): (0, p(j, t)))] * 3

    def body(n_ref, c_ref, *refs):
        for b in (0, 1):
            wg, wu, wd = refs[3 * b : 3 * b + 3]
            act, gg, ug = refs[6 + 3 * b : 9 + 3 * b]

            @pl.when(pl.program_id(0) == b)
            def _(wg=wg, wu=wu, wd=wd, act=act, gg=gg, ug=ug):
                for i in range(tokens // step):
                    rows = slice(step * i, step * i + step)
                    gate, up, back = dot(n_ref[rows, :], wg[...]), dot(n_ref[rows, :], wu[...]), dot(c_ref[rows, :], wd[...])
                    sig = sigmoid(gate)
                    silu = gate * sig
                    act[rows, :] = (silu * up).astype(bf16)
                    gg[rows, :] = (back * up * sig * (1.0 + gate * (1.0 - sig))).astype(bf16)
                    ug[rows, :] = (back * silu).astype(bf16)

    out = run(
        body, (2, tiles), in_specs, out_specs, [jax.ShapeDtypeStruct((tokens, cols), bf16)] * 6, [], args,
        "feed_forward", pl.CostEstimate(flops=12 * tokens * cols * width, bytes_accessed=12 * tokens * cols, transcendentals=0),
    )
    return [out[0], out[3]], [out[1], out[4]], [out[2], out[5]]


def carry_only(load, name):
    run(None, (1,), [], [], [], [], [], name, None, load)


ALL = (slice(None),)


def low_sum(a, b):
    return a + b


class Gather:
    def __init__(self, key, shard, n):
        rows, cols = shard.shape
        self.n, self.key, self.phase = n, key, 0
        self.shard = shard.reshape(2, rows // 2, cols)
        self.cols = cols

    def moves(self):
        k, n = self.key, self.n
        q = n // 4
        s, a, b = k + "s", k + "0", k + "1"
        if self.phase == 0:
            whole = jax.ShapeDtypeStruct((2, n) + self.shard.shape[1:], bf16)
            copies = [
                (s, (i,), a, (i, m), ("fsdp", m << 2) if m else None) for m in range(q) for i in (0, 1)
            ]
            return {s: self.shard}, {}, {a: whole, b: whole}, copies
        near, far, both = slice(0, q), slice(q, 2 * q), slice(0, 2 * q)
        if self.phase == 1:
            copies = [(a, (0, near), b, (0, near), ("tp", 1)), (a, (1, near), a, (1, far), ("fsdp", 2))]
        elif self.phase == 2:
            copies = [
                (a, (0, near), a, (0, far), ("fsdp", 2)),
                (b, (0, near), b, (0, far), ("fsdp", 2)),
                (a, (1, both), b, (1, both), ("tp", 1)),
            ]
        else:
            copies = [(h, (i, both), h, (i, slice(2 * q, 4 * q)), ("fsdp", 1)) for h in (a, b) for i in (0, 1)]
        return {}, {a: self.halves[0], b: self.halves[1]}, {}, copies

    def take(self, got):
        self.halves = [got[self.key + "0"], got[self.key + "1"]]
        self.phase += 1
        if self.phase == 4:
            self.full = [h.reshape(-1, self.cols) for h in self.halves]


class Scatter:
    def __init__(self, key, grads, n, piece=0, pieces=1):
        self.n, self.key, self.phase = n, f"{key}{piece}_", 0
        cols = grads[0].shape[1]
        self.cols = cols // pieces
        self.rows = grads[0].shape[0] // n
        self.now = [g.reshape(2, n, self.rows // 2, cols) for g in grads]
        self.range = slice(piece * self.cols, (piece + 1) * self.cols)

    def moves(self):
        n, v = self.n, self.now
        q = n // 4
        part = (self.rows // 2, self.cols)
        far, rest = slice(q, 2 * q), slice(2 * q, 4 * q)

        def name(i):
            return f"{self.key}{i}"

        def new(*dims):
            return jax.ShapeDtypeStruct(dims + part, bf16)

        if self.phase == 0:
            news = [new(2, 2 * q), new(2, 2 * q)]
            copies = [
                (b, (i, rest, slice(None), self.range), b, (i,), ("fsdp", 1)) for b in (0, 1) for i in (0, 1)
            ]
        elif self.phase == 1:
            news = [new(q), new(q), new(2 * q)]
            copies = [
                (0, (0, far), 0, ALL, ("fsdp", 2)),
                (1, (0, far), 1, ALL, ("fsdp", 2)),
                (1, (1,), 2, ALL, ("tp", 1)),
            ]
        elif self.phase == 2:
            news = [new(q), new(q)]
            copies = [(1, ALL, 0, ALL, ("tp", 1)), (2, (far,), 1, ALL, ("fsdp", 2))]
        else:
            news = [new(2) for _ in range(1, q)]
            copies = [(i, (m,), m - 1, (i,), ("fsdp", m << 2)) for m in range(1, q) for i in (0, 1)]
        reads = {name(f"v{i}"): a for i, a in enumerate(v) if any(c[0] == i for c in copies)}
        self.names = [name(f"r{i}") for i in range(len(news))]
        copies = [(name(f"v{c[0]}"), c[1], self.names[c[2]], c[3], c[4]) for c in copies]
        return reads, {}, dict(zip(self.names, news)), copies

    def take(self, got):
        r, v = [got[k] for k in self.names], self.now
        q = self.n // 4
        if self.phase == 0:
            self.now = [low_sum(p[:, : 2 * q, :, self.range], a) for p, a in zip(v, r)]
        elif self.phase == 1:
            self.now = [low_sum(v[0][0, :q], r[0]), low_sum(v[1][0, :q], r[1]), low_sum(v[0][1], r[2])]
        elif self.phase == 2:
            self.now = [low_sum(v[0], r[0]), low_sum(v[2][:q], r[1])]
        else:
            total = jnp.stack([v[0][0], v[1][0]]).astype(f32)
            for p in r:
                total = total + p.astype(f32)
            self.out = total.reshape(self.rows, self.cols)
        self.phase += 1


def specs(blocks, ch, reverse):
    def at(q):
        return blocks - 1 - q if reverse else q

    def whole(rows, cols):
        return pl.BlockSpec((rows, cols), lambda q: (0, 0))

    return dict(
        main=pl.BlockSpec((Q, ch), lambda q: (at(q), 0)),
        prev=pl.BlockSpec((HALO, ch), lambda q: (jnp.maximum(at(q) * (Q // HALO) - 1, 0), 0)),
        tile=pl.BlockSpec((Q, 128), lambda q: (at(q), 0)),
        state=pl.BlockSpec((STATES, ch), lambda q: (at(q), 0)),
        halo=whole(HALO, ch), row8=whole(8, ch), row24=whole(24, ch), row16=whole(STATES, ch), small=whole(8, 128),
    )


def shape(dims, dtype):
    return jax.ShapeDtypeStruct(dims, dtype)


def cost(flops, moved):
    return pl.CostEstimate(flops=int(flops), bytes_accessed=int(moved), transcendentals=0)


def conv_state(x, halo, cw, e, hp, marks, tag="", load=None):
    tokens, ch = x.shape
    s = specs(tokens // Q, ch, False)
    return run(
        conv_state_kernel,
        (tokens // Q,),
        [s["main"], s["prev"], s["halo"], s["row8"], s["tile"], s["small"], s["tile"]],
        [s["main"], s["row16"], s["tile"], s["tile"], s["tile"]],
        [shape((tokens, ch), f32), shape((STATES, ch), f32)] + [shape((tokens, 128), f32)] * 3,
        [],
        [x, x, halo, cw, e, hp, marks],
        "conv_state" + tag,
        cost(tokens * ch * 5000, 4 * tokens * ch),
        load,
    )


def scan_forward(u, z, col, row, e, et, s0, cw, tag="", load=None):
    tokens, ch = u.shape
    s = specs(tokens // Q, ch, False)
    return run(
        scan_kernel,
        (tokens // Q,),
        [s["main"], s["main"], s["tile"], s["tile"], s["tile"], s["tile"], s["row16"], s["row8"]],
        [s["main"], s["main"], s["state"]],
        [shape((tokens, ch), bf16), shape((tokens, ch), f32), shape((tokens // Q * STATES, ch), f32)],
        [pltpu.VMEM((STATES, ch), f32)],
        [u, z, col, row, e, et, s0, cw],
        "scan_forward" + tag,
        cost(tokens * ch * 10000, 8 * tokens * ch),
        load,
    )


def gate_backward(gg, z, y, col, et, tag="", load=None):
    tokens, ch = z.shape
    s = specs(tokens // Q, ch, True)
    return run(
        gate_back_kernel,
        (tokens // Q,),
        [s["main"], s["main"], s["main"], s["tile"], s["tile"]],
        [s["main"], s["main"], s["row16"]],
        [shape((tokens, ch), f32), shape((tokens, ch), bf16), shape((STATES, ch), f32)],
        [],
        [gg, z, y, col, et],
        "gate_backward" + tag,
        cost(tokens * ch * 5000, 10 * tokens * ch),
        load,
    )


def scan_backward(u, dy, x, halo, cw, col, row, e, et, st, de, hp, tag="", load=None):
    tokens, ch = u.shape
    s = specs(tokens // Q, ch, True)
    place = jnp.arange(2 * Q)
    lower = ((place[:, None] >= place[None, :]) & (place[:, None] // Q == place[None, :] // Q)).astype(bf16)
    strict = (jnp.arange(Q)[:, None] < (place % Q)[None, :]).astype(f32)
    pairs = ch // 128
    lane = jnp.arange(3 * 128)
    target = (lane // 128) * HEADS + 2 * jnp.arange(pairs)[:, None] + ((lane % 128) // HEADDIM)[None, :]
    pick = (target[:, :, None] == jnp.arange(128)[None, None, :]).astype(bf16)
    by_head = (jnp.arange(ch)[:, None] // HEADDIM == jnp.arange(128)[None, :]).astype(f32)
    return run(
        scan_back_kernel,
        (tokens // Q,),
        [
            s["main"], s["main"], s["main"], s["prev"], s["halo"], s["row8"], s["tile"], s["tile"], s["tile"],
            s["tile"], s["state"], s["row16"], s["small"],
            pl.BlockSpec((2 * Q, 2 * Q), lambda q: (0, 0)), pl.BlockSpec((Q, 2 * Q), lambda q: (0, 0)),
            pl.BlockSpec((pairs, 3 * 128, 128), lambda q: (0, 0, 0)), pl.BlockSpec((ch, 128), lambda q: (0, 0)),
        ],
        [s["main"], s["tile"], s["row8"], s["row24"], s["small"]],
        [
            shape((tokens, ch), bf16), shape((tokens, 128), f32), shape((8, ch), f32), shape((24, ch), f32),
            shape((8, 128), f32),
        ],
        [
            pltpu.VMEM((STATES, ch), f32), pltpu.VMEM((128, Q), f32), pltpu.VMEM((8, ch), f32),
            pltpu.VMEM((Q, ch), bf16), pltpu.VMEM((Q, ch), bf16), pltpu.VMEM((128, ch), f32),
            pltpu.VMEM((128, ch), f32), pltpu.VMEM((Q, 128), f32), pltpu.VMEM((Q, Q), f32),
        ],
        [u, dy, x, x, halo, cw, col, row, e, et, st, de, hp, lower, strict, pick, by_head],
        "scan_backward" + tag,
        cost(tokens * ch * 25000, 12 * tokens * ch),
        load,
    )


def norm_specs(width):
    main = pl.BlockSpec((Q, width), lambda q: (q, 0))
    return main, pl.BlockSpec((width, Q), lambda q: (0, q)), pl.BlockSpec((1, width), lambda q: (0, 0))


def norm_forward(rows, gain_row, name, load=None):
    tokens, width = rows[0].shape
    main, turned, one = norm_specs(width)
    return run(
        norm_kernel,
        (tokens // Q,),
        [main] * len(rows) + [one],
        [main, main, turned],
        [shape((tokens, width), f32), shape((tokens, width), bf16), shape((width, tokens), bf16)],
        [],
        [*rows, gain_row],
        name,
        cost(tokens * width * 20, 12 * tokens * width),
        load,
    )


def norm_back(grads, rows, gain_row, bases, name, load=None, transpose=False):
    tokens, width = rows.shape
    main, turned, one = norm_specs(width)
    high, low, part, *high_t = run(
        functools.partial(norm_back_kernel, len(grads), len(grads) + len(bases)),
        (tokens // Q,),
        [main, one] + [main] * (len(grads) + len(bases)),
        [main, main, pl.BlockSpec((8, width), lambda q: (0, 0))] + [turned] * transpose,
        [shape((tokens, width), bf16), shape((tokens, width), bf16), shape((8, width), f32)]
        + [shape((width, tokens), bf16)] * transpose,
        [],
        [rows, gain_row, *grads, *bases],
        name,
        cost(tokens * width * 20, 16 * tokens * width),
        load,
    )
    return high, low, part[0], *high_t


def token_marks(seg, seg_before):
    tokens = seg.shape[0]
    by_block = seg.reshape(tokens // Q, Q)
    before = jnp.concatenate([seg_before[2:3], by_block[:-1, Q - 1]])
    padded = jnp.concatenate([seg_before, seg])
    found = [seg.astype(f32)] + [(padded[3 - k : 3 - k + tokens] == seg).astype(f32) for k in (1, 2, 3)]
    found.append((by_block == before[:, None]).astype(f32).reshape(-1))
    found.append((by_block == by_block[:, Q - 1 :]).astype(f32).reshape(-1))
    lane = jnp.arange(128)[None, :]
    out = jnp.zeros((tokens, 128), f32)
    for i, v in enumerate(found):
        out = jnp.where(lane == SEG + i, v[:, None], out)
    return out


def swap(x, axis, n, mask):
    return lax.ppermute(x, axis, [(i, i ^ mask) for i in range(n)])


def bf_dot(a, b):
    return jnp.dot(a, b, preferred_element_type=f32)


def make_local(n):
    def local(
        layer_in, seg_ids, gain_one, x_weight, z_weight, dt_weight, bc_weight, conv_weight, conv_bias,
        dt_bias, a_log, d_skip, out_weight, gain_two, gate_weight, up_weight, down_weight, cotangent,
    ):
        tokens, width = layer_in.shape
        rows, ch = x_weight.shape
        heads = dt_weight.shape[1]
        states = bc_weight.shape[1] // 2
        me, half = lax.axis_index("fsdp"), lax.axis_index("tp")

        epack = jnp.concatenate([dt_weight, bc_weight, jnp.zeros((rows, EXTRA - heads - 2 * states), bf16)], axis=1)
        X, E = Gather("x", x_weight, n), Gather("e", epack, n)
        Z, O = Gather("z", z_weight, n), Gather("o", out_weight, n)
        G, U, D = Gather("g", gate_weight, n), Gather("u", up_weight, n), Gather("d", down_weight, n)

        rate = -jnp.exp(a_log)
        pad = jnp.zeros((128 - heads,), f32)
        by_head = jnp.stack([jnp.concatenate([dt_bias, pad]), jnp.concatenate([rate, pad])])
        small = jnp.concatenate(
            [
                conv_weight,
                conv_bias[None, :],
                jnp.repeat(d_skip, HEADDIM)[None, :],
                jnp.pad(by_head, ((0, 0), (0, ch - 128))),
            ],
            axis=0,
        )
        smalls = [small, swap(small, "tp", 2, 1)]
        head_rows = [jnp.pad(v[6:8, :128], ((0, 6), (0, 0))) for v in smalls]
        before_rows = lax.ppermute(layer_in[tokens - HALO :], "tp", [(0, 1)])
        seg = lax.dynamic_slice(seg_ids, (half * tokens,), (tokens,))
        seg_before = jnp.where(half == 0, -1, seg_ids[tokens - 3 : tokens])

        part = rows // 2
        place = jnp.arange(2 * n)
        q = n // 4
        p = place % n
        part_at = (me ^ (p // (2 * q) + 2 * ((p // q) % 2) + 4 * (p % q))) * 2 + place // n
        seek = (place // 2) ^ me
        place_of = (place % 2) * n + (seek % 2) * 2 * q + ((seek // 2) % 2) * q + seek // 4
        col_at = (part_at[:, None] * part + jnp.arange(part)[None, :]).reshape(-1)
        turn = (jnp.arange(width)[:, None] == col_at[None, :]).astype(bf16)

        def to_local(v):
            return jnp.take(v.reshape(2 * n, part), part_at, axis=0).reshape(-1)

        def to_global(v):
            return jnp.take(v.reshape(2 * n, part), place_of, axis=0).reshape(-1)

        gain_one, gain_two = to_local(gain_one)[None, :], to_local(gain_two)[None, :]
        (rows_in,) = matmul([[(layer_in, turn)]], f32, 512, "turn_rows", Load(X, E))
        rows_in, normed, normed_t = norm_forward([rows_in], gain_one, "norm_one", Load(X, E, Z))
        cot_low, cot_t = matmul([[(cotangent, turn)]], bf16, 512, "turn_cotangent", Load(X, E, O), turned=True)
        carry_only(Load(X, E, Z), "carry_one")
        halo_rows = bf_dot(before_rows, turn)
        halo_scale = lax.rsqrt(jnp.mean(halo_rows * halo_rows, axis=-1, keepdims=True) + epsilon)
        normed_before = (halo_rows * halo_scale * gain_one).astype(bf16)
        marks = token_marks(seg, seg_before)

        found = matmul(
            [[(normed, w)] for w in X.full], f32, 512, "project_x", Load(Z, O, G), beside=(normed_before, E.full)
        )
        xs, halos, es = found[:2], found[2:4], found[4:]
        saved = []
        for b in (0, 1):
            v = dict(x=xs[b], cw=smalls[b], hp=head_rows[b])
            v["e"], v["halo"] = es[b], halos[b]
            load = Load(Z, O, G, U) if b == 0 else Load(G, O, D)
            v["u"], v["end"], v["col"], v["row"], v["et"] = conv_state(
                v["x"], v["halo"], v["cw"], v["e"], v["hp"], marks, tag=str(b), load=load
            )
            saved.append(v)
        starts = lax.ppermute(jnp.stack([v["end"] for v in saved]), "tp", [(0, 1)])[::-1]
        zs = matmul([[(normed, w)] for w in Z.full], f32, 512, "project_z", Load(G, U, D))
        for b in (0, 1):
            v = saved[b]
            v["z"] = zs[b]
            v["gated"], v["y"], v["states"] = scan_forward(
                v["u"], v["z"], v["col"], v["row"], v["e"], v["et"], starts[b], v["cw"],
                tag=str(b), load=Load(U) if b == 0 else Load(U, D),
            )
        (mixed,) = matmul(
            [[(v["gated"], w) for v, w in zip(saved, O.full)]], f32, 512, "project_out", Load(D), nt=True
        )
        hidden, normed_two, two_t = norm_forward([rows_in, mixed], gain_two, "norm_two")

        acts, gate_grads, up_grads = feed_forward(normed_two, cot_low, G.full, U.full, D.full)
        def halves(key, grads):
            return [Scatter(key, grads, n, i, 2) for i in (0, 1)]

        da, db = halves("d", matmul([[(cot_t, a)] for a in acts], bf16, 512, "down_grad"))
        ga, gb = halves("g", matmul([[(two_t, a)] for a in gate_grads], bf16, 512, "gate_grad", Load(da, db)))
        ua, ub = halves("u", matmul([[(two_t, a)] for a in up_grads], bf16, 512, "up_grad", Load(da, ga, gb)))
        (fed,) = matmul([list(zip(acts, D.full))], f32, 512, "project_down", Load(db, da, ua, ub), nt=True)
        out_low = (hidden + fed).astype(bf16)
        (grad_two,) = matmul(
            [list(zip(gate_grads, G.full)) + list(zip(up_grads, U.full))], f32, 256, "two_back",
            Load(ga, gb, db, da), nt=True,
        )
        mixed_grad, mixed_low, gain_two_part, mixed_t = norm_back(
            [grad_two], hidden, gain_two, [cot_low], "norm_two_back", Load(ga, db), True
        )

        so = Scatter("o", matmul([[(mixed_t, v["gated"])] for v in saved], bf16, 512, "out_grad", Load(ua, ga)), n)
        gg = matmul([[(mixed_grad, w)] for w in O.full], f32, 512, "gated_back", Load(gb, so))
        for b in (0, 1):
            v = saved[b]
            v["dy"], v["dz"], v["ds"] = gate_backward(
                gg[b], v["z"], v["y"], v["col"], v["et"], tag=str(b), load=Load(ua, gb) if b == 0 else None
            )
        ends = lax.ppermute(jnp.stack([v["ds"] for v in saved]), "tp", [(1, 0)])[::-1]
        sz = Scatter("z", matmul([[(normed_t, v["dz"])] for v in saved], bf16, 512, "z_grad", Load(ua)), n)

        def back(b, load):
            v = saved[b]
            v["dx"], v["de"], v["cg"], v["edge"], v["hg"] = scan_backward(
                v["u"], v["dy"], v["x"], v["halo"], v["cw"], v["col"], v["row"], v["e"], v["et"], v["states"],
                ends[b], v["hp"], tag=str(b), load=load,
            )
            cw, edge = v["cw"], v["edge"].reshape(3, 8, ch)
            fix = [jnp.zeros((HALO - 3, ch), f32)]
            for j in (3, 2, 1):
                fix.append(sum(cw[k : k + 1] * edge[k - 1, k - j : k - j + 1] for k in range(j, 4)))
            v["fix"] = jnp.concatenate(fix, axis=0)

        def x_gradient(b, load):
            v = saved[b]
            return matmul(
                [[(normed_t, v["dx"]), (before_t, v["fix"].astype(bf16))]], bf16, 512, f"x_grad{b}", load
            )[0]

        before_t = normed_before.T
        back(1, Load(so, ub, sz))
        sx = LateScatter("x", n, x_gradient(1, Load(so)))
        (grad_z,) = matmul(
            [[(v["dz"], w) for v, w in zip(saved, Z.full)]], f32, 512, "z_back", Load(sx, ub), nt=True
        )
        back(0, Load(sz, sx, so, ub))
        sx.given(x_gradient(0, None))
        fixes = lax.ppermute(jnp.stack([v["fix"] for v in saved]), "tp", [(1, 0)])[::-1]
        own, other = ([v["cg"][:6].reshape(-1), v["hg"][:2].reshape(-1)] for v in saved)
        gain_two_part = to_global(gain_two_part)
        own, other = jnp.concatenate(own + [gain_two_part]), jnp.concatenate(other + [gain_two_part])
        smalls_sum = SumAll("p", own, other, n)

        shared = 0.5 * (saved[0]["de"] + saved[1]["de"])
        own_lane = jnp.arange(EXTRA)[None, :] < heads
        for b in (0, 1):
            v = saved[b]
            last = v["dx"][tokens - HALO :].astype(f32) + fixes[b]
            v["dx"] = lax.dynamic_update_slice(v["dx"], last.astype(bf16), (tokens - HALO, 0))
            v["de"] = jnp.where(own_lane, v["de"], shared).astype(bf16)
        se = Scatter("e", matmul([[(normed_t, v["de"])] for v in saved], bf16, 128, "e_grad"), n)
        pairs = [(v["dx"], w) for v, w in zip(saved, X.full)] + [(v["de"], w) for v, w in zip(saved, E.full)]
        (grad_x,) = matmul([pairs], f32, 512, "x_back", Load(sx, se, sz, smalls_sum), nt=True)
        high, low, gain_one_part = norm_back(
            [grad_x, grad_z], rows_in, gain_one, [mixed_grad, mixed_low], "norm_one_back", Load(se, smalls_sum)
        )
        gain_one_part = to_global(gain_one_part)
        gain_sum = SumAll("q", gain_one_part, gain_one_part, n)
        (layer_out,) = matmul([[(out_low, turn)]], bf16, 512, "turn_out", Load(sx, se, sz, gain_sum), nt=True)
        (input_grad,) = matmul([[(high, turn), (low, turn)]], f32, 512, "turn_back", Load(sx, se, gain_sum), nt=True)

        total = smalls_sum.out
        cg, hg = total[: 6 * ch].reshape(6, ch), total[6 * ch : 6 * ch + 256].reshape(2, 128)
        gain_one_total, gain_two_total = gain_sum.out, total[6 * ch + 256 :]
        dt_b_total, a_total = hg[0, :heads], hg[1, :heads]
        skip_total = jnp.sum(cg[5].reshape(heads, HEADDIM), axis=1)
        return (
            layer_out,
            input_grad,
            gain_one_total,
            sx.out,
            sz.out,
            se.out[:, :heads],
            2.0 * se.out[:, heads : heads + 2 * states],
            cg[:4],
            cg[4],
            dt_b_total,
            a_total,
            skip_total,
            so.out,
            gain_two_total,
            jnp.concatenate([ga.out, gb.out], axis=1),
            jnp.concatenate([ua.out, ub.out], axis=1),
            jnp.concatenate([da.out, db.out], axis=1),
        )

    return local


def solution(mesh):
    rows = P(("fsdp", "tp"), None)
    weight = P("fsdp", "tp")
    in_specs = (
        rows, P("fsdp"), P(), weight, weight, weight, P("fsdp", None), P(None, "tp"), P("tp"), P("tp"), P("tp"),
        P("tp"), weight, P(), weight, weight, weight, rows,
    )
    out_specs = (
        rows, rows, P(), weight, weight, weight, P("fsdp", None), P(None, "tp"), P("tp"), P("tp"), P("tp"), P("tp"),
        weight, P(), weight, weight, weight,
    )
    return jax.shard_map(
        make_local(mesh.shape["fsdp"]), mesh=mesh, in_specs=in_specs, out_specs=out_specs, check_vma=False
    )
```

```python
import functools

import jax
import jax.numpy as jnp
from jax import lax
from jax.experimental import pallas as pl
from jax.experimental.pallas import tpu as pltpu
from jax.sharding import PartitionSpec as P

HEADDIM = 64
HEADS = 24
STATES = 16
Q = 128
HALO = 16
EXTRA = 128
RUN, DT, DEC, TAIL, SEG, CONT, LAST, LOGDT = 0, 24, 48, 72, 96, 100, 101, 104
COLB, COLC = HEADS, HEADS + STATES

f32 = jnp.float32
bf16 = jnp.bfloat16
highest = lax.Precision.HIGHEST
epsilon = 1e-05
NEG = -1e30


def dot(a, b, precision=None):
    return jnp.dot(a, b, preferred_element_type=f32, precision=precision)


def dot_t(a, b):
    return lax.dot_general(a, b, (((1,), (1,)), ((), ())), preferred_element_type=f32)


def split(v):
    high = v.astype(bf16)
    return high, (v - high.astype(f32)).astype(bf16)


def wide_left(v):
    high, low = split(v)
    return jnp.concatenate([high, low, high], axis=1)


def stack_right(v):
    high, low = split(v)
    return jnp.concatenate([high, high, low], axis=0)


def sigmoid(v):
    return 0.5 * jnp.tanh(0.5 * v) + 0.5


def lanes_of(rows=Q):
    return lax.broadcasted_iota(jnp.int32, (rows, 128), 1)


def pair_cols(col, first, j, left):
    a = col[:, first + 2 * j : first + 2 * j + 1]
    b = col[:, first + 2 * j + 1 : first + 2 * j + 2]
    return jnp.where(left, a, b)


def triangle(strict=False, transposed=False):
    i = lax.broadcasted_iota(jnp.int32, (Q, Q), 1 if transposed else 0)
    k = lax.broadcasted_iota(jnp.int32, (Q, Q), 0 if transposed else 1)
    return (i > k) if strict else (i >= k)


def spread_marks(col):
    return [jnp.broadcast_to(col[:, SEG + k : SEG + k + 1], (Q, 128)) for k in (1, 2, 3)]


def conv_rows(x_ref, xp_ref, halo_ref, cw_ref, marks, q, lanes):
    x = x_ref[:, lanes]
    prev = jnp.where(q == 0, halo_ref[:, lanes], xp_ref[:, lanes])
    cat = jnp.concatenate([prev, x], axis=0)
    acc = cw_ref[4:5, lanes] + cw_ref[0:1, lanes] * x
    shifted = []
    for k in (1, 2, 3):
        back = pltpu.roll(cat, k, 0)[HALO:, :] * marks[k - 1]
        shifted.append(back)
        acc = acc + cw_ref[k : k + 1, lanes] * back
    return x, shifted, acc


def conv_state_kernel(
    x_ref, xp_ref, halo_ref, cw_ref, e_ref, hp_ref, mark_ref, u_ref, end_ref, col_ref, row_ref, et_ref
):
    q = pl.program_id(0)

    @pl.when(q == 0)
    def _():
        end_ref[...] = jnp.zeros_like(end_ref)

    e, marks = e_ref[...], mark_ref[...]
    lane = lanes_of()
    head = lane < HEADS
    raw = e + hp_ref[0:1, :]
    dt = jnp.where(head, jnp.maximum(raw, 0.0) + jnp.log1p(jnp.exp(-jnp.abs(raw))), 0.0)
    run = dot(jnp.where(triangle(), 1.0, 0.0), dt * hp_ref[1:2, :], highest)
    dec = jnp.where(head, jnp.exp(run) * marks[:, CONT : CONT + 1], 0.0)
    tail = jnp.where(head, jnp.exp(run[Q - 1 : Q, :] - run) * marks[:, LAST : LAST + 1], 0.0)
    log_dt = jnp.where(head, jnp.log(dt), 0.0)
    col = (
        run
        + pltpu.roll(dt, DT, 1)
        + pltpu.roll(dec, DEC, 1)
        + pltpu.roll(tail, TAIL, 1)
        + marks
        + pltpu.roll(log_dt, LOGDT, 1)
    )
    col_ref[...] = col
    row_ref[...] = col.T
    et = e.T
    et_ref[...] = et
    bt = wide_left(et[COLB:COLC, :])
    left = lane < HEADDIM
    spread = spread_marks(col)
    for j in range(x_ref.shape[1] // 128):
        lanes = slice(128 * j, 128 * j + 128)
        _, _, acc = conv_rows(x_ref, xp_ref, halo_ref, cw_ref, spread, q, lanes)
        u = acc * sigmoid(acc)
        u_ref[:, lanes] = u
        scaled = u * (pair_cols(col, DT, j, left) * pair_cols(col, TAIL, j, left))
        keep = pair_cols(col[Q - 1 : Q, :], DEC, j, left[:1])
        end_ref[:, lanes] = keep * end_ref[:, lanes] + dot(bt, stack_right(scaled))


def scan_kernel(
    u_ref, z_ref, col_ref, row_ref, e_ref, et_ref, s0_ref, cw_ref, gated_ref, y_ref, st_ref, S
):
    @pl.when(pl.program_id(0) == 0)
    def _():
        S[...] = s0_ref[...]

    col, row = col_ref[...], row_ref[...]
    left = lanes_of() < HEADDIM
    c = e_ref[:, COLC : COLC + STATES]
    bt = et_ref[COLB:COLC, :]
    scores = dot(c, bt, highest)
    neg = jnp.where((col[:, SEG : SEG + 1] == row[SEG : SEG + 1, :]) & triangle(), 0.0, NEG)
    c, bt = wide_left(c), wide_left(bt)
    for j in range(u_ref.shape[1] // 128):
        lanes = slice(128 * j, 128 * j + 128)
        uf = u_ref[:, lanes]
        u, u_low = split(uf)
        state = S[:, lanes]
        st_ref[:, lanes] = state
        parts, rest = [], []
        for h in (2 * j, 2 * j + 1):
            gap = col[:, h : h + 1] - (row[h : h + 1, :] - row[LOGDT + h : LOGDT + h + 1, :])
            high, low = split(jnp.exp(gap + neg) * scores)
            parts.append(high)
            rest.append(low)
        zero = jnp.zeros_like(u)
        both = [jnp.where(left, u, zero), jnp.where(left, zero, u)]
        both_low = [jnp.where(left, u_low, zero), jnp.where(left, zero, u_low)]
        y = dot(jnp.concatenate(parts + rest + parts, axis=1), jnp.concatenate(both + both + both_low, axis=0))
        y = y + dot(c, stack_right(state)) * pair_cols(col, DEC, j, left) + cw_ref[5:6, lanes] * uf
        z = z_ref[:, lanes]
        y_ref[:, lanes] = y
        gated_ref[:, lanes] = (y * (z * sigmoid(z))).astype(bf16)
        scaled = uf * (pair_cols(col, DT, j, left) * pair_cols(col, TAIL, j, left))
        keep = pair_cols(col[Q - 1 : Q, :], DEC, j, left[:1])
        S[:, lanes] = keep * state + dot(bt, stack_right(scaled))


def gate_back_kernel(gg_ref, z_ref, y_ref, col_ref, et_ref, dy_ref, dz_ref, ds_ref):
    @pl.when(pl.program_id(0) == 0)
    def _():
        ds_ref[...] = jnp.zeros_like(ds_ref)

    col = col_ref[...]
    left = lanes_of() < HEADDIM
    ct = et_ref[COLC : COLC + STATES, :].astype(bf16)
    for j in range(z_ref.shape[1] // 128):
        lanes = slice(128 * j, 128 * j + 128)
        z = z_ref[:, lanes]
        gg = gg_ref[:, lanes]
        sig = sigmoid(z)
        dy = gg * (z * sig)
        dy_ref[:, lanes] = dy
        dz_ref[:, lanes] = (gg * y_ref[:, lanes] * (sig * (1.0 + z * (1.0 - sig)))).astype(bf16)
        scaled = (dy * pair_cols(col, DEC, j, left)).astype(bf16)
        keep = pair_cols(col[Q - 1 : Q, :], DEC, j, left[:1])
        ds_ref[:, lanes] = keep * ds_ref[:, lanes] + dot(ct, scaled)


def scan_back_kernel(
    u_ref, dy_ref, x_ref, xp_ref, halo_ref, cw_ref, col_ref, row_ref, e_ref, et_ref, st_ref, de_ref, hp_ref,
    lw_ref, sm_ref, pick_ref, head_ref,
    dx_ref, de_out_ref, cg_ref, edge_ref, hg_ref,
    D, WA, CONST, TAILS, DECS, DS, ST, SUMS, DG,
):
    step = pl.program_id(0)
    q = pl.num_programs(0) - 1 - step

    @pl.when(step == 0)
    def _():
        D[...] = de_ref[...]
        cg_ref[...] = jnp.zeros_like(cg_ref)
        edge_ref[...] = jnp.zeros_like(edge_ref)
        hg_ref[...] = jnp.zeros_like(hg_ref)
        WA[...] = jnp.zeros_like(WA)
        CONST[...] = jnp.zeros_like(CONST)
        DS[...] = jnp.zeros_like(DS)
        ST[...] = jnp.zeros_like(ST)

    col, row = col_ref[...], row_ref[...]
    lane = lanes_of()
    left = lane < HEADDIM
    e = e_ref[...]
    b, ct = e[:, COLB:COLC], et_ref[COLC : COLC + STATES, :]
    scores = dot(b, ct, highest)
    neg = jnp.where((col[:, SEG : SEG + 1] == row[SEG : SEG + 1, :]) & triangle(transposed=True), 0.0, NEG)
    b, ct, c = wide_left(b), ct.astype(bf16), wide_left(e[:, COLC : COLC + STATES])
    spread = spread_marks(col)
    DG[...] = jnp.zeros_like(DG)
    SUMS[...] = jnp.zeros_like(SUMS)
    for j in range(u_ref.shape[1] // 128):
        lanes = slice(128 * j, 128 * j + 128)
        u = u_ref[:, lanes]
        dyf = dy_ref[:, lanes]
        dy = dyf.astype(bf16)
        dt = pair_cols(col, DT, j, left)
        dec = pair_cols(col, DEC, j, left)
        tail = pair_cols(col, TAIL, j, left)
        keep = pair_cols(col[Q - 1 : Q, :], DEC, j, left[:1])
        state, grad_state = st_ref[:, lanes], D[:, lanes]
        DS[COLB:COLC, lanes] = grad_state
        ST[COLC : COLC + STATES, lanes] = state
        xs = u * dt
        zero = jnp.zeros_like(dy)
        both = jnp.concatenate([jnp.where(left, dy, zero), jnp.where(left, zero, dy)], axis=0)
        d_mat = dot_t(xs.astype(bf16), both)
        mats, pairs, d_scores = [], [], None
        for i, h in enumerate((2 * j, 2 * j + 1)):
            decay = jnp.exp((row[h : h + 1, :] - col[:, h : h + 1]) + neg)
            mat = decay * scores
            dm = d_mat[:, Q * i : Q * i + Q]
            d_scores = decay * dm if d_scores is None else d_scores + decay * dm
            mats.append(mat.astype(bf16))
            pairs.append((mat * dm).astype(bf16))
        DG[...] += d_scores
        dxs = dot(jnp.concatenate(mats, axis=1), both)
        spans = dot(jnp.concatenate(pairs, axis=1), lw_ref[...]) * sm_ref[...]
        sums = jnp.sum(spans, axis=0, keepdims=True)
        WA[2 * j : 2 * j + 1, :] = sums[:, :Q]
        WA[2 * j + 1 : 2 * j + 2, :] = sums[:, Q:]
        from_tail = tail * dot(b, stack_right(grad_state))
        dxs = dxs + from_tail
        ydec = dyf * dec
        found = [u * dxs, ydec * dot(c, stack_right(state)), xs * from_tail]
        SUMS[...] += dot(jnp.concatenate([v.astype(bf16) for v in found], axis=1), pick_ref[j])
        TAILS[:, lanes] = (xs * tail).astype(bf16)
        low_dec = ydec.astype(bf16)
        DECS[:, lanes] = low_dec
        CONST[0:1, lanes] = keep * jnp.sum(state * grad_state, axis=0, keepdims=True)
        D[:, lanes] = keep * grad_state + dot(ct, low_dec)

        x, shifted, acc = conv_rows(x_ref, xp_ref, halo_ref, cw_ref, spread, q, lanes)
        sig = sigmoid(acc)
        dconv = (dxs * dt + cw_ref[5:6, lanes] * dyf) * (sig * (1.0 + acc * (1.0 - sig)))
        dx = cw_ref[0:1, lanes] * dconv
        cg_ref[0:1, lanes] += jnp.sum(dconv * x, axis=0, keepdims=True)
        for k in (1, 2, 3):
            masked = dconv * spread[k - 1]
            after = edge_ref[8 * (k - 1) : 8 * k, lanes]
            cat = jnp.concatenate([masked, after], axis=0)
            dx = dx + cw_ref[k : k + 1, lanes] * pltpu.roll(cat, Q + 8 - k, 0)[:Q, :]
            edge_ref[8 * (k - 1) : 8 * k, lanes] = masked[:8, :]
            cg_ref[k : k + 1, lanes] += jnp.sum(dconv * shifted[k - 1], axis=0, keepdims=True)
        cg_ref[4:5, lanes] += jnp.sum(dconv, axis=0, keepdims=True)
        cg_ref[5:6, lanes] += jnp.sum(dyf * u, axis=0, keepdims=True)
        dx_ref[:, lanes] = dx.astype(bf16)

    head = lane < HEADS
    found = SUMS[...]
    suffix = jnp.where(triangle(transposed=True), 1.0, 0.0)
    prefix = jnp.where(triangle(strict=True), 1.0, 0.0)
    d_step = (
        WA[...].T
        + dot(suffix, pltpu.roll(found, 128 - HEADS, 1), highest)
        + dot(prefix, pltpu.roll(found, 128 - 2 * HEADS, 1), highest)
        + dot(CONST[...], head_ref[...], highest)[0:1, :]
    )
    d_dt = d_step * hp_ref[1:2, :] + found
    d_raw = jnp.where(head, d_dt * sigmoid(e + hp_ref[0:1, :]), 0.0)
    step_dt = jnp.where(head, pltpu.roll(col, 128 - DT, 1), 0.0)
    hg_ref[0:1, :] += jnp.sum(d_raw, axis=0, keepdims=True)
    hg_ref[1:2, :] += jnp.sum(jnp.where(head, d_step, 0.0) * step_dt, axis=0, keepdims=True) * hp_ref[1:2, :]
    total = DG[...]
    b_part = jnp.where((lane >= COLB) & (lane < COLC), e, 0.0)
    c_part = jnp.where((lane >= COLC) & (lane < COLC + STATES), e, 0.0)
    de_out_ref[...] = (
        d_raw
        + dot_t(TAILS[...], DS[...].astype(bf16))
        + dot_t(DECS[...], ST[...].astype(bf16))
        + dot(total, pltpu.roll(c_part, 128 - STATES, 1), highest)
        + dot(total.T, pltpu.roll(b_part, STATES, 1), highest)
    )


def norm_kernel(*refs):
    *row_refs, gain_ref, hidden_ref, out_ref, turned_ref = refs
    rows = row_refs[0][...]
    for r in row_refs[1:]:
        rows = rows + r[...]
    hidden_ref[...] = rows
    scale = lax.rsqrt(jnp.mean(rows * rows, axis=-1, keepdims=True) + epsilon)
    normed = rows * scale * gain_ref[...]
    out_ref[...] = normed.astype(bf16)
    turned_ref[...] = normed.T.astype(bf16)


def norm_back_kernel(n_grads, n_given, rows_ref, gain_ref, *refs):
    given, (high_ref, low_ref, part_ref), turned_refs = refs[:n_given], refs[n_given : n_given + 3], refs[n_given + 3 :]

    @pl.when(pl.program_id(0) == 0)
    def _():
        part_ref[...] = jnp.zeros_like(part_ref)

    rows, grad = rows_ref[...], given[0][...]
    for r in given[1:n_grads]:
        grad = grad + r[...]
    scale = lax.rsqrt(jnp.mean(rows * rows, axis=-1, keepdims=True) + epsilon)
    unit = rows * scale
    part_ref[0:1, :] += jnp.sum(grad * unit, axis=0, keepdims=True)
    unit_grad = grad * gain_ref[...]
    total = scale * (unit_grad - unit * jnp.mean(unit_grad * unit, axis=-1, keepdims=True))
    for r in given[n_grads:]:
        total = total + r[...].astype(f32)
    high = total.astype(bf16)
    high_ref[...] = high
    low_ref[...] = (total - high.astype(f32)).astype(bf16)
    for r in turned_refs:
        r[...] = total.T.astype(bf16)


def flip(i, mask):
    bit = 1
    while bit <= mask:
        if mask & bit:
            i = i + bit * (1 - 2 * ((i // bit) % 2))
        bit *= 2
    return i


class Load:
    def __init__(self, *movers):
        self.reads, self.updates, self.news, self.copies = {}, {}, {}, []
        self.movers = movers
        for mover in movers:
            reads, updates, news, copies = mover.moves()
            self.reads.update(reads)
            self.updates.update(updates)
            self.news.update(news)
            self.copies += copies

    def arrive(self, got):
        for mover in self.movers:
            mover.take(got)


IDS = {}


def run(body, grid, in_specs, out_specs, out_shape, scratch, args, name, estimate=None, load=None, vmem=56):
    params = dict(dimension_semantics=("arbitrary",) * len(grid), vmem_limit_bytes=vmem * 1024 * 1024)
    if load is None:
        return pl.pallas_call(
            body, name=name, grid=grid, in_specs=in_specs, out_specs=out_specs, out_shape=out_shape,
            scratch_shapes=scratch, compiler_params=pltpu.CompilerParams(**params), cost_estimate=estimate,
        )(*args)
    cid = IDS.setdefault(name, len(IDS) + 1)
    reads, updates, news = list(load.reads), list(load.updates), list(load.news)
    n_in, n_out, n_scratch, n_copies = len(args), len(out_shape), len(scratch), len(load.copies)
    routes = []
    for c in load.copies:
        if c[4] is not None and c[4] not in routes:
            routes.append(c[4])

    def kernel(*refs):
        ins, rest = refs[:n_in], refs[n_in:]
        held = dict(zip(reads, rest))
        rest = rest[len(reads) + len(updates) :]
        outs, rest = rest[:n_out], rest[n_out:]
        held.update(zip(updates + news, rest))
        rest = rest[len(updates) + len(news) :]
        mine, (send, recv) = rest[:n_scratch], rest[n_scratch:]

        def device(route):
            return {axis: flip(lax.axis_index(axis), mask) for axis, mask in zip(route[::2], route[1::2])}

        def make(i, c):
            src, dst = held[c[0]].at[c[1]], held[c[2]].at[c[3]]
            if c[4] is None:
                return pltpu.make_async_copy(src, dst, recv.at[i])
            return pltpu.make_async_remote_copy(
                src_ref=src, dst_ref=dst, send_sem=send.at[i], recv_sem=recv.at[i],
                device_id=device(c[4]), device_id_type=pl.DeviceIdType.MESH,
            )

        first, last = pl.program_id(0) == 0, pl.program_id(0) == grid[0] - 1
        for axis in range(1, len(grid)):
            first = first & (pl.program_id(axis) == 0)
            last = last & (pl.program_id(axis) == grid[axis] - 1)

        @pl.when(first)
        def _():
            barrier = pltpu.get_barrier_semaphore()
            for route in routes:
                pl.semaphore_signal(
                    barrier, inc=1, device_id=device(route), device_id_type=pl.DeviceIdType.MESH
                )
            pl.semaphore_wait(barrier, len(routes))
            for i, c in enumerate(load.copies):
                make(i, c).start()

        if body is not None:
            body(*ins, *outs, *mine)

        @pl.when(last)
        def _():
            for i, c in enumerate(load.copies):
                make(i, c).wait()

    hbm = pl.BlockSpec(memory_space=pltpu.HBM)
    result = pl.pallas_call(
        kernel,
        name=name,
        grid=grid,
        in_specs=list(in_specs) + [hbm] * (len(reads) + len(updates)),
        out_specs=list(out_specs) + [hbm] * (len(updates) + len(news)),
        out_shape=list(out_shape)
        + [jax.ShapeDtypeStruct(load.updates[k].shape, load.updates[k].dtype) for k in updates]
        + [load.news[k] for k in news],
        scratch_shapes=list(scratch) + [pltpu.SemaphoreType.DMA((n_copies,)), pltpu.SemaphoreType.DMA((n_copies,))],
        input_output_aliases={n_in + len(reads) + i: n_out + i for i in range(len(updates))},
        compiler_params=pltpu.CompilerParams(collective_id=cid, has_side_effects=True, **params),
        cost_estimate=estimate,
    )(*args, *[load.reads[k] for k in reads], *[load.updates[k] for k in updates])
    load.arrive(dict(zip(updates + news, result[n_out:])))
    return result[:n_out]


def matmul(jobs, dtype, tile, name, load=None, nt=False, turned=False, beside=None):
    n_jobs, n_pairs = len(jobs), len(jobs[0])
    rows = jobs[0][0][0].shape[0]
    columns = jobs[0][0][1].shape[0 if nt else 1]
    tiles = columns // tile

    def at(job):
        def place(j, t):
            return jnp.where(j == job, t, jnp.where(j < job, 0, tiles - 1))

        return place

    args, in_specs = [], []
    for job, pairs in enumerate(jobs):
        for left, right in pairs:
            args += [left, right]
            k = left.shape[1]
            in_specs.append(pl.BlockSpec((rows, k), lambda j, t: (0, 0), pipeline_mode=pl.Buffered(1)))
            if nt:
                in_specs.append(pl.BlockSpec((tile, k), lambda j, t, p=at(job): (p(j, t), 0)))
            else:
                in_specs.append(pl.BlockSpec((k, tile), lambda j, t, p=at(job): (0, p(j, t))))
    out_specs = [pl.BlockSpec((rows, tile), lambda j, t, p=at(job): (0, p(j, t))) for job in range(n_jobs)]
    out_shape = [jax.ShapeDtypeStruct((rows, columns), dtype)] * n_jobs
    if turned:
        out_specs += [pl.BlockSpec((tile, rows), lambda j, t, p=at(job): (p(j, t), 0)) for job in range(n_jobs)]
        out_shape += [jax.ShapeDtypeStruct((columns, rows), dtype)] * n_jobs
    if beside:
        few, narrow = beside
        args += [few, *narrow]
        in_specs += [pl.BlockSpec(v.shape, lambda j, t: (0, 0), pipeline_mode=pl.Buffered(1)) for v in (few, *narrow)]
        out_specs += [pl.BlockSpec((few.shape[0], tile), lambda j, t, p=at(job): (0, p(j, t))) for job in range(n_jobs)]
        out_shape += [jax.ShapeDtypeStruct((few.shape[0], columns), dtype)] * n_jobs
        out_specs += [pl.BlockSpec((rows, v.shape[1]), lambda j, t: (0, 0)) for v in narrow]
        out_shape += [jax.ShapeDtypeStruct((rows, v.shape[1]), dtype) for v in narrow]
    n_in = len(args)

    def body(*refs):
        ins, outs = refs[:n_in], refs[n_in:]
        for job in range(n_jobs):

            @pl.when(pl.program_id(0) == job)
            def _(job=job):
                total = None
                for p in range(n_pairs):
                    left, right = ins[2 * (job * n_pairs + p)], ins[2 * (job * n_pairs + p) + 1]
                    term = (dot_t if nt else dot)(left[...], right[...])
                    total = term if total is None else total + term
                outs[job][...] = total.astype(dtype)
                if turned:
                    outs[n_jobs + job][...] = total.T.astype(dtype)
                if beside:
                    left, right, few = ins[2 * job * n_pairs], ins[2 * job * n_pairs + 1], ins[2 * n_jobs * n_pairs]
                    outs[n_jobs + job][...] = dot(few[...], right[...]).astype(dtype)

                    @pl.when(pl.program_id(1) == 0)
                    def _():
                        narrow = ins[2 * n_jobs * n_pairs + 1 + job]
                        outs[2 * n_jobs + job][...] = dot(left[...], narrow[...]).astype(dtype)

    depth = sum(p[0].shape[1] for p in jobs[0])
    return run(
        body, (n_jobs, tiles), in_specs, out_specs, out_shape, [], args, name,
        pl.CostEstimate(
            flops=2 * n_jobs * rows * columns * depth, bytes_accessed=4 * n_jobs * rows * columns, transcendentals=0
        ),
        load,
    )


class LateScatter:
    def __init__(self, key, n, other):
        self.key, self.n, self.phase = key, n, 0
        self.given(other)

    def given(self, grad):
        self.rows, self.cols = grad.shape[0] // self.n, grad.shape[1]
        self.now = grad.reshape(2, self.n, self.rows // 2, self.cols)

    def moves(self):
        k, q, v = self.key, self.n // 4, self.now
        far, rest = slice(q, 2 * q), slice(2 * q, 4 * q)

        def new(*dims):
            return jax.ShapeDtypeStruct(dims + (self.rows // 2, self.cols), bf16)

        core = [(k + "v", (i, rest), k + "r", (i,), ("fsdp", 1)) for i in (0, 1)]
        if self.phase == 0:
            return {k + "v": v}, {}, {k + "r": new(2, 2 * q)}, core
        if self.phase == 1:
            copies = [(k + "v", (0, far), k + "r", ALL, ("fsdp", 2)), (k + "v", (1,), k + "s", ALL, ("tp", 1))]
            return {k + "v": v}, {}, {k + "r": new(q), k + "s": new(2 * q)}, copies
        if self.phase == 2:
            copies = core + [(k + "a", ALL, k + "s", ALL, ("tp", 1))]
            return {k + "v": v, k + "a": self.other}, {}, {k + "r": new(2, 2 * q), k + "s": new(q)}, copies
        if self.phase == 3:
            copies = [(k + "v", (far,), k + "r", ALL, ("fsdp", 2)), (k + "a", (far,), k + "s", ALL, ("fsdp", 2))]
            return {k + "v": v[0], k + "a": v[1]}, {}, {k + "r": new(q), k + "s": new(q)}, copies
        news = {f"{k}r{m}": new(2) for m in range(1, q)}
        copies = [(f"{k}v{i}", (m,), f"{k}r{m}", (i,), ("fsdp", m << 2)) for m in range(1, q) for i in (0, 1)]
        return {k + "v0": v[0], k + "v1": v[1]}, {}, news, copies

    def take(self, got):
        k, q, v = self.key, self.n // 4, self.now
        if self.phase == 0:
            self.now = low_sum(v[:, : 2 * q], got[k + "r"])
        elif self.phase == 1:
            self.other, self.lower = low_sum(v[0, :q], got[k + "r"]), got[k + "s"]
        elif self.phase == 2:
            own = [v[i, : 2 * q].astype(f32) + got[k + "r"][i].astype(f32) for i in (0, 1)]
            self.now = [own[0].astype(bf16), (own[1] + self.lower.astype(f32)).astype(bf16)]
            self.other = got[k + "s"]
        elif self.phase == 3:
            upper = v[0][:q].astype(f32) + got[k + "r"].astype(f32) + self.other.astype(f32)
            self.now = [upper.astype(bf16), low_sum(v[1][:q], got[k + "s"])]
        else:
            total = jnp.stack([v[0][0], v[1][0]]).astype(f32)
            for m in range(1, q):
                total = total + got[f"{k}r{m}"].astype(f32)
            self.out = total.reshape(self.rows, self.cols)
        self.phase += 1


class SumAll:
    def __init__(self, key, own, other, n):
        self.key, self.n, self.phase, self.size = key, n, 0, own.shape[0]
        rows = -(-self.size // 1024) * 8
        self.own, self.other = (jnp.pad(v, (0, rows * 128 - self.size)).reshape(rows, 128) for v in (own, other))

    def moves(self):
        k = self.key
        new = jax.ShapeDtypeStruct(self.own.shape, f32)
        if self.phase == 0:
            reads = {k + "v": self.own, k + "w": self.other}
            steps = [(m % 4, m // 4) for m in range(1, 8)]
            routes = [(("fsdp", f) if f else ()) + (("tp", t) if t else ()) for f, t in steps]
            sources = [k + ("w" if t else "v") for f, t in steps]
        else:
            reads, routes = {k + "v": self.own}, [("fsdp", m << 2) for m in range(1, self.n // 4)]
            sources = [k + "v"] * len(routes)
        names = [f"{k}r{i}" for i in range(len(routes))]
        copies = [(a, ALL, b, ALL, c) for a, b, c in zip(sources, names, routes)]
        return reads, {}, {b: new for b in names}, copies

    def take(self, got):
        count = 8 if self.phase == 0 else self.n // 4
        terms = [self.own] + [got[f"{self.key}r{i}"] for i in range(count - 1)]
        while len(terms) > 1:
            terms = [a + b for a, b in zip(terms[::2], terms[1::2])]
        self.own = terms[0]
        self.phase += 1
        self.out = self.own.reshape(-1)[: self.size]


def feed_forward(normed, cot, gate_w, up_w, down_w):
    tokens, width = normed.shape
    cols, tile, step = gate_w[0].shape[1], 512, 256
    tiles = cols // tile

    def at(job):
        def place(j, t):
            return jnp.where(j == job, t, jnp.where(j < job, 0, tiles - 1))

        return place

    whole = pl.BlockSpec((tokens, width), lambda j, t: (0, 0), pipeline_mode=pl.Buffered(1))
    args, in_specs, out_specs = [normed, cot], [whole, whole], []
    for b in (0, 1):
        args += [gate_w[b], up_w[b], down_w[b]]
        in_specs += [pl.BlockSpec((width, tile), lambda j, t, p=at(b): (0, p(j, t)))] * 3
        out_specs += [pl.BlockSpec((tokens, tile), lambda j, t, p=at(b): (0, p(j, t)))] * 3

    def body(n_ref, c_ref, *refs):
        for b in (0, 1):
            wg, wu, wd = refs[3 * b : 3 * b + 3]
            act, gg, ug = refs[6 + 3 * b : 9 + 3 * b]

            @pl.when(pl.program_id(0) == b)
            def _(wg=wg, wu=wu, wd=wd, act=act, gg=gg, ug=ug):
                for i in range(tokens // step):
                    rows = slice(step * i, step * i + step)
                    gate, up, back = dot(n_ref[rows, :], wg[...]), dot(n_ref[rows, :], wu[...]), dot(c_ref[rows, :], wd[...])
                    sig = sigmoid(gate)
                    silu = gate * sig
                    act[rows, :] = (silu * up).astype(bf16)
                    gg[rows, :] = (back * up * sig * (1.0 + gate * (1.0 - sig))).astype(bf16)
                    ug[rows, :] = (back * silu).astype(bf16)

    out = run(
        body, (2, tiles), in_specs, out_specs, [jax.ShapeDtypeStruct((tokens, cols), bf16)] * 6, [], args,
        "feed_forward", pl.CostEstimate(flops=12 * tokens * cols * width, bytes_accessed=12 * tokens * cols, transcendentals=0),
    )
    return [out[0], out[3]], [out[1], out[4]], [out[2], out[5]]


def carry_only(load, name):
    run(None, (1,), [], [], [], [], [], name, None, load)


ALL = (slice(None),)


def low_sum(a, b):
    return a + b


class Gather:
    def __init__(self, key, shard, n):
        rows, cols = shard.shape
        self.n, self.key, self.phase = n, key, 0
        self.shard = shard.reshape(2, rows // 2, cols)
        self.cols = cols

    def moves(self):
        k, n = self.key, self.n
        q = n // 4
        s, a, b = k + "s", k + "0", k + "1"
        if self.phase == 0:
            whole = jax.ShapeDtypeStruct((2, n) + self.shard.shape[1:], bf16)
            copies = [
                (s, (i,), a, (i, m), ("fsdp", m << 2) if m else None) for m in range(q) for i in (0, 1)
            ]
            return {s: self.shard}, {}, {a: whole, b: whole}, copies
        near, far, both = slice(0, q), slice(q, 2 * q), slice(0, 2 * q)
        if self.phase == 1:
            copies = [(a, (0, near), b, (0, near), ("tp", 1)), (a, (1, near), a, (1, far), ("fsdp", 2))]
        elif self.phase == 2:
            copies = [
                (a, (0, near), a, (0, far), ("fsdp", 2)),
                (b, (0, near), b, (0, far), ("fsdp", 2)),
                (a, (1, both), b, (1, both), ("tp", 1)),
            ]
        else:
            copies = [(h, (i, both), h, (i, slice(2 * q, 4 * q)), ("fsdp", 1)) for h in (a, b) for i in (0, 1)]
        return {}, {a: self.halves[0], b: self.halves[1]}, {}, copies

    def take(self, got):
        self.halves = [got[self.key + "0"], got[self.key + "1"]]
        self.phase += 1
        if self.phase == 4:
            self.full = [h.reshape(-1, self.cols) for h in self.halves]


class Scatter:
    def __init__(self, key, grads, n, piece=0, pieces=1):
        self.n, self.key, self.phase = n, f"{key}{piece}_", 0
        cols = grads[0].shape[1]
        self.cols = cols // pieces
        self.rows = grads[0].shape[0] // n
        self.now = [g.reshape(2, n, self.rows // 2, cols) for g in grads]
        self.range = slice(piece * self.cols, (piece + 1) * self.cols)

    def moves(self):
        n, v = self.n, self.now
        q = n // 4
        part = (self.rows // 2, self.cols)
        far, rest = slice(q, 2 * q), slice(2 * q, 4 * q)

        def name(i):
            return f"{self.key}{i}"

        def new(*dims):
            return jax.ShapeDtypeStruct(dims + part, bf16)

        if self.phase == 0:
            news = [new(2, 2 * q), new(2, 2 * q)]
            copies = [
                (b, (i, rest, slice(None), self.range), b, (i,), ("fsdp", 1)) for b in (0, 1) for i in (0, 1)
            ]
        elif self.phase == 1:
            news = [new(q), new(q), new(2 * q)]
            copies = [
                (0, (0, far), 0, ALL, ("fsdp", 2)),
                (1, (0, far), 1, ALL, ("fsdp", 2)),
                (1, (1,), 2, ALL, ("tp", 1)),
            ]
        elif self.phase == 2:
            news = [new(q), new(q)]
            copies = [(1, ALL, 0, ALL, ("tp", 1)), (2, (far,), 1, ALL, ("fsdp", 2))]
        else:
            news = [new(2) for _ in range(1, q)]
            copies = [(i, (m,), m - 1, (i,), ("fsdp", m << 2)) for m in range(1, q) for i in (0, 1)]
        reads = {name(f"v{i}"): a for i, a in enumerate(v) if any(c[0] == i for c in copies)}
        self.names = [name(f"r{i}") for i in range(len(news))]
        copies = [(name(f"v{c[0]}"), c[1], self.names[c[2]], c[3], c[4]) for c in copies]
        return reads, {}, dict(zip(self.names, news)), copies

    def take(self, got):
        r, v = [got[k] for k in self.names], self.now
        q = self.n // 4
        if self.phase == 0:
            self.now = [low_sum(p[:, : 2 * q, :, self.range], a) for p, a in zip(v, r)]
        elif self.phase == 1:
            self.now = [low_sum(v[0][0, :q], r[0]), low_sum(v[1][0, :q], r[1]), low_sum(v[0][1], r[2])]
        elif self.phase == 2:
            self.now = [low_sum(v[0], r[0]), low_sum(v[2][:q], r[1])]
        else:
            total = jnp.stack([v[0][0], v[1][0]]).astype(f32)
            for p in r:
                total = total + p.astype(f32)
            self.out = total.reshape(self.rows, self.cols)
        self.phase += 1


def specs(blocks, ch, reverse):
    def at(q):
        return blocks - 1 - q if reverse else q

    def whole(rows, cols):
        return pl.BlockSpec((rows, cols), lambda q: (0, 0))

    return dict(
        main=pl.BlockSpec((Q, ch), lambda q: (at(q), 0)),
        prev=pl.BlockSpec((HALO, ch), lambda q: (jnp.maximum(at(q) * (Q // HALO) - 1, 0), 0)),
        tile=pl.BlockSpec((Q, 128), lambda q: (at(q), 0)),
        state=pl.BlockSpec((STATES, ch), lambda q: (at(q), 0)),
        halo=whole(HALO, ch), row8=whole(8, ch), row24=whole(24, ch), row16=whole(STATES, ch), small=whole(8, 128),
    )


def shape(dims, dtype):
    return jax.ShapeDtypeStruct(dims, dtype)


def cost(flops, moved):
    return pl.CostEstimate(flops=int(flops), bytes_accessed=int(moved), transcendentals=0)


def conv_state(x, halo, cw, e, hp, marks, tag="", load=None):
    tokens, ch = x.shape
    s = specs(tokens // Q, ch, False)
    return run(
        conv_state_kernel,
        (tokens // Q,),
        [s["main"], s["prev"], s["halo"], s["row8"], s["tile"], s["small"], s["tile"]],
        [s["main"], s["row16"], s["tile"], s["tile"], s["tile"]],
        [shape((tokens, ch), f32), shape((STATES, ch), f32)] + [shape((tokens, 128), f32)] * 3,
        [],
        [x, x, halo, cw, e, hp, marks],
        "conv_state" + tag,
        cost(tokens * ch * 5000, 4 * tokens * ch),
        load,
    )


def scan_forward(u, z, col, row, e, et, s0, cw, tag="", load=None):
    tokens, ch = u.shape
    s = specs(tokens // Q, ch, False)
    return run(
        scan_kernel,
        (tokens // Q,),
        [s["main"], s["main"], s["tile"], s["tile"], s["tile"], s["tile"], s["row16"], s["row8"]],
        [s["main"], s["main"], s["state"]],
        [shape((tokens, ch), bf16), shape((tokens, ch), f32), shape((tokens // Q * STATES, ch), f32)],
        [pltpu.VMEM((STATES, ch), f32)],
        [u, z, col, row, e, et, s0, cw],
        "scan_forward" + tag,
        cost(tokens * ch * 10000, 8 * tokens * ch),
        load,
    )


def gate_backward(gg, z, y, col, et, tag="", load=None):
    tokens, ch = z.shape
    s = specs(tokens // Q, ch, True)
    return run(
        gate_back_kernel,
        (tokens // Q,),
        [s["main"], s["main"], s["main"], s["tile"], s["tile"]],
        [s["main"], s["main"], s["row16"]],
        [shape((tokens, ch), f32), shape((tokens, ch), bf16), shape((STATES, ch), f32)],
        [],
        [gg, z, y, col, et],
        "gate_backward" + tag,
        cost(tokens * ch * 5000, 10 * tokens * ch),
        load,
    )


def scan_backward(u, dy, x, halo, cw, col, row, e, et, st, de, hp, tag="", load=None):
    tokens, ch = u.shape
    s = specs(tokens // Q, ch, True)
    place = jnp.arange(2 * Q)
    lower = ((place[:, None] >= place[None, :]) & (place[:, None] // Q == place[None, :] // Q)).astype(bf16)
    strict = (jnp.arange(Q)[:, None] < (place % Q)[None, :]).astype(f32)
    pairs = ch // 128
    lane = jnp.arange(3 * 128)
    target = (lane // 128) * HEADS + 2 * jnp.arange(pairs)[:, None] + ((lane % 128) // HEADDIM)[None, :]
    pick = (target[:, :, None] == jnp.arange(128)[None, None, :]).astype(bf16)
    by_head = (jnp.arange(ch)[:, None] // HEADDIM == jnp.arange(128)[None, :]).astype(f32)
    return run(
        scan_back_kernel,
        (tokens // Q,),
        [
            s["main"], s["main"], s["main"], s["prev"], s["halo"], s["row8"], s["tile"], s["tile"], s["tile"],
            s["tile"], s["state"], s["row16"], s["small"],
            pl.BlockSpec((2 * Q, 2 * Q), lambda q: (0, 0)), pl.BlockSpec((Q, 2 * Q), lambda q: (0, 0)),
            pl.BlockSpec((pairs, 3 * 128, 128), lambda q: (0, 0, 0)), pl.BlockSpec((ch, 128), lambda q: (0, 0)),
        ],
        [s["main"], s["tile"], s["row8"], s["row24"], s["small"]],
        [
            shape((tokens, ch), bf16), shape((tokens, 128), f32), shape((8, ch), f32), shape((24, ch), f32),
            shape((8, 128), f32),
        ],
        [
            pltpu.VMEM((STATES, ch), f32), pltpu.VMEM((128, Q), f32), pltpu.VMEM((8, ch), f32),
            pltpu.VMEM((Q, ch), bf16), pltpu.VMEM((Q, ch), bf16), pltpu.VMEM((128, ch), f32),
            pltpu.VMEM((128, ch), f32), pltpu.VMEM((Q, 128), f32), pltpu.VMEM((Q, Q), f32),
        ],
        [u, dy, x, x, halo, cw, col, row, e, et, st, de, hp, lower, strict, pick, by_head],
        "scan_backward" + tag,
        cost(tokens * ch * 25000, 12 * tokens * ch),
        load,
    )


def norm_specs(width):
    main = pl.BlockSpec((Q, width), lambda q: (q, 0))
    return main, pl.BlockSpec((width, Q), lambda q: (0, q)), pl.BlockSpec((1, width), lambda q: (0, 0))


def norm_forward(rows, gain_row, name, load=None):
    tokens, width = rows[0].shape
    main, turned, one = norm_specs(width)
    return run(
        norm_kernel,
        (tokens // Q,),
        [main] * len(rows) + [one],
        [main, main, turned],
        [shape((tokens, width), f32), shape((tokens, width), bf16), shape((width, tokens), bf16)],
        [],
        [*rows, gain_row],
        name,
        cost(tokens * width * 20, 12 * tokens * width),
        load,
    )


def norm_back(grads, rows, gain_row, bases, name, load=None, transpose=False):
    tokens, width = rows.shape
    main, turned, one = norm_specs(width)
    high, low, part, *high_t = run(
        functools.partial(norm_back_kernel, len(grads), len(grads) + len(bases)),
        (tokens // Q,),
        [main, one] + [main] * (len(grads) + len(bases)),
        [main, main, pl.BlockSpec((8, width), lambda q: (0, 0))] + [turned] * transpose,
        [shape((tokens, width), bf16), shape((tokens, width), bf16), shape((8, width), f32)]
        + [shape((width, tokens), bf16)] * transpose,
        [],
        [rows, gain_row, *grads, *bases],
        name,
        cost(tokens * width * 20, 16 * tokens * width),
        load,
    )
    return high, low, part[0], *high_t


def token_marks(seg, seg_before):
    tokens = seg.shape[0]
    by_block = seg.reshape(tokens // Q, Q)
    before = jnp.concatenate([seg_before[2:3], by_block[:-1, Q - 1]])
    padded = jnp.concatenate([seg_before, seg])
    found = [seg.astype(f32)] + [(padded[3 - k : 3 - k + tokens] == seg).astype(f32) for k in (1, 2, 3)]
    found.append((by_block == before[:, None]).astype(f32).reshape(-1))
    found.append((by_block == by_block[:, Q - 1 :]).astype(f32).reshape(-1))
    lane = jnp.arange(128)[None, :]
    out = jnp.zeros((tokens, 128), f32)
    for i, v in enumerate(found):
        out = jnp.where(lane == SEG + i, v[:, None], out)
    return out


def swap(x, axis, n, mask):
    return lax.ppermute(x, axis, [(i, i ^ mask) for i in range(n)])


def bf_dot(a, b):
    return jnp.dot(a, b, preferred_element_type=f32)


def make_local(n):
    def local(
        layer_in, seg_ids, gain_one, x_weight, z_weight, dt_weight, bc_weight, conv_weight, conv_bias,
        dt_bias, a_log, d_skip, out_weight, gain_two, gate_weight, up_weight, down_weight, cotangent,
    ):
        tokens, width = layer_in.shape
        rows, ch = x_weight.shape
        heads = dt_weight.shape[1]
        states = bc_weight.shape[1] // 2
        me, half = lax.axis_index("fsdp"), lax.axis_index("tp")

        epack = jnp.concatenate([dt_weight, bc_weight, jnp.zeros((rows, EXTRA - heads - 2 * states), bf16)], axis=1)
        X, E = Gather("x", x_weight, n), Gather("e", epack, n)
        Z, O = Gather("z", z_weight, n), Gather("o", out_weight, n)
        G, U, D = Gather("g", gate_weight, n), Gather("u", up_weight, n), Gather("d", down_weight, n)

        rate = -jnp.exp(a_log)
        pad = jnp.zeros((128 - heads,), f32)
        by_head = jnp.stack([jnp.concatenate([dt_bias, pad]), jnp.concatenate([rate, pad])])
        small = jnp.concatenate(
            [
                conv_weight,
                conv_bias[None, :],
                jnp.repeat(d_skip, HEADDIM)[None, :],
                jnp.pad(by_head, ((0, 0), (0, ch - 128))),
            ],
            axis=0,
        )
        smalls = [small, swap(small, "tp", 2, 1)]
        head_rows = [jnp.pad(v[6:8, :128], ((0, 6), (0, 0))) for v in smalls]
        before_rows = lax.ppermute(layer_in[tokens - HALO :], "tp", [(0, 1)])
        seg = lax.dynamic_slice(seg_ids, (half * tokens,), (tokens,))
        seg_before = jnp.where(half == 0, -1, seg_ids[tokens - 3 : tokens])

        part = rows // 2
        place = jnp.arange(2 * n)
        q = n // 4
        p = place % n
        part_at = (me ^ (p // (2 * q) + 2 * ((p // q) % 2) + 4 * (p % q))) * 2 + place // n
        seek = (place // 2) ^ me
        place_of = (place % 2) * n + (seek % 2) * 2 * q + ((seek // 2) % 2) * q + seek // 4
        col_at = (part_at[:, None] * part + jnp.arange(part)[None, :]).reshape(-1)
        turn = (jnp.arange(width)[:, None] == col_at[None, :]).astype(bf16)

        def to_local(v):
            return jnp.take(v.reshape(2 * n, part), part_at, axis=0).reshape(-1)

        def to_global(v):
            return jnp.take(v.reshape(2 * n, part), place_of, axis=0).reshape(-1)

        gain_one, gain_two = to_local(gain_one)[None, :], to_local(gain_two)[None, :]
        (rows_in,) = matmul([[(layer_in, turn)]], f32, 512, "turn_rows", Load(X, E))
        rows_in, normed, normed_t = norm_forward([rows_in], gain_one, "norm_one", Load(X, E, Z))
        cot_low, cot_t = matmul([[(cotangent, turn)]], bf16, 512, "turn_cotangent", Load(X, E, O), turned=True)
        carry_only(Load(X, E, Z), "carry_one")
        halo_rows = bf_dot(before_rows, turn)
        halo_scale = lax.rsqrt(jnp.mean(halo_rows * halo_rows, axis=-1, keepdims=True) + epsilon)
        normed_before = (halo_rows * halo_scale * gain_one).astype(bf16)
        marks = token_marks(seg, seg_before)

        found = matmul(
            [[(normed, w)] for w in X.full], f32, 512, "project_x", Load(Z, O, G), beside=(normed_before, E.full)
        )
        xs, halos, es = found[:2], found[2:4], found[4:]
        saved = []
        for b in (0, 1):
            v = dict(x=xs[b], cw=smalls[b], hp=head_rows[b])
            v["e"], v["halo"] = es[b], halos[b]
            load = Load(Z, O, G, U) if b == 0 else Load(G, O, D)
            v["u"], v["end"], v["col"], v["row"], v["et"] = conv_state(
                v["x"], v["halo"], v["cw"], v["e"], v["hp"], marks, tag=str(b), load=load
            )
            saved.append(v)
        starts = lax.ppermute(jnp.stack([v["end"] for v in saved]), "tp", [(0, 1)])[::-1]
        zs = matmul([[(normed, w)] for w in Z.full], f32, 512, "project_z", Load(G, U, D))
        for b in (0, 1):
            v = saved[b]
            v["z"] = zs[b]
            v["gated"], v["y"], v["states"] = scan_forward(
                v["u"], v["z"], v["col"], v["row"], v["e"], v["et"], starts[b], v["cw"],
                tag=str(b), load=Load(U) if b == 0 else Load(U, D),
            )
        (mixed,) = matmul(
            [[(v["gated"], w) for v, w in zip(saved, O.full)]], f32, 512, "project_out", Load(D), nt=True
        )
        hidden, normed_two, two_t = norm_forward([rows_in, mixed], gain_two, "norm_two")

        acts, gate_grads, up_grads = feed_forward(normed_two, cot_low, G.full, U.full, D.full)
        def halves(key, grads):
            return [Scatter(key, grads, n, i, 2) for i in (0, 1)]

        da, db = halves("d", matmul([[(cot_t, a)] for a in acts], bf16, 512, "down_grad"))
        ga, gb = halves("g", matmul([[(two_t, a)] for a in gate_grads], bf16, 512, "gate_grad", Load(da, db)))
        ua, ub = halves("u", matmul([[(two_t, a)] for a in up_grads], bf16, 512, "up_grad", Load(da, ga, gb)))
        (fed,) = matmul([list(zip(acts, D.full))], f32, 512, "project_down", Load(db, da, ua, ub), nt=True)
        out_low = (hidden + fed).astype(bf16)
        (grad_two,) = matmul(
            [list(zip(gate_grads, G.full)) + list(zip(up_grads, U.full))], f32, 256, "two_back",
            Load(ga, gb, db, da), nt=True,
        )
        mixed_grad, mixed_low, gain_two_part, mixed_t = norm_back(
            [grad_two], hidden, gain_two, [cot_low], "norm_two_back", Load(ga, db), True
        )

        so = Scatter("o", matmul([[(mixed_t, v["gated"])] for v in saved], bf16, 512, "out_grad", Load(ua, ga)), n)
        gg = matmul([[(mixed_grad, w)] for w in O.full], f32, 512, "gated_back", Load(gb, so))
        for b in (0, 1):
            v = saved[b]
            v["dy"], v["dz"], v["ds"] = gate_backward(
                gg[b], v["z"], v["y"], v["col"], v["et"], tag=str(b), load=Load(ua) if b == 0 else None
            )
        ends = lax.ppermute(jnp.stack([v["ds"] for v in saved]), "tp", [(1, 0)])[::-1]
        sz = Scatter("z", matmul([[(normed_t, v["dz"])] for v in saved], bf16, 512, "z_grad"), n)

        def back(b, load):
            v = saved[b]
            v["dx"], v["de"], v["cg"], v["edge"], v["hg"] = scan_backward(
                v["u"], v["dy"], v["x"], v["halo"], v["cw"], v["col"], v["row"], v["e"], v["et"], v["states"],
                ends[b], v["hp"], tag=str(b), load=load,
            )
            cw, edge = v["cw"], v["edge"].reshape(3, 8, ch)
            fix = [jnp.zeros((HALO - 3, ch), f32)]
            for j in (3, 2, 1):
                fix.append(sum(cw[k : k + 1] * edge[k - 1, k - j : k - j + 1] for k in range(j, 4)))
            v["fix"] = jnp.concatenate(fix, axis=0)

        def x_gradient(b, load):
            v = saved[b]
            return matmul(
                [[(normed_t, v["dx"]), (before_t, v["fix"].astype(bf16))]], bf16, 512, f"x_grad{b}", load
            )[0]

        before_t = normed_before.T
        back(1, Load(so, ub, sz, ua, gb))
        sx = LateScatter("x", n, x_gradient(1, Load(so)))
        (grad_z,) = matmul(
            [[(v["dz"], w) for v, w in zip(saved, Z.full)]], f32, 512, "z_back", Load(sx, ub), nt=True
        )
        back(0, Load(sz, sx, so, ub))
        sx.given(x_gradient(0, None))
        fixes = lax.ppermute(jnp.stack([v["fix"] for v in saved]), "tp", [(1, 0)])[::-1]
        own, other = ([v["cg"][:6].reshape(-1), v["hg"][:2].reshape(-1)] for v in saved)
        gain_two_part = to_global(gain_two_part)
        own, other = jnp.concatenate(own + [gain_two_part]), jnp.concatenate(other + [gain_two_part])
        smalls_sum = SumAll("p", own, other, n)

        shared = 0.5 * (saved[0]["de"] + saved[1]["de"])
        own_lane = jnp.arange(EXTRA)[None, :] < heads
        for b in (0, 1):
            v = saved[b]
            last = v["dx"][tokens - HALO :].astype(f32) + fixes[b]
            v["dx"] = lax.dynamic_update_slice(v["dx"], last.astype(bf16), (tokens - HALO, 0))
            v["de"] = jnp.where(own_lane, v["de"], shared).astype(bf16)
        se = Scatter("e", matmul([[(normed_t, v["de"])] for v in saved], bf16, 128, "e_grad"), n)
        pairs = [(v["dx"], w) for v, w in zip(saved, X.full)] + [(v["de"], w) for v, w in zip(saved, E.full)]
        (grad_x,) = matmul([pairs], f32, 512, "x_back", Load(sx, se, sz, smalls_sum), nt=True)
        high, low, gain_one_part = norm_back(
            [grad_x, grad_z], rows_in, gain_one, [mixed_grad, mixed_low], "norm_one_back", Load(se, smalls_sum)
        )
        gain_one_part = to_global(gain_one_part)
        gain_sum = SumAll("q", gain_one_part, gain_one_part, n)
        (layer_out,) = matmul([[(out_low, turn)]], bf16, 512, "turn_out", Load(sx, se, sz, gain_sum), nt=True)
        (input_grad,) = matmul([[(high, turn), (low, turn)]], f32, 512, "turn_back", Load(sx, se, gain_sum), nt=True)

        total = smalls_sum.out
        cg, hg = total[: 6 * ch].reshape(6, ch), total[6 * ch : 6 * ch + 256].reshape(2, 128)
        gain_one_total, gain_two_total = gain_sum.out, total[6 * ch + 256 :]
        dt_b_total, a_total = hg[0, :heads], hg[1, :heads]
        skip_total = jnp.sum(cg[5].reshape(heads, HEADDIM), axis=1)
        return (
            layer_out,
            input_grad,
            gain_one_total,
            sx.out,
            sz.out,
            se.out[:, :heads],
            2.0 * se.out[:, heads : heads + 2 * states],
            cg[:4],
            cg[4],
            dt_b_total,
            a_total,
            skip_total,
            so.out,
            gain_two_total,
            jnp.concatenate([ga.out, gb.out], axis=1),
            jnp.concatenate([ua.out, ub.out], axis=1),
            jnp.concatenate([da.out, db.out], axis=1),
        )

    return local


def solution(mesh):
    rows = P(("fsdp", "tp"), None)
    weight = P("fsdp", "tp")
    in_specs = (
        rows, P("fsdp"), P(), weight, weight, weight, P("fsdp", None), P(None, "tp"), P("tp"), P("tp"), P("tp"),
        P("tp"), weight, P(), weight, weight, weight, rows,
    )
    out_specs = (
        rows, rows, P(), weight, weight, weight, P("fsdp", None), P(None, "tp"), P("tp"), P("tp"), P("tp"), P("tp"),
        weight, P(), weight, weight, weight,
    )
    return jax.shard_map(
        make_local(mesh.shape["fsdp"]), mesh=mesh, in_specs=in_specs, out_specs=out_specs, check_vma=False
    )
```
